256 devices in a mesh: gx: 4 (over x), gy: 8 (over y, core), gz: 8 (over z).
Axes of the slice: x: 4, y: 4, z: 8, core: 2. Of those that a mesh axis runs over, the one named last changes fastest.
Arguments:
- earlier_basis: float32 [8, 4, 16, 128, 1024], P(None, None, 'gx', 'gy', 'gz'), may hold values from -40 to 40
- diffusivity: float32 [4, 16, 128, 1024], P(None, 'gx', 'gy', 'gz'), may hold values from 0.5 to 4
- reaction: float32 [4, 4, 16, 128, 1024], P(None, None, 'gx', 'gy', 'gz'), may hold values from -4 to 4
Outputs:
- new_basis: float32 [4, 4, 16, 128, 1024], P(None, None, 'gx', 'gy', 'gz')
- coefficients: float32 [8, 4], replicated
- triangle: float32 [4, 4], replicated
The draws below stay inside these ranges and needn't reach their ends.
All inputs are finite; a program needn't handle non-finite values.
Results may differ from the reference program's by a relative error of at most 0.00027.
Values sent between devices are 32-bit elements; how exact they have to be, the bound alone decides.
No kernel may reach another device: no remote copies, remote signals or barrier semaphores. Data moves between devices by JAX's collectives and lax.ppermute only.
A program may use at most 64 MiB of HBM per device.

```python
import math
import jax
import jax.numpy as jnp
from jax import lax

SPECIES = 4
STEPS = 4
EARLIER = 8
NX = 16
NY = 128
NZ = 1024


def draw_earlier_basis(key, part):
    first, second, third = jax.random.split(jax.random.fold_in(key, 7), 3)
    coord_x = jnp.arange(NX, dtype=jnp.float32)[:, None, None] / NX
    coord_y = jnp.arange(NY, dtype=jnp.float32)[None, :, None] / NY
    coord_z = jnp.arange(NZ, dtype=jnp.float32)[None, None, :] / NZ
    trend = jnp.exp(jnp.log(3.0) * (coord_x + coord_y + coord_z) / 3.0)
    cell_scale = jnp.exp(jax.random.uniform(first, (SPECIES, NX, NY, NZ), jnp.float32) * jnp.log(10.0))
    shape = (EARLIER, SPECIES, NX, NY, NZ)
    noise = jnp.clip(jax.random.normal(second, shape, jnp.float32), -4.0, 4.0)
    fields = noise * cell_scale * trend / 6.0
    weights = 0.35 * jax.random.normal(third, (EARLIER - 1,), jnp.float32)
    last = (fields[EARLIER - 1] + jnp.tensordot(weights, fields[:EARLIER - 1], 1)) / jnp.sqrt(1.0 + jnp.sum(weights * weights))
    result = jnp.concatenate([fields[:EARLIER - 1], last[None]], 0)
    return jnp.clip(result, -40.0, 40.0)


def steps_of(rng, dims, pieces, smallest, largest):
    def one(dim, parts):
        steps = jax.random.uniform(jax.random.fold_in(jax.random.fold_in(rng, 6), dim), (parts,), jnp.float32, smallest / len(pieces), largest / len(pieces))
        return jnp.repeat(jnp.exp(steps), dims[dim] // parts).reshape((-1,) + (1,) * (len(dims) - dim - 1))

    loudness = one(*pieces[0])
    for cut in pieces[1:]:
        loudness = loudness * one(*cut)
    return loudness


def normal_values(rng, extent, deviation, reach, cuts=(), kind=jnp.bfloat16):
    level = steps_of(rng, extent, cuts, -0.22, 0.18) if cuts else 1.0
    array = jax.random.normal(rng, extent, jnp.float32) * deviation * level
    return jnp.minimum(jnp.maximum(array, -reach), reach).astype(kind)


def setup_inputs(seed: int = 0) -> dict:
    key_of = jax.random.split(jax.random.key(seed), 4)
    return {
        "earlier_basis": draw_earlier_basis(jax.random.fold_in(key_of[3], 71), 0),
        "diffusivity": jnp.clip(jnp.exp(math.log(4.0) - 2.0794415 * jax.random.uniform(key_of[1], (SPECIES, NX, NY, NZ), jnp.float32) ** steps_of(key_of[1], (SPECIES, NX, NY, NZ), ((1, 4), (2, 8), (3, 8)), -0.2, 0.2)), 0.5, 4.0),
        "reaction": normal_values(key_of[2], (SPECIES, SPECIES, NX, NY, NZ), 1.0, 4.0, ((2, 4), (3, 8), (4, 8)), jnp.float32),
    }


SHIFTS = (6.0, 9.0, 14.0, 17.0)
DAMPING = 0.2
HIGHEST = lax.Precision.HIGHEST

def operate(padded, conduct, reaction_local):
    center = padded[:, 1:-1, 1:-1, 1:-1]
    middle = conduct[:, 1:-1, 1:-1, 1:-1]
    applied = center
    for source in range(SPECIES):
        applied = applied + reaction_local[:, source] * center[source]
    sides = [(padded[:, 2:, 1:-1, 1:-1], conduct[:, 2:, 1:-1, 1:-1]), (padded[:, :-2, 1:-1, 1:-1], conduct[:, :-2, 1:-1, 1:-1]), (padded[:, 1:-1, 2:, 1:-1], conduct[:, 1:-1, 2:, 1:-1]), (padded[:, 1:-1, :-2, 1:-1], conduct[:, 1:-1, :-2, 1:-1]), (padded[:, 1:-1, 1:-1, 2:], conduct[:, 1:-1, 1:-1, 2:]), (padded[:, 1:-1, 1:-1, :-2], conduct[:, 1:-1, 1:-1, :-2])]
    for other_value, other_conduct in sides:
        applied = applied + 0.5 * (middle + other_conduct) * (center - other_value)
    return (applied, center)

def reference(earlier_basis, diffusivity, reaction):
    widths = ((0, 0), (1, 1), (1, 1), (1, 1))
    conduct = jnp.pad(diffusivity, widths)
    vector = earlier_basis[EARLIER - 1]
    columns = []
    for degree in range(STEPS):
        applied, center = operate(jnp.pad(vector, widths), conduct, reaction)
        vector = (applied - SHIFTS[degree] * center) * DAMPING
        columns.append(vector.reshape(-1))
    flat_block = jnp.stack(columns)
    flat_basis = earlier_basis.reshape(EARLIER, -1)
    entries = flat_basis.shape[1]
    coeffs = jnp.dot(flat_basis, flat_block.T, precision=HIGHEST) / entries
    residue = flat_block - jnp.dot(coeffs.T, flat_basis, precision=HIGHEST)
    block_gram = jnp.dot(residue, residue.T, precision=HIGHEST) / entries
    factor = jnp.linalg.cholesky(block_gram)
    renewed = lax.linalg.triangular_solve(factor, residue, left_side=True, lower=True)
    return (renewed.reshape((STEPS,) + diffusivity.shape), coeffs, factor.T)
```

```python
import functools

import jax
import jax.numpy as jnp
from jax import lax
from jax.experimental import pallas as pl
from jax.experimental.pallas import tpu as pltpu
from jax.sharding import PartitionSpec as P

SPECIES = 4
STEPS = 4
EARLIER = 8
SHIFTS = (6.0, 9.0, 14.0, 17.0)
DAMPING = 0.2
AXES = ("gx", "gy", "gz")

VECTORS = EARLIER + STEPS
SLOT = {}
for _b in range(VECTORS):
    for _a in range(_b + 1):
        SLOT[(_a, _b)] = len(SLOT)


def pack_faces(planes, x_lo, x_hi, y_lo, y_hi, z_lo, z_hi, first):
    span_x, span_y, span_z = planes[0].shape
    lane = lax.broadcasted_iota(jnp.int32, (span_y, span_z), 1)
    low, high = z_lo, z_hi
    for number, value in enumerate(planes):
        field = first + number
        x_lo[field] = value[0]
        x_hi[field] = value[span_x - 1]
        for x in range(span_x):
            k = field * span_x + x
            y_lo[k : k + 1, :] = value[x, 0:1, :]
            y_hi[k : k + 1, :] = value[x, span_y - 1 : span_y, :]
            shift_low, shift_high = k % span_z, (k + 1) % span_z
            to_low = pltpu.roll(value[x], shift_low, 1) if shift_low else value[x]
            to_high = pltpu.roll(value[x], shift_high, 1) if shift_high else value[x]
            low = jnp.where(lane == k, to_low, low)
            high = jnp.where(lane == k, to_high, high)
    return low, high


def first_faces(v_ref, d_ref, xl, xh, yl, yh, zl, zh):
    zero = jnp.zeros(zl.shape, jnp.float32)
    low, high = pack_faces([v_ref[0, s] for s in range(SPECIES)], xl, xh, yl, yh, zero, zero, 0)
    low, high = pack_faces([d_ref[s] for s in range(SPECIES)], xl, xh, yl, yh, low, high, SPECIES)
    zl[...] = low
    zh[...] = high


def edges():
    flags = []
    for axis in AXES:
        index = lax.axis_index(axis)
        flags += [index == 0, index == lax.axis_size(axis) - 1]
    return flags


def neighbours(value, halos, flags, field):
    span_x, span_y, span_z = value.shape
    xl, xh, yl, yh, zl, zh = halos
    k = field * span_x
    row = lax.broadcasted_iota(jnp.int32, value.shape, 1)
    lane = lax.broadcasted_iota(jnp.int32, value.shape, 2)

    def inside(flag, halo):
        return jnp.where(flag, jnp.zeros_like(halo), halo)

    before_x = jnp.concatenate([inside(flags[0], xl[field])[None], value[:-1]], 0)
    after_x = jnp.concatenate([value[1:], inside(flags[1], xh[field])[None]], 0)
    low_y = inside(flags[2], yl[k : k + span_x, :])[:, None, :]
    high_y = inside(flags[3], yh[k : k + span_x, :])[:, None, :]
    before_y = jnp.where(row == 0, low_y, pltpu.roll(value, 1, 1))
    after_y = jnp.where(row == span_y - 1, high_y, pltpu.roll(value, span_y - 1, 1))
    low_z, high_z = inside(flags[4], zl[...]), inside(flags[5], zh[...])

    def moved(face, shift):
        shift %= span_z
        return pltpu.roll(face, shift, 1) if shift else face

    low_z = jnp.stack([moved(low_z, -(k + x)) for x in range(span_x)])
    high_z = jnp.stack([moved(high_z, span_z - 1 - (k + x)) for x in range(span_x)])
    before_z = jnp.where(lane == 0, low_z, pltpu.roll(value, 1, 2))
    after_z = jnp.where(lane == span_z - 1, high_z, pltpu.roll(value, span_z - 1, 2))
    return before_x, after_x, before_y, after_y, before_z, after_z


def apply_operator(degree, v_of, d_ref, r_ref, d_halos, v_halos, store):
    flags = edges()
    for s in range(SPECIES):
        v = v_of(s)
        d = d_ref[s]
        applied = v * (1.0 - SHIFTS[degree])
        for t in range(SPECIES):
            applied = applied + r_ref[s, t] * v_of(t)
        near_v = neighbours(v, v_halos, flags, s)
        near_d = neighbours(d, d_halos, flags, SPECIES + s)
        for other_v, other_d in zip(near_v, near_d):
            applied = applied + (0.5 * (d + other_d)) * (v - other_v)
        store(s, applied * DAMPING)


def step_kernel(degree, *refs):
    v_ref, d_ref, r_ref = refs[:3]
    d_halos = refs[3:9]
    v_halos = d_halos if degree == 0 else refs[9:15]
    rest = refs[9:] if degree == 0 else refs[15:]
    out_ref, xl, xh, yl, yh, zl, zh = rest
    v_of = (lambda s: v_ref[0, s]) if degree == 0 else (lambda s: v_ref[s])

    def store(s, value):
        out_ref[s] = value

    apply_operator(degree, v_of, d_ref, r_ref, d_halos, v_halos, store)
    zero = jnp.zeros(zl.shape, jnp.float32)
    low, high = pack_faces([out_ref[s] for s in range(SPECIES)], xl, xh, yl, yh, zero, zero, 0)
    zl[...] = low
    zh[...] = high


def products(pairs, load, count):
    def body(i, sums):
        values = load(i)
        return tuple(total + values[a] * values[b] for total, (a, b) in zip(sums, pairs))

    zero = jnp.zeros((8, 128), jnp.float32)
    sums = lax.fori_loop(0, count, body, (zero,) * len(pairs))
    lane = lax.broadcasted_iota(jnp.int32, (8, 128), 1)
    row = zero
    for total, pair in zip(sums, pairs):
        row = jnp.where(lane == SLOT[pair], jnp.sum(total, 1, keepdims=True), row)
    return row


def earlier_products(q_ref, out_ref):
    pairs = [(a, b) for b in range(EARLIER) for a in range(b + 1)]
    out_ref[...] = products(pairs, lambda i: [q_ref[a, i] for a in range(EARLIER)], q_ref.shape[1])


def new_pairs(number):
    return [(a, EARLIER + number) for a in range(EARLIER + number + 1)]


def new_products(number, q_ref, *refs):
    v_refs, (before_ref, out_ref) = refs[: number + 1], refs[number + 1 :]

    def load(i):
        return [q_ref[a, i] for a in range(EARLIER)] + [v[i] for v in v_refs]

    out_ref[...] = before_ref[...] + products(new_pairs(number), load, q_ref.shape[1])


def last_kernel(*refs):
    v_ref, d_ref, r_ref = refs[:3]
    d_halos, v_halos = refs[3:9], refs[9:15]
    q_ref, v1, v2, before_ref, out_ref, sums_ref = refs[15:]
    span_x, span_y, span_z = d_ref.shape[1:]
    count = q_ref.shape[1]

    def store(s, value):
        per = span_x * span_y // 8
        out_ref[s * per : (s + 1) * per] = value.reshape(per, 8, span_z)

    apply_operator(STEPS - 1, lambda s: v_ref[s], d_ref, r_ref, d_halos, v_halos, store)
    v3 = v_ref.reshape(count, 8, span_z)

    def load(i):
        return [q_ref[a, i] for a in range(EARLIER)] + [v1[i], v2[i], v3[i], out_ref[i]]

    row = before_ref[...] + products(new_pairs(STEPS - 1), load, count)
    sums_ref[...] = jnp.broadcast_to(jnp.sum(row, 0, keepdims=True), sums_ref.shape)


def finish_kernel(entries, sums_ref, q_ref, *refs):
    v_refs, (new_ref, coeff_ref, triangle_ref) = refs[:STEPS], refs[STEPS:]
    total = sums_ref[0]
    for i in range(1, sums_ref.shape[0]):
        total = total + sums_ref[i]
    total = jnp.broadcast_to(jnp.sum(total, 0, keepdims=True), total.shape) * (1.0 / entries)

    def entry(a, b):
        k = SLOT[(min(a, b), max(a, b))]
        return jnp.broadcast_to(total[:, k : k + 1], total.shape)

    coeff = [[entry(i, EARLIER + j) for j in range(STEPS)] for i in range(EARLIER)]
    overlap = {(a, b): entry(a, b) for b in range(EARLIER) for a in range(b + 1)}
    gram = {}
    for k in range(STEPS):
        mixed = []
        for i in range(EARLIER):
            term = -2.0 * coeff[i][k]
            for m in range(EARLIER):
                term = term + overlap[(min(i, m), max(i, m))] * coeff[m][k]
            mixed.append(term)
        for j in range(k, STEPS):
            value = entry(EARLIER + k, EARLIER + j)
            for i in range(EARLIER):
                value = value + coeff[i][j] * mixed[i]
            gram[(j, k)] = value
    factor, inverse = {}, []
    for k in range(STEPS):
        pivot = gram[(k, k)]
        for m in range(k):
            pivot = pivot - factor[(k, m)] * factor[(k, m)]
        factor[(k, k)] = jnp.sqrt(pivot)
        inverse.append(1.0 / factor[(k, k)])
        for j in range(k + 1, STEPS):
            value = gram[(j, k)]
            for m in range(k):
                value = value - factor[(j, m)] * factor[(k, m)]
            factor[(j, k)] = value * inverse[k]
    row = lax.broadcasted_iota(jnp.int32, total.shape, 0)
    lane = lax.broadcasted_iota(jnp.int32, total.shape, 1)
    table = jnp.zeros_like(total)
    for i in range(EARLIER):
        for j in range(STEPS):
            table = jnp.where((row == i) & (lane == j), coeff[i][j], table)
    coeff_ref[...] = table[:, :STEPS]
    table = jnp.zeros_like(total)
    for (j, k), value in factor.items():
        table = jnp.where((row == k) & (lane == j), value, table)
    triangle_ref[...] = table[:STEPS, :STEPS]

    def body(n, carry):
        earlier = [q_ref[i, n] for i in range(EARLIER)]
        done = []
        for j in range(STEPS):
            value = v_refs[j][n]
            for i in range(EARLIER):
                value = value - coeff[i][j] * earlier[i]
            for k in range(j):
                value = value - factor[(j, k)] * done[k]
            done.append(value * inverse[j])
            new_ref[j, n] = done[j]
        return carry

    lax.fori_loop(0, q_ref.shape[1], body, 0)


def call(body, outs, cost, *args, **more):
    return pl.pallas_call(
        body,
        out_shape=[jax.ShapeDtypeStruct(shape, jnp.float32) for shape in outs],
        cost_estimate=pl.CostEstimate(flops=cost, bytes_accessed=cost, transcendentals=0),
        compiler_params=pltpu.CompilerParams(vmem_limit_bytes=8 << 20),
        **more,
    )(*args)


def exchange(faces):
    halos = []
    for number, axis in enumerate(AXES):
        count = lax.axis_size(axis)
        up = [(i, (i + 1) % count) for i in range(count)]
        down = [(target, source) for source, target in up]
        low, high = faces[2 * number : 2 * number + 2]
        halos += [lax.ppermute(high, axis, up), lax.ppermute(low, axis, down)]
    return halos


def on_device(earlier_basis, diffusivity, reaction):
    block = diffusivity.shape[1:]
    span_x, span_y, span_z = block
    tiles = SPECIES * span_x * span_y // 8
    devices = 1
    for axis in AXES:
        devices *= lax.axis_size(axis)
    entries = tiles * 8 * span_z * devices
    field = (SPECIES,) + block
    whole = pl.BlockSpec(memory_space=pltpu.VMEM)
    start = pl.BlockSpec((1,) + field, lambda i: (EARLIER - 1, 0, 0, 0, 0))

    def shapes(fields):
        plane, rows = (fields, span_y, span_z), (fields * span_x, span_z)
        return [plane, plane, rows, rows, (span_y, span_z), (span_y, span_z)]

    def spec_of(shape):
        return pl.BlockSpec(shape, lambda i: (0,) * len(shape))

    small = shapes(2 * SPECIES)
    faces = call(
        first_faces,
        small,
        1 << 20,
        earlier_basis,
        diffusivity,
        grid=(1,),
        in_specs=[start, spec_of(field)],
        out_specs=[spec_of(s) for s in small],
    )
    first_halos = exchange(faces)
    basis = earlier_basis.reshape(EARLIER, tiles, 8, span_z)
    (sums,) = call(earlier_products, [(8, span_z)], 4 << 20, basis)
    outs = [field] + shapes(SPECIES)
    out = call(
        functools.partial(step_kernel, 0),
        outs,
        1 << 20,
        earlier_basis,
        diffusivity,
        reaction,
        *first_halos,
        grid=(1,),
        in_specs=[start, spec_of(field), spec_of(reaction.shape)] + [spec_of(s) for s in small],
        out_specs=[spec_of(s) for s in outs],
    )
    columns = []
    for degree in range(1, STEPS):
        vector, halos = out[0], exchange(out[1:])
        columns.append(vector.reshape(tiles, 8, span_z))
        (sums,) = call(
            functools.partial(new_products, degree - 1),
            [(8, span_z)],
            4 << 20,
            basis,
            *columns,
            sums,
        )
        if degree < STEPS - 1:
            out = call(
                functools.partial(step_kernel, degree),
                outs,
                1 << 20,
                vector,
                diffusivity,
                reaction,
                *first_halos,
                *halos,
            )
    last, rows = call(
        last_kernel,
        [(tiles, 8, span_z), (devices, span_z)],
        1 << 20,
        vector,
        diffusivity,
        reaction,
        *first_halos,
        *halos,
        basis,
        columns[0],
        columns[1],
        sums,
    )
    columns.append(last)
    rows = lax.all_to_all(rows.reshape(devices, 1, span_z), AXES, 0, 0)
    new, coeff, triangle = call(
        functools.partial(finish_kernel, entries),
        [(STEPS, tiles, 8, span_z), (EARLIER, STEPS), (STEPS, STEPS)],
        1 << 20,
        rows.reshape(devices // 8, 8, span_z),
        basis,
        *columns,
    )
    return new.reshape((STEPS,) + field), coeff, triangle


def solution(mesh):
    in_specs = (
        P(None, None, "gx", "gy", "gz"),
        P(None, "gx", "gy", "gz"),
        P(None, None, "gx", "gy", "gz"),
    )
    out_specs = (P(None, None, "gx", "gy", "gz"), P(), P())
    return jax.shard_map(
        on_device, mesh=mesh, in_specs=in_specs, out_specs=out_specs, check_vma=False
    )
```

```python
import functools

import jax
import jax.numpy as jnp
from jax import lax
from jax.experimental import pallas as pl
from jax.experimental.pallas import tpu as pltpu
from jax.sharding import PartitionSpec as P

SPECIES = 4
STEPS = 4
EARLIER = 8
SHIFTS = (6.0, 9.0, 14.0, 17.0)
DAMPING = 0.2
AXES = ("gx", "gy", "gz")

VECTORS = EARLIER + STEPS
SLOT = {}
for _b in range(VECTORS):
    for _a in range(_b + 1):
        SLOT[(_a, _b)] = len(SLOT)


def pack_faces(planes, x_lo, x_hi, y_lo, y_hi, z_lo, z_hi, first):
    span_x, span_y, span_z = planes[0].shape
    lane = lax.broadcasted_iota(jnp.int32, (span_y, span_z), 1)
    low, high = z_lo, z_hi
    for number, value in enumerate(planes):
        field = first + number
        x_lo[field] = value[0]
        x_hi[field] = value[span_x - 1]
        for x in range(span_x):
            k = field * span_x + x
            y_lo[k : k + 1, :] = value[x, 0:1, :]
            y_hi[k : k + 1, :] = value[x, span_y - 1 : span_y, :]
            shift_low, shift_high = k % span_z, (k + 1) % span_z
            to_low = pltpu.roll(value[x], shift_low, 1) if shift_low else value[x]
            to_high = pltpu.roll(value[x], shift_high, 1) if shift_high else value[x]
            low = jnp.where(lane == k, to_low, low)
            high = jnp.where(lane == k, to_high, high)
    return low, high


def first_faces(q_ref, d_hbm, v_ref, xl, xh, yl, yh, zl, zh, d_ref, v_sem, d_sem):
    v_copy = pltpu.make_async_copy(q_ref.at[EARLIER - 1], v_ref, v_sem)
    d_copy = pltpu.make_async_copy(d_hbm, d_ref, d_sem)
    v_copy.start()
    d_copy.start()
    v_copy.wait()
    zero = jnp.zeros(zl.shape, jnp.float32)
    low, high = pack_faces([v_ref[s] for s in range(SPECIES)], xl, xh, yl, yh, zero, zero, 0)
    d_copy.wait()
    low, high = pack_faces([d_ref[s] for s in range(SPECIES)], xl, xh, yl, yh, low, high, SPECIES)
    zl[...] = low
    zh[...] = high


def edges():
    flags = []
    for axis in AXES:
        index = lax.axis_index(axis)
        flags += [index == 0, index == lax.axis_size(axis) - 1]
    return flags


def neighbours(value, halos, flags, field):
    span_x, span_y, span_z = value.shape
    xl, xh, yl, yh, zl, zh = halos
    k = field * span_x
    row = lax.broadcasted_iota(jnp.int32, value.shape, 1)
    lane = lax.broadcasted_iota(jnp.int32, value.shape, 2)

    def inside(flag, halo):
        return jnp.where(flag, jnp.zeros_like(halo), halo)

    before_x = jnp.concatenate([inside(flags[0], xl[field])[None], value[:-1]], 0)
    after_x = jnp.concatenate([value[1:], inside(flags[1], xh[field])[None]], 0)
    low_y = inside(flags[2], yl[k : k + span_x, :])[:, None, :]
    high_y = inside(flags[3], yh[k : k + span_x, :])[:, None, :]
    before_y = jnp.where(row == 0, low_y, pltpu.roll(value, 1, 1))
    after_y = jnp.where(row == span_y - 1, high_y, pltpu.roll(value, span_y - 1, 1))
    low_z, high_z = inside(flags[4], zl[...]), inside(flags[5], zh[...])

    def moved(face, shift):
        shift %= span_z
        return pltpu.roll(face, shift, 1) if shift else face

    low_z = jnp.stack([moved(low_z, -(k + x)) for x in range(span_x)])
    high_z = jnp.stack([moved(high_z, span_z - 1 - (k + x)) for x in range(span_x)])
    before_z = jnp.where(lane == 0, low_z, pltpu.roll(value, 1, 2))
    after_z = jnp.where(lane == span_z - 1, high_z, pltpu.roll(value, span_z - 1, 2))
    return before_x, after_x, before_y, after_y, before_z, after_z


def apply_operator(degree, v_of, d_ref, r_ref, d_halos, v_halos, store):
    flags = edges()
    for s in range(SPECIES):
        v = v_of(s)
        d = d_ref[s]
        applied = v * (1.0 - SHIFTS[degree])
        for t in range(SPECIES):
            applied = applied + r_ref[s, t] * v_of(t)
        near_v = neighbours(v, v_halos, flags, s)
        near_d = neighbours(d, d_halos, flags, SPECIES + s)
        for other_v, other_d in zip(near_v, near_d):
            applied = applied + (0.5 * (d + other_d)) * (v - other_v)
        store(s, applied * DAMPING)


def step_kernel(degree, *refs):
    v_ref, d_ref, r_ref = refs[:3]
    d_halos = refs[3:9]
    v_halos = d_halos if degree == 0 else refs[9:15]
    rest = refs[9:] if degree == 0 else refs[15:]
    out_ref, xl, xh, yl, yh, zl, zh = rest
    v_of = lambda s: v_ref[s]

    def store(s, value):
        out_ref[s] = value

    apply_operator(degree, v_of, d_ref, r_ref, d_halos, v_halos, store)
    zero = jnp.zeros(zl.shape, jnp.float32)
    low, high = pack_faces([out_ref[s] for s in range(SPECIES)], xl, xh, yl, yh, zero, zero, 0)
    zl[...] = low
    zh[...] = high


def products(pairs, load, count):
    def body(i, sums):
        values = load(i)
        return tuple(total + values[a] * values[b] for total, (a, b) in zip(sums, pairs))

    zero = jnp.zeros((8, 128), jnp.float32)
    sums = lax.fori_loop(0, count, body, (zero,) * len(pairs))
    lane = lax.broadcasted_iota(jnp.int32, (8, 128), 1)
    row = zero
    for total, pair in zip(sums, pairs):
        row = jnp.where(lane == SLOT[pair], jnp.sum(total, 1, keepdims=True), row)
    return row


def earlier_products(q_ref, out_ref):
    pairs = [(a, b) for b in range(EARLIER) for a in range(b + 1)]
    out_ref[...] = products(pairs, lambda i: [q_ref[a, i] for a in range(EARLIER)], q_ref.shape[1])


def new_pairs(number):
    return [(a, EARLIER + number) for a in range(EARLIER + number + 1)]


def new_products(number, q_ref, *refs):
    v_refs, (before_ref, out_ref) = refs[: number + 1], refs[number + 1 :]

    def load(i):
        return [q_ref[a, i] for a in range(EARLIER)] + [v[i] for v in v_refs]

    out_ref[...] = before_ref[...] + products(new_pairs(number), load, q_ref.shape[1])


def last_kernel(*refs):
    v_ref, d_ref, r_ref = refs[:3]
    d_halos, v_halos = refs[3:9], refs[9:15]
    q_ref, v1, v2, before_ref, out_ref, sums_ref = refs[15:]
    span_x, span_y, span_z = d_ref.shape[1:]
    count = q_ref.shape[1]

    def store(s, value):
        per = span_x * span_y // 8
        out_ref[s * per : (s + 1) * per] = value.reshape(per, 8, span_z)

    apply_operator(STEPS - 1, lambda s: v_ref[s], d_ref, r_ref, d_halos, v_halos, store)
    v3 = v_ref.reshape(count, 8, span_z)

    def load(i):
        return [q_ref[a, i] for a in range(EARLIER)] + [v1[i], v2[i], v3[i], out_ref[i]]

    row = before_ref[...] + products(new_pairs(STEPS - 1), load, count)
    sums_ref[...] = jnp.broadcast_to(jnp.sum(row, 0, keepdims=True), sums_ref.shape)


def finish_kernel(entries, sums_ref, q_ref, *refs):
    v_refs, (new_ref, coeff_ref, triangle_ref) = refs[:STEPS], refs[STEPS:]
    total = sums_ref[0]
    for i in range(1, sums_ref.shape[0]):
        total = total + sums_ref[i]
    total = jnp.broadcast_to(jnp.sum(total, 0, keepdims=True), total.shape) * (1.0 / entries)

    def entry(a, b):
        k = SLOT[(min(a, b), max(a, b))]
        return jnp.broadcast_to(total[:, k : k + 1], total.shape)

    coeff = [[entry(i, EARLIER + j) for j in range(STEPS)] for i in range(EARLIER)]
    overlap = {(a, b): entry(a, b) for b in range(EARLIER) for a in range(b + 1)}
    gram = {}
    for k in range(STEPS):
        mixed = []
        for i in range(EARLIER):
            term = -2.0 * coeff[i][k]
            for m in range(EARLIER):
                term = term + overlap[(min(i, m), max(i, m))] * coeff[m][k]
            mixed.append(term)
        for j in range(k, STEPS):
            value = entry(EARLIER + k, EARLIER + j)
            for i in range(EARLIER):
                value = value + coeff[i][j] * mixed[i]
            gram[(j, k)] = value
    factor, inverse = {}, []
    for k in range(STEPS):
        pivot = gram[(k, k)]
        for m in range(k):
            pivot = pivot - factor[(k, m)] * factor[(k, m)]
        factor[(k, k)] = jnp.sqrt(pivot)
        inverse.append(1.0 / factor[(k, k)])
        for j in range(k + 1, STEPS):
            value = gram[(j, k)]
            for m in range(k):
                value = value - factor[(j, m)] * factor[(k, m)]
            factor[(j, k)] = value * inverse[k]
    row = lax.broadcasted_iota(jnp.int32, total.shape, 0)
    lane = lax.broadcasted_iota(jnp.int32, total.shape, 1)
    table = jnp.zeros_like(total)
    for i in range(EARLIER):
        for j in range(STEPS):
            table = jnp.where((row == j) & (lane == i), coeff[i][j], table)
    coeff_ref[...] = table[:STEPS, :EARLIER]
    table = jnp.zeros_like(total)
    for (j, k), value in factor.items():
        table = jnp.where((row == k) & (lane == j), value, table)
    triangle_ref[...] = table[:STEPS, :STEPS]

    def body(n, carry):
        earlier = [q_ref[i, n] for i in range(EARLIER)]
        done = []
        for j in range(STEPS):
            value = v_refs[j][n]
            for i in range(EARLIER):
                value = value - coeff[i][j] * earlier[i]
            for k in range(j):
                value = value - factor[(j, k)] * done[k]
            done.append(value * inverse[j])
            new_ref[j, n] = done[j]
        return carry

    lax.fori_loop(0, q_ref.shape[1], body, 0)


def call(body, outs, cost, *args, **more):
    return pl.pallas_call(
        body,
        out_shape=[jax.ShapeDtypeStruct(shape, jnp.float32) for shape in outs],
        cost_estimate=pl.CostEstimate(flops=cost, bytes_accessed=cost, transcendentals=0),
        compiler_params=pltpu.CompilerParams(vmem_limit_bytes=8 << 20),
        **more,
    )(*args)


def exchange(faces):
    halos = []
    for number, axis in enumerate(AXES):
        count = lax.axis_size(axis)
        up = [(i, (i + 1) % count) for i in range(count)]
        down = [(target, source) for source, target in up]
        low, high = faces[2 * number : 2 * number + 2]
        halos += [lax.ppermute(high, axis, up), lax.ppermute(low, axis, down)]
    return halos


def on_device(earlier_basis, diffusivity, reaction):
    block = diffusivity.shape[1:]
    span_x, span_y, span_z = block
    tiles = SPECIES * span_x * span_y // 8
    devices = 1
    for axis in AXES:
        devices *= lax.axis_size(axis)
    entries = tiles * 8 * span_z * devices
    field = (SPECIES,) + block
    in_hbm = pl.BlockSpec(memory_space=pltpu.HBM)

    def shapes(fields):
        plane, rows = (fields, span_y, span_z), (fields * span_x, span_z)
        return [plane, plane, rows, rows, (span_y, span_z), (span_y, span_z)]

    vector, *faces = call(
        first_faces,
        [field] + shapes(2 * SPECIES),
        1 << 20,
        pltpu.with_memory_space_constraint(earlier_basis, pltpu.HBM),
        pltpu.with_memory_space_constraint(diffusivity, pltpu.HBM),
        in_specs=[in_hbm, in_hbm],
        scratch_shapes=[pltpu.VMEM(field, jnp.float32), pltpu.SemaphoreType.DMA, pltpu.SemaphoreType.DMA],
    )
    first_halos = exchange(faces)
    basis = earlier_basis.reshape(EARLIER, tiles, 8, span_z)
    (sums,) = call(earlier_products, [(8, span_z)], 4 << 20, basis)
    outs = [field] + shapes(SPECIES)
    out = call(
        functools.partial(step_kernel, 0),
        outs,
        1 << 20,
        vector,
        diffusivity,
        reaction,
        *first_halos,
    )
    columns = []
    for degree in range(1, STEPS):
        vector, halos = out[0], exchange(out[1:])
        columns.append(vector.reshape(tiles, 8, span_z))
        (sums,) = call(
            functools.partial(new_products, degree - 1),
            [(8, span_z)],
            4 << 20,
            basis,
            *columns,
            sums,
        )
        if degree < STEPS - 1:
            out = call(
                functools.partial(step_kernel, degree),
                outs,
                1 << 20,
                vector,
                diffusivity,
                reaction,
                *first_halos,
                *halos,
            )
    last, rows = call(
        last_kernel,
        [(tiles, 8, span_z), (devices, span_z)],
        1 << 20,
        vector,
        diffusivity,
        reaction,
        *first_halos,
        *halos,
        basis,
        columns[0],
        columns[1],
        sums,
    )
    columns.append(last)
    rows = lax.all_to_all(rows.reshape(devices, 1, span_z), AXES, 0, 0)
    new, coeff, triangle = call(
        functools.partial(finish_kernel, entries),
        [(STEPS, tiles, 8, span_z), (STEPS, EARLIER), (STEPS, STEPS)],
        1 << 20,
        rows.reshape(devices // 8, 8, span_z),
        basis,
        *columns,
    )
    return new.reshape((STEPS,) + field), coeff.T, triangle


def solution(mesh):
    in_specs = (
        P(None, None, "gx", "gy", "gz"),
        P(None, "gx", "gy", "gz"),
        P(None, None, "gx", "gy", "gz"),
    )
    out_specs = (P(None, None, "gx", "gy", "gz"), P(), P())
    return jax.shard_map(
        on_device, mesh=mesh, in_specs=in_specs, out_specs=out_specs, check_vma=False
    )
```

```python
import functools

import jax
import jax.numpy as jnp
from jax import lax
from jax.experimental import pallas as pl
from jax.experimental.pallas import tpu as pltpu
from jax.sharding import PartitionSpec as P

SPECIES = 4
STEPS = 4
EARLIER = 8
SHIFTS = (6.0, 9.0, 14.0, 17.0)
DAMPING = 0.2
AXES = ("gx", "gy", "gz")

VECTORS = EARLIER + STEPS
SLOT = {}
for _b in range(VECTORS):
    for _a in range(_b + 1):
        SLOT[(_a, _b)] = len(SLOT)

WIDE = 2
DEEP = 4
ROWS = 24
V_PLANES = tuple(range(-WIDE, 4 + WIDE))
R_PLANES = tuple(range(-1, 5))
V_BASE = 0
D_BASE = SPECIES * len(V_PLANES)
R_BASE = 2 * D_BASE
PLANES = R_BASE + SPECIES * SPECIES * len(R_PLANES)
PER_BLOCK = 32
BLOCKS = PLANES // PER_BLOCK


def v_at(s, x):
    return V_BASE + s * len(V_PLANES) + x + WIDE


def d_at(s, x):
    return D_BASE + s * len(V_PLANES) + x + WIDE


def r_at(s, t, x):
    return R_BASE + (s * SPECIES + t) * len(R_PLANES) + x + 1


def iota(shape, dim):
    return lax.broadcasted_iota(jnp.int32, shape, dim)


def roll(value, shift, axis):
    shift %= value.shape[axis]
    return pltpu.roll(value, shift, axis) if shift else value


def x_faces(q_ref, d_ref, r_ref, low_ref, high_ref, v_out, d_out, sems):
    copies = [(q_ref.at[EARLIER - 1], v_out), (d_ref, d_out)]
    for face, planes, plane in ((low_ref, pl.ds(0, WIDE), 0), (high_ref, pl.ds(4 - WIDE, WIDE), 3)):
        for s in range(SPECIES):
            copies.append((q_ref.at[EARLIER - 1, s, planes], face.at[pl.ds(s * WIDE, WIDE)]))
            copies.append((d_ref.at[s, planes], face.at[pl.ds((SPECIES + s) * WIDE, WIDE)]))
            start = 2 * SPECIES * WIDE + s * SPECIES
            copies.append((r_ref.at[s, :, plane], face.at[pl.ds(start, SPECIES)]))
    started = [pltpu.make_async_copy(a, b, sems.at[n]) for n, (a, b) in enumerate(copies)]
    for copy in started:
        copy.start()
    for copy in started:
        copy.wait()


def own_planes(v_ref, d_ref, r_ref, before_ref, after_ref):
    def pick(own, slot, width, x):
        if x < 0:
            return lambda rows: before_ref[slot + x + width, rows]
        if x > 3:
            return lambda rows: after_ref[slot + x - 4, rows]
        return lambda rows: own(x, rows)

    planes = []
    for s in range(SPECIES):
        for x in V_PLANES:
            planes.append(pick(lambda x, rows, s=s: v_ref[s, x, rows], s * WIDE, WIDE, x))
    for s in range(SPECIES):
        for x in V_PLANES:
            planes.append(pick(lambda x, rows, s=s: d_ref[s, x, rows], (SPECIES + s) * WIDE, WIDE, x))
    for s in range(SPECIES):
        for t in range(SPECIES):
            slot = 2 * SPECIES * WIDE + s * SPECIES + t
            for x in R_PLANES:
                planes.append(pick(lambda x, rows, s=s, t=t: r_ref[s, t, x, rows], slot, 1, x))
    return planes


def y_faces(v_ref, d_ref, r_ref, before_ref, after_ref, low_ref, high_ref):
    planes = own_planes(v_ref, d_ref, r_ref, before_ref, after_ref)
    top = iota((8, 128), 0) < DEEP
    for m in range(PLANES // 2):
        a, b = planes[2 * m], planes[2 * m + 1]
        low_ref[m] = jnp.where(top, a(pl.ds(0, 8)), roll(b(pl.ds(0, 8)), DEEP, 0))
        high_ref[m] = jnp.where(top, roll(a(pl.ds(8, 8)), DEEP, 0), b(pl.ds(8, 8)))


def z_faces(v_ref, d_ref, r_ref, before_ref, after_ref, y_before_ref, y_after_ref, main_ref, low_ref, high_ref):
    planes = own_planes(v_ref, d_ref, r_ref, before_ref, after_ref)
    top = iota((8, 128), 0) < DEEP
    group = iota((ROWS, 128), 1) // DEEP
    for block in range(BLOCKS):
        low = high = jnp.zeros((ROWS, 128), jnp.float32)
        for k in range(PER_BLOCK):
            plane = block * PER_BLOCK + k
            before, after = y_before_ref[plane // 2], y_after_ref[plane // 2]
            if plane % 2:
                halo = jnp.where(top, roll(after, DEEP, 0), before)
            else:
                halo = jnp.where(top, after, roll(before, DEEP, 0))
            value = jnp.concatenate([planes[plane](pl.ds(0, 16)), halo], 0)
            main_ref[plane] = value
            low = jnp.where(group == k, roll(value, DEEP * k, 1), low)
            high = jnp.where(group == k, roll(value, DEEP * k + DEEP, 1), high)
        low_ref[block] = low
        high_ref[block] = high


def masks():
    first = {axis: lax.axis_index(axis) == 0 for axis in AXES}
    final = {axis: lax.axis_index(axis) == lax.axis_size(axis) - 1 for axis in AXES}

    def keep(flag):
        return jnp.where(flag, 0.0, 1.0).astype(jnp.float32)

    row, lane = iota((ROWS, 128), 0), iota((ROWS, 128), 1)
    after, before = keep(final["gy"]), keep(first["gy"])
    main = jnp.where(row < 16, 1.0, jnp.where(row < 16 + DEEP, after, before))
    side = main * jnp.where(lane < 64, keep(final["gz"]), keep(first["gz"]))
    return (main, side), keep(first["gx"]), keep(final["gx"])


def mask_of(x, pair, before, after):
    if 0 <= x < 4:
        return pair
    factor = before if x < 0 else after
    return tuple(mask * factor for mask in pair)


def next_y(value):
    return roll(value, -1, 0)


def next_z(main, side):
    end = iota(main.shape, 1) == 127
    moved_main, moved_side = roll(main, -1, 1), roll(side, -1, 1)
    return jnp.where(end, moved_side, moved_main), jnp.where(end, moved_main, moved_side)


def previous_z(main, side):
    end = iota(main.shape, 1) == 0
    moved_main, moved_side = roll(main, 1, 1), roll(side, 1, 1)
    return jnp.where(end, moved_side, moved_main), jnp.where(end, moved_main, moved_side)


def cx_at(s, x):
    return s * 7 + x + 2


def cy_at(s, x):
    return SPECIES * 7 + s * 6 + x + 1


def cz_at(s, x):
    return SPECIES * 13 + s * 6 + x + 1


CONDUCTS = SPECIES * 19


def conduct(d_of, out_ref):
    for s in range(SPECIES):
        for x in V_PLANES:
            d = d_of(s, x)
            if x < V_PLANES[-1]:
                after = d_of(s, x + 1)
                for part in range(2):
                    out_ref[part, cx_at(s, x)] = 0.5 * (d[part] + after[part])
            if x in R_PLANES:
                after = next_z(*d)
                for part in range(2):
                    out_ref[part, cy_at(s, x)] = 0.5 * (d[part] + next_y(d[part]))
                    out_ref[part, cz_at(s, x)] = 0.5 * (d[part] + after[part])


def step(degree, planes, v_of, main_ref, side_ref, c_ref, mask, store):
    for x in planes:
        factor = mask_of(x, *mask)
        here = [v_of(t, x) for t in range(SPECIES)]
        for s in range(SPECIES):
            v, before, after = here[s], v_of(s, x - 1), v_of(s, x + 1)
            follow = next_z(*v)
            flux = [c_ref[part, cz_at(s, x)] * (v[part] - follow[part]) for part in range(2)]
            came = previous_z(*flux)
            out = []
            for part, r_ref in ((0, main_ref), (1, side_ref)):
                value = v[part] * (1.0 - SHIFTS[degree]) + (flux[part] - came[part])
                for t in range(SPECIES):
                    value = value + r_ref[r_at(s, t, x)] * here[t][part]
                value = value + c_ref[part, cx_at(s, x)] * (v[part] - after[part])
                value = value + c_ref[part, cx_at(s, x - 1)] * (v[part] - before[part])
                along = c_ref[part, cy_at(s, x)] * (v[part] - next_y(v[part]))
                value = value + (along - roll(along, 1, 0))
                out.append(value * (DAMPING * factor[part]))
            store(s, x, out)


def put_own(out_ref, s, x, value):
    out_ref[8 * s + 2 * x] = value[:8]
    out_ref[8 * s + 2 * x + 1] = value[8:16]


def first_steps(main_ref, before_ref, after_ref, v1_ref, v2_ref, wide_ref, low_ref, high_ref, side_ref, c_ref, v_in, v_mid):
    lane = iota((ROWS, 128), 1)
    near = lane < 64
    for plane in range(PLANES):
        block, k = divmod(plane, PER_BLOCK)
        after, before = roll(after_ref[block], -DEEP * k, 1), roll(before_ref[block], 128 - DEEP - DEEP * k, 1)
        side_ref[plane] = jnp.where(near, after, before)
    mask = masks()

    def inside(plane, x):
        factor = mask_of(x, *mask)
        return main_ref[plane] * factor[0], side_ref[plane] * factor[1]

    conduct(lambda s, x: inside(d_at(s, x), x), c_ref)
    for s in range(SPECIES):
        for x in V_PLANES:
            v_in[0, v_at(s, x)], v_in[1, v_at(s, x)] = inside(v_at(s, x), x)

    def store_mid(s, x, value):
        for part in range(2):
            v_mid[part, 6 * s + x + 1] = value[part]
        if 0 <= x < 4:
            put_own(v1_ref, s, x, value[0])

    def store_wide(s, x, value):
        for part in range(2):
            wide_ref[part, 4 * s + x] = value[part]
        put_own(v2_ref, s, x, value[0])

    def first(s, x):
        return v_in[0, v_at(s, x)], v_in[1, v_at(s, x)]

    def middle(s, x):
        return v_mid[0, 6 * s + x + 1], v_mid[1, 6 * s + x + 1]

    step(0, R_PLANES, first, main_ref, side_ref, c_ref, mask, store_mid)
    step(1, range(4), middle, main_ref, side_ref, c_ref, mask, store_wide)
    group = ((lane + DEEP) // 8) % 16
    for face, start in ((low_ref, 0), (high_ref, 4 - WIDE)):
        packed = jnp.zeros((ROWS, 128), jnp.float32)
        for s in range(SPECIES):
            for n in range(WIDE):
                k = s * WIDE + n
                face[k] = wide_ref[0, 4 * s + start + n]
                packed = jnp.where(group == k, roll(wide_ref[1, 4 * s + start + n], 8 * k, 1), packed)
        face[SPECIES * WIDE] = packed


def last_steps(main_ref, side_ref, c_ref, wide_ref, before_ref, after_ref, q_ref, v1_ref, v2_ref, sums_in, v3_ref, v4_ref, sums_ref, v_in, v_mid):
    mask = masks()
    for s in range(SPECIES):
        for face, start, factor in ((before_ref, -WIDE, mask[1]), (after_ref, 4, mask[2])):
            for n in range(WIDE):
                k = s * WIDE + n
                v_in[0, v_at(s, start + n)] = face[k] * factor
                v_in[1, v_at(s, start + n)] = roll(face[SPECIES * WIDE], -8 * k, 1) * factor

    def first(s, x):
        if 0 <= x < 4:
            return wide_ref[0, 4 * s + x], wide_ref[1, 4 * s + x]
        return v_in[0, v_at(s, x)], v_in[1, v_at(s, x)]

    def middle(s, x):
        return v_mid[0, 6 * s + x + 1], v_mid[1, 6 * s + x + 1]

    def store_mid(s, x, value):
        for part in range(2):
            v_mid[part, 6 * s + x + 1] = value[part]
        if 0 <= x < 4:
            put_own(v3_ref, s, x, value[0])

    step(2, R_PLANES, first, main_ref, side_ref, c_ref, mask, store_mid)
    step(3, range(4), middle, main_ref, side_ref, c_ref, mask, lambda s, x, value: put_own(v4_ref, s, x, value[0]))

    def load(i):
        return [q_ref[a, i] for a in range(EARLIER)] + [v1_ref[i], v2_ref[i], v3_ref[i], v4_ref[i]]

    row = sums_in[...] + products(new_pairs(2) + new_pairs(3), load, q_ref.shape[1])
    sums_ref[...] = jnp.broadcast_to(jnp.sum(row, 0, keepdims=True), sums_ref.shape)


def middle_products(q_ref, v1_ref, v2_ref, before_ref, out_ref):
    def load(i):
        return [q_ref[a, i] for a in range(EARLIER)] + [v1_ref[i], v2_ref[i]]

    out_ref[...] = before_ref[...] + products(new_pairs(0) + new_pairs(1), load, q_ref.shape[1])


def products(pairs, load, count):
    def body(i, sums):
        values = load(i)
        return tuple(total + values[a] * values[b] for total, (a, b) in zip(sums, pairs))

    zero = jnp.zeros((8, 128), jnp.float32)
    sums = lax.fori_loop(0, count, body, (zero,) * len(pairs))
    lane = lax.broadcasted_iota(jnp.int32, (8, 128), 1)
    row = zero
    for total, pair in zip(sums, pairs):
        row = jnp.where(lane == SLOT[pair], jnp.sum(total, 1, keepdims=True), row)
    return row


def earlier_products(q_ref, out_ref):
    pairs = [(a, b) for b in range(EARLIER) for a in range(b + 1)]
    out_ref[...] = products(pairs, lambda i: [q_ref[a, i] for a in range(EARLIER)], q_ref.shape[1])


def new_pairs(number):
    return [(a, EARLIER + number) for a in range(EARLIER + number + 1)]


def finish_kernel(entries, sums_ref, q_ref, *refs):
    v_refs, (new_ref, coeff_ref, triangle_ref) = refs[:STEPS], refs[STEPS:]
    total = sums_ref[0]
    for i in range(1, sums_ref.shape[0]):
        total = total + sums_ref[i]
    total = jnp.broadcast_to(jnp.sum(total, 0, keepdims=True), total.shape) * (1.0 / entries)

    def entry(a, b):
        k = SLOT[(min(a, b), max(a, b))]
        return jnp.broadcast_to(total[:, k : k + 1], total.shape)

    coeff = [[entry(i, EARLIER + j) for j in range(STEPS)] for i in range(EARLIER)]
    overlap = {(a, b): entry(a, b) for b in range(EARLIER) for a in range(b + 1)}
    gram = {}
    for k in range(STEPS):
        mixed = []
        for i in range(EARLIER):
            term = -2.0 * coeff[i][k]
            for m in range(EARLIER):
                term = term + overlap[(min(i, m), max(i, m))] * coeff[m][k]
            mixed.append(term)
        for j in range(k, STEPS):
            value = entry(EARLIER + k, EARLIER + j)
            for i in range(EARLIER):
                value = value + coeff[i][j] * mixed[i]
            gram[(j, k)] = value
    factor, inverse = {}, []
    for k in range(STEPS):
        pivot = gram[(k, k)]
        for m in range(k):
            pivot = pivot - factor[(k, m)] * factor[(k, m)]
        factor[(k, k)] = jnp.sqrt(pivot)
        inverse.append(1.0 / factor[(k, k)])
        for j in range(k + 1, STEPS):
            value = gram[(j, k)]
            for m in range(k):
                value = value - factor[(j, m)] * factor[(k, m)]
            factor[(j, k)] = value * inverse[k]
    row = lax.broadcasted_iota(jnp.int32, total.shape, 0)
    lane = lax.broadcasted_iota(jnp.int32, total.shape, 1)
    table = jnp.zeros_like(total)
    for i in range(EARLIER):
        for j in range(STEPS):
            table = jnp.where((row == j) & (lane == i), coeff[i][j], table)
    coeff_ref[...] = table[:STEPS, :EARLIER]
    table = jnp.zeros_like(total)
    for (j, k), value in factor.items():
        table = jnp.where((row == k) & (lane == j), value, table)
    triangle_ref[...] = table[:STEPS, :STEPS]

    def body(n, carry):
        earlier = [q_ref[i, n] for i in range(EARLIER)]
        done = []
        for j in range(STEPS):
            value = v_refs[j][n]
            for i in range(EARLIER):
                value = value - coeff[i][j] * earlier[i]
            for k in range(j):
                value = value - factor[(j, k)] * done[k]
            done.append(value * inverse[j])
            new_ref[j, n] = done[j]
        return carry

    lax.fori_loop(0, q_ref.shape[1], body, 0)


def call(body, outs, cost, *args, **more):
    return pl.pallas_call(
        body,
        out_shape=[jax.ShapeDtypeStruct(shape, jnp.float32) for shape in outs],
        cost_estimate=pl.CostEstimate(flops=cost, bytes_accessed=cost, transcendentals=0),
        compiler_params=pltpu.CompilerParams(vmem_limit_bytes=24 << 20),
        **more,
    )(*args)


def exchange(axis, low, high):
    count = lax.axis_size(axis)
    up = [(i, (i + 1) % count) for i in range(count)]
    down = [(target, source) for source, target in up]
    return lax.ppermute(high, axis, up), lax.ppermute(low, axis, down)


def on_device(earlier_basis, diffusivity, reaction):
    span_x, span_y, span_z = diffusivity.shape[1:]
    tiles = SPECIES * span_x * span_y // 8
    devices = 1
    for axis in AXES:
        devices *= lax.axis_size(axis)
    entries = tiles * 8 * span_z * devices
    in_hbm = pl.BlockSpec(memory_space=pltpu.HBM)
    given = (earlier_basis, diffusivity, reaction)
    face = (2 * SPECIES * WIDE + SPECIES * SPECIES, span_y, span_z)
    field = diffusivity.shape
    low, high, *kept = call(
        x_faces,
        [face, face, field, field],
        1 << 20,
        *[pltpu.with_memory_space_constraint(a, pltpu.HBM) for a in given],
        in_specs=[in_hbm] * 3,
        scratch_shapes=[pltpu.SemaphoreType.DMA((6 * SPECIES + 2,))],
    )
    x_halos = exchange("gx", low, high)
    kept.append(reaction)
    face = (PLANES // 2, 8, span_z)
    y_halos = exchange("gy", *call(y_faces, [face, face], 1 << 20, *kept, *x_halos))
    face = (BLOCKS, ROWS, span_z)
    whole = (PLANES, ROWS, span_z)
    main, low, high = call(z_faces, [whole, face, face], 1 << 20, *kept, *x_halos, *y_halos)
    z_halos = exchange("gz", low, high)
    basis = earlier_basis.reshape(EARLIER, tiles, 8, span_z)
    (sums,) = call(earlier_products, [(8, span_z)], 4 << 20, basis)
    own = (tiles, 8, span_z)
    face = (SPECIES * WIDE + 1, ROWS, span_z)
    scratch = [
        pltpu.VMEM((2, SPECIES * len(V_PLANES), ROWS, span_z), jnp.float32),
        pltpu.VMEM((2, SPECIES * len(R_PLANES), ROWS, span_z), jnp.float32),
    ]
    v1, v2, wide, low, high, side, conducts = call(
        first_steps,
        [own, own, (2, SPECIES * span_x, ROWS, span_z), face, face, whole, (2, CONDUCTS, ROWS, span_z)],
        1 << 20,
        main,
        *z_halos,
        scratch_shapes=scratch,
    )
    halos = exchange("gx", low, high)
    (sums,) = call(middle_products, [(8, span_z)], 4 << 20, basis, v1, v2, sums)
    v3, v4, rows = call(
        last_steps,
        [own, own, (devices, span_z)],
        1 << 20,
        main,
        side,
        conducts,
        wide,
        *halos,
        basis,
        v1,
        v2,
        sums,
        scratch_shapes=scratch,
    )
    rows = lax.all_to_all(rows.reshape(devices, 1, span_z), AXES, 0, 0)
    new, coeff, triangle = call(
        functools.partial(finish_kernel, entries),
        [(STEPS, tiles, 8, span_z), (STEPS, EARLIER), (STEPS, STEPS)],
        1 << 20,
        rows.reshape(devices // 8, 8, span_z),
        basis,
        v1,
        v2,
        v3,
        v4,
    )
    return new.reshape((STEPS, SPECIES, span_x, span_y, span_z)), coeff.T, triangle


def solution(mesh):
    in_specs = (
        P(None, None, "gx", "gy", "gz"),
        P(None, "gx", "gy", "gz"),
        P(None, None, "gx", "gy", "gz"),
    )
    out_specs = (P(None, None, "gx", "gy", "gz"), P(), P())
    return jax.shard_map(
        on_device, mesh=mesh, in_specs=in_specs, out_specs=out_specs, check_vma=False
    )
```

```python
import functools

import jax
import jax.numpy as jnp
from jax import lax
from jax.experimental import pallas as pl
from jax.experimental.pallas import tpu as pltpu
from jax.sharding import PartitionSpec as P

SPECIES = 4
STEPS = 4
EARLIER = 8
SHIFTS = (6.0, 9.0, 14.0, 17.0)
DAMPING = 0.2
AXES = ("gx", "gy", "gz")

VECTORS = EARLIER + STEPS
SLOT = {}
for _b in range(VECTORS):
    for _a in range(_b + 1):
        SLOT[(_a, _b)] = len(SLOT)

WIDE = 2
DEEP = 4
ROWS = 24
V_PLANES = tuple(range(-WIDE, 4 + WIDE))
R_PLANES = tuple(range(-1, 5))
V_BASE = 0
D_BASE = SPECIES * len(V_PLANES)
R_BASE = 2 * D_BASE
PLANES = R_BASE + SPECIES * SPECIES * len(R_PLANES)
HALVES = SPECIES // 2
SIDES = 2 * HALVES + HALVES * SPECIES
BLOCKS = SIDES // 2


def v_at(s, x):
    return V_BASE + s * len(V_PLANES) + x + WIDE


def d_at(s, x):
    return D_BASE + s * len(V_PLANES) + x + WIDE


def r_at(s, t, x):
    return R_BASE + (s * SPECIES + t) * len(R_PLANES) + x + 1


def iota(shape, dim):
    return lax.broadcasted_iota(jnp.int32, shape, dim)


def roll(value, shift, axis):
    shift %= value.shape[axis]
    return pltpu.roll(value, shift, axis) if shift else value


def x_faces(q_ref, d_ref, r_ref, low_ref, high_ref, v_out, d_out, sems):
    copies = [(q_ref.at[EARLIER - 1], v_out), (d_ref, d_out)]
    for face, planes, plane in ((low_ref, pl.ds(0, WIDE), 0), (high_ref, pl.ds(4 - WIDE, WIDE), 3)):
        for s in range(SPECIES):
            copies.append((q_ref.at[EARLIER - 1, s, planes], face.at[pl.ds(s * WIDE, WIDE)]))
            copies.append((d_ref.at[s, planes], face.at[pl.ds((SPECIES + s) * WIDE, WIDE)]))
            start = 2 * SPECIES * WIDE + s * SPECIES
            copies.append((r_ref.at[s, :, plane], face.at[pl.ds(start, SPECIES)]))
    started = [pltpu.make_async_copy(a, b, sems.at[n]) for n, (a, b) in enumerate(copies)]
    for copy in started:
        copy.start()
    for copy in started:
        copy.wait()


def own_planes(v_ref, d_ref, r_ref, before_ref, after_ref):
    def pick(own, slot, width, x):
        if x < 0:
            return lambda rows: before_ref[slot + x + width, rows]
        if x > 3:
            return lambda rows: after_ref[slot + x - 4, rows]
        return lambda rows: own(x, rows)

    planes = []
    for s in range(SPECIES):
        for x in V_PLANES:
            planes.append(pick(lambda x, rows, s=s: v_ref[s, x, rows], s * WIDE, WIDE, x))
    for s in range(SPECIES):
        for x in V_PLANES:
            planes.append(pick(lambda x, rows, s=s: d_ref[s, x, rows], (SPECIES + s) * WIDE, WIDE, x))
    for s in range(SPECIES):
        for t in range(SPECIES):
            slot = 2 * SPECIES * WIDE + s * SPECIES + t
            for x in R_PLANES:
                planes.append(pick(lambda x, rows, s=s, t=t: r_ref[s, t, x, rows], slot, 1, x))
    return planes


def y_faces(v_ref, d_ref, r_ref, before_ref, after_ref, low_ref, high_ref):
    planes = own_planes(v_ref, d_ref, r_ref, before_ref, after_ref)
    top = iota((8, 128), 0) < DEEP
    for m in range(PLANES // 2):
        a, b = planes[2 * m], planes[2 * m + 1]
        low_ref[m] = jnp.where(top, a(pl.ds(0, 8)), roll(b(pl.ds(0, 8)), DEEP, 0))
        high_ref[m] = jnp.where(top, roll(a(pl.ds(8, 8)), DEEP, 0), b(pl.ds(8, 8)))


def side_planes(side):
    found = []
    for half in range(2):
        for x in V_PLANES:
            if side < 2 * HALVES:
                s = side % HALVES * 2 + half
                found.append(v_at(s, x) if side < HALVES else d_at(s, x))
            else:
                pair, t = divmod(side - 2 * HALVES, SPECIES)
                found.append(r_at(2 * pair + half, t, x) if x in R_PLANES else None)
    return found


def z_faces(v_ref, d_ref, r_ref, before_ref, after_ref, y_before_ref, y_after_ref, main_ref, low_ref, high_ref):
    planes = own_planes(v_ref, d_ref, r_ref, before_ref, after_ref)
    top = iota((8, 128), 0) < DEEP
    group = iota((ROWS, 128), 1) // DEEP
    for block in range(BLOCKS):
        low = high = jnp.zeros((ROWS, 128), jnp.float32)
        for part in range(2):
            for slot, plane in enumerate(side_planes(2 * block + part)):
                if plane is None:
                    continue
                before, after = y_before_ref[plane // 2], y_after_ref[plane // 2]
                if plane % 2:
                    halo = jnp.where(top, roll(after, DEEP, 0), before)
                else:
                    halo = jnp.where(top, after, roll(before, DEEP, 0))
                value = jnp.concatenate([planes[plane](pl.ds(0, 16)), halo], 0)
                main_ref[plane] = value
                k = 2 * slot + part
                low = jnp.where(group == k, roll(value, DEEP * k, 1), low)
                high = jnp.where(group == k, roll(value, DEEP * k + DEEP, 1), high)
        low_ref[block] = low
        high_ref[block] = high


def masks():
    first = {axis: lax.axis_index(axis) == 0 for axis in AXES}
    final = {axis: lax.axis_index(axis) == lax.axis_size(axis) - 1 for axis in AXES}

    def keep(flag):
        return jnp.where(flag, 0.0, 1.0).astype(jnp.float32)

    row, lane = iota((ROWS, 128), 0), iota((ROWS, 128), 1)
    main = jnp.where(row < 16, 1.0, jnp.where(row < 16 + DEEP, keep(final["gy"]), keep(first["gy"])))
    slot = lane // 8 % 8
    side = main * jnp.where(lane % 8 < DEEP, keep(first["gz"]), keep(final["gz"]))
    before, after = keep(first["gx"]), keep(final["gx"])
    side = side * jnp.where(slot < WIDE, before, jnp.where(slot < WIDE + 4, 1.0, after))
    return main, side, before, after


def mask_of(x, main, before, after):
    if 0 <= x < 4:
        return main
    return main * (before if x < 0 else after)


def next_y(value):
    return roll(value, -1, 0)


def slot_of(s, x):
    return 64 * (s % 2) + 8 * (x + WIDE)


def column(planes, value_of, source, target):
    lane = iota((ROWS, 128), 1)
    found = []
    for half in range(HALVES):
        value = jnp.zeros((ROWS, 128), jnp.float32)
        for s in (2 * half, 2 * half + 1):
            for x in planes:
                place = slot_of(s, x) + target
                value = jnp.where(lane == place, roll(value_of(s, x), place - source, 1), value)
        found.append(value)
    return found


def next_z(value, side, place):
    lane = iota((ROWS, 128), 1)
    return jnp.where(lane == 127, roll(side, 127 - place - DEEP, 1), roll(value, -1, 1))


def previous_z(value, side, place):
    lane = iota((ROWS, 128), 1)
    return jnp.where(lane == 0, roll(side, -(place + DEEP - 1), 1), roll(value, 1, 1))


def side_next_z(side, edge):
    return jnp.where(iota((ROWS, 128), 1) % 8 == DEEP - 1, edge, roll(side, -1, 1))


def side_previous_z(side, edge):
    return jnp.where(iota((ROWS, 128), 1) % 8 == DEEP, edge, roll(side, 1, 1))


def cx_at(s, x):
    return s * 7 + x + 2


def cy_at(s, x):
    return SPECIES * 7 + s * 6 + x + 1


def cz_at(s, x):
    return SPECIES * 13 + s * 6 + x + 1


CONDUCTS = SPECIES * 19


def conduct(d_of, d_side, c_ref, c_side):
    for s in range(SPECIES):
        for x in V_PLANES:
            d = d_of(s, x)
            if x < V_PLANES[-1]:
                c_ref[cx_at(s, x)] = 0.5 * (d + d_of(s, x + 1))
            if x in R_PLANES:
                c_ref[cy_at(s, x)] = 0.5 * (d + next_y(d))
                c_ref[cz_at(s, x)] = 0.5 * (d + next_z(d, d_side[s // 2], slot_of(s, x)))
    edges = column(R_PLANES, d_of, 0, DEEP - 1)
    for half in range(HALVES):
        d = d_side[half]
        c_side[3 * half] = 0.5 * (d + roll(d, -8, 1))
        c_side[3 * half + 1] = 0.5 * (d + next_y(d))
        c_side[3 * half + 2] = 0.5 * (d + side_next_z(d, edges[half]))


def step(degree, planes, v_of, v_side, main_ref, side_ref, c_ref, c_side, mask, store, sides=True):
    lane = iota((ROWS, 128), 1)
    edges = column(planes, v_of, 0, DEEP - 1)
    flux_side = [c_side[3 * h + 2] * (v_side[h] - side_next_z(v_side[h], edges[h])) for h in range(HALVES)]
    last = [jnp.zeros((ROWS, 128), jnp.float32)] * HALVES
    for x in planes:
        factor = DAMPING * mask_of(x, mask[0], *mask[2:])
        here = [v_of(t, x) for t in range(SPECIES)]
        for s in range(SPECIES):
            half, place, v = s // 2, slot_of(s, x), here[s]
            flux = c_ref[cz_at(s, x)] * (v - next_z(v, v_side[half], place))
            value = v * (1.0 - SHIFTS[degree]) + (flux - previous_z(flux, flux_side[half], place))
            if sides:
                moved = roll(flux, place + DEEP - 127, 1)
                last[half] = jnp.where(lane == place + DEEP, moved, last[half])
            for t in range(SPECIES):
                value = value + main_ref[r_at(s, t, x)] * here[t]
            value = value + c_ref[cx_at(s, x)] * (v - v_of(s, x + 1))
            value = value + c_ref[cx_at(s, x - 1)] * (v - v_of(s, x - 1))
            along = c_ref[cy_at(s, x)] * (v - next_y(v))
            value = value + (along - roll(along, 1, 0))
            store(s, x, value * factor)
    if not sides:
        return None
    both = []
    for half in range(HALVES):
        other = roll(v_side[half], 64, 1)
        both.append(jnp.where(lane < 64, v_side[half], other))
        both.append(jnp.where(lane < 64, other, v_side[half]))
    result = []
    for half in range(HALVES):
        v = v_side[half]
        value = v * (1.0 - SHIFTS[degree]) + (flux_side[half] - side_previous_z(flux_side[half], last[half]))
        for t in range(SPECIES):
            value = value + side_ref[2 * HALVES + SPECIES * half + t] * both[t]
        across = c_side[3 * half] * (v - roll(v, -8, 1))
        value = value + (across - roll(across, 8, 1))
        along = c_side[3 * half + 1] * (v - next_y(v))
        value = value + (along - roll(along, 1, 0))
        result.append(value * (DAMPING * mask[1]))
    return result


def put_own(out_ref, s, x, value):
    out_ref[8 * s + 2 * x] = value[:8]
    out_ref[8 * s + 2 * x + 1] = value[8:16]


def first_steps(main_ref, before_ref, after_ref, v1_ref, v2_ref, wide_ref, wide_side, low_ref, high_ref, side_ref, c_ref, c_side, v_in, v_mid):
    lane = iota((ROWS, 128), 1)
    early = lane % 8 < DEEP
    for block in range(BLOCKS):
        before, after = before_ref[block], after_ref[block]
        side_ref[2 * block] = jnp.where(early, before, roll(after, DEEP, 1))
        side_ref[2 * block + 1] = jnp.where(early, roll(before, -DEEP, 1), after)
    mask = masks()

    def inside(plane, x):
        return main_ref[plane] * mask_of(x, mask[0], *mask[2:])

    v_side = [side_ref[half] * mask[1] for half in range(HALVES)]
    d_side = [side_ref[HALVES + half] * mask[1] for half in range(HALVES)]
    for s in range(SPECIES):
        for x in V_PLANES:
            v_mid[v_at(s, x)] = inside(d_at(s, x), x)
            v_in[v_at(s, x)] = inside(v_at(s, x), x)
    conduct(lambda s, x: v_mid[v_at(s, x)], d_side, c_ref, c_side)

    def store_mid(s, x, value):
        v_mid[v_at(s, x)] = value
        if 0 <= x < 4:
            put_own(v1_ref, s, x, value)

    def store_wide(s, x, value):
        wide_ref[4 * s + x] = value
        put_own(v2_ref, s, x, value)

    more = (main_ref, side_ref, c_ref, c_side, mask)
    v_side = step(0, R_PLANES, lambda s, x: v_in[v_at(s, x)], v_side, *more, store_mid)
    v_side = step(1, range(4), lambda s, x: v_mid[v_at(s, x)], v_side, *more, store_wide)
    for half in range(HALVES):
        wide_side[half] = v_side[half]
    slot = lane // 8 % 8
    for face, start, shift in ((low_ref, 0, -16), (high_ref, 4 - WIDE, 16)):
        for s in range(SPECIES):
            for n in range(WIDE):
                face[s * WIDE + n] = wide_ref[4 * s + start + n]
        kept = (slot >= start + WIDE) & (slot < start + 2 * WIDE)
        face[SPECIES * WIDE] = jnp.where(kept, v_side[0], roll(v_side[1], shift, 1))


def last_steps(main_ref, side_ref, c_ref, c_side, wide_ref, wide_side, before_ref, after_ref, q_ref, v1_ref, v2_ref, sums_in, v3_ref, v4_ref, sums_ref, v_in, v_mid):
    mask = masks()
    for s in range(SPECIES):
        for face, start, factor in ((before_ref, -WIDE, mask[2]), (after_ref, 4, mask[3])):
            for n in range(WIDE):
                v_in[v_at(s, start + n)] = face[s * WIDE + n] * factor
    slot = iota((ROWS, 128), 1) // 8 % 8
    before, after = before_ref[SPECIES * WIDE] * mask[2], after_ref[SPECIES * WIDE] * mask[3]
    v_side = []
    for half in range(HALVES):
        value = jnp.where(slot < WIDE, roll(before, -32 - 16 * half, 1), wide_side[half])
        v_side.append(jnp.where(slot >= WIDE + 4, roll(after, 32 + 16 * half, 1), value))

    def first(s, x):
        return wide_ref[4 * s + x] if 0 <= x < 4 else v_in[v_at(s, x)]

    def store_mid(s, x, value):
        v_mid[v_at(s, x)] = value
        if 0 <= x < 4:
            put_own(v3_ref, s, x, value)

    def store_last(s, x, value):
        put_own(v4_ref, s, x, value)

    more = (main_ref, side_ref, c_ref, c_side, mask)
    v_side = step(2, R_PLANES, first, v_side, *more, store_mid)
    step(3, range(4), lambda s, x: v_mid[v_at(s, x)], v_side, *more, store_last, sides=False)

    def load(i):
        return [q_ref[a, i] for a in range(EARLIER)] + [v1_ref[i], v2_ref[i], v3_ref[i], v4_ref[i]]

    row = sums_in[...] + products(new_pairs(2) + new_pairs(3), load, q_ref.shape[1])
    sums_ref[...] = jnp.broadcast_to(jnp.sum(row, 0, keepdims=True), sums_ref.shape)


def middle_products(q_ref, v1_ref, v2_ref, before_ref, out_ref):
    def load(i):
        return [q_ref[a, i] for a in range(EARLIER)] + [v1_ref[i], v2_ref[i]]

    out_ref[...] = before_ref[...] + products(new_pairs(0) + new_pairs(1), load, q_ref.shape[1])


def products(pairs, load, count):
    def body(i, sums):
        values = load(i)
        return tuple(total + values[a] * values[b] for total, (a, b) in zip(sums, pairs))

    zero = jnp.zeros((8, 128), jnp.float32)
    sums = lax.fori_loop(0, count, body, (zero,) * len(pairs))
    lane = lax.broadcasted_iota(jnp.int32, (8, 128), 1)
    row = zero
    for total, pair in zip(sums, pairs):
        row = jnp.where(lane == SLOT[pair], jnp.sum(total, 1, keepdims=True), row)
    return row


def earlier_products(q_ref, out_ref):
    pairs = [(a, b) for b in range(EARLIER) for a in range(b + 1)]
    out_ref[...] = products(pairs, lambda i: [q_ref[a, i] for a in range(EARLIER)], q_ref.shape[1])


def new_pairs(number):
    return [(a, EARLIER + number) for a in range(EARLIER + number + 1)]


def finish_kernel(entries, sums_ref, q_ref, *refs):
    v_refs, (new_ref, coeff_ref, triangle_ref) = refs[:STEPS], refs[STEPS:]
    total = sums_ref[0]
    for i in range(1, sums_ref.shape[0]):
        total = total + sums_ref[i]
    total = jnp.broadcast_to(jnp.sum(total, 0, keepdims=True), total.shape) * (1.0 / entries)

    def entry(a, b):
        k = SLOT[(min(a, b), max(a, b))]
        return jnp.broadcast_to(total[:, k : k + 1], total.shape)

    coeff = [[entry(i, EARLIER + j) for j in range(STEPS)] for i in range(EARLIER)]
    overlap = {(a, b): entry(a, b) for b in range(EARLIER) for a in range(b + 1)}
    gram = {}
    for k in range(STEPS):
        mixed = []
        for i in range(EARLIER):
            term = -2.0 * coeff[i][k]
            for m in range(EARLIER):
                term = term + overlap[(min(i, m), max(i, m))] * coeff[m][k]
            mixed.append(term)
        for j in range(k, STEPS):
            value = entry(EARLIER + k, EARLIER + j)
            for i in range(EARLIER):
                value = value + coeff[i][j] * mixed[i]
            gram[(j, k)] = value
    factor, inverse = {}, []
    for k in range(STEPS):
        pivot = gram[(k, k)]
        for m in range(k):
            pivot = pivot - factor[(k, m)] * factor[(k, m)]
        factor[(k, k)] = jnp.sqrt(pivot)
        inverse.append(1.0 / factor[(k, k)])
        for j in range(k + 1, STEPS):
            value = gram[(j, k)]
            for m in range(k):
                value = value - factor[(j, m)] * factor[(k, m)]
            factor[(j, k)] = value * inverse[k]
    row = lax.broadcasted_iota(jnp.int32, total.shape, 0)
    lane = lax.broadcasted_iota(jnp.int32, total.shape, 1)
    table = jnp.zeros_like(total)
    for i in range(EARLIER):
        for j in range(STEPS):
            table = jnp.where((row == j) & (lane == i), coeff[i][j], table)
    coeff_ref[...] = table[:STEPS, :EARLIER]
    table = jnp.zeros_like(total)
    for (j, k), value in factor.items():
        table = jnp.where((row == k) & (lane == j), value, table)
    triangle_ref[...] = table[:STEPS, :STEPS]

    def body(n, carry):
        earlier = [q_ref[i, n] for i in range(EARLIER)]
        done = []
        for j in range(STEPS):
            value = v_refs[j][n]
            for i in range(EARLIER):
                value = value - coeff[i][j] * earlier[i]
            for k in range(j):
                value = value - factor[(j, k)] * done[k]
            done.append(value * inverse[j])
            new_ref[j, n] = done[j]
        return carry

    lax.fori_loop(0, q_ref.shape[1], body, 0)


def call(body, outs, cost, *args, **more):
    return pl.pallas_call(
        body,
        out_shape=[jax.ShapeDtypeStruct(shape, jnp.float32) for shape in outs],
        cost_estimate=pl.CostEstimate(flops=cost, bytes_accessed=cost, transcendentals=0),
        compiler_params=pltpu.CompilerParams(vmem_limit_bytes=24 << 20),
        **more,
    )(*args)


def exchange(axis, low, high):
    count = lax.axis_size(axis)
    up = [(i, (i + 1) % count) for i in range(count)]
    down = [(target, source) for source, target in up]
    return lax.ppermute(high, axis, up), lax.ppermute(low, axis, down)


def on_device(earlier_basis, diffusivity, reaction):
    span_x, span_y, span_z = diffusivity.shape[1:]
    tiles = SPECIES * span_x * span_y // 8
    devices = 1
    for axis in AXES:
        devices *= lax.axis_size(axis)
    entries = tiles * 8 * span_z * devices
    in_hbm = pl.BlockSpec(memory_space=pltpu.HBM)
    given = (earlier_basis, diffusivity, reaction)
    face = (2 * SPECIES * WIDE + SPECIES * SPECIES, span_y, span_z)
    field = diffusivity.shape
    low, high, *kept = call(
        x_faces,
        [face, face, field, field],
        1 << 20,
        *[pltpu.with_memory_space_constraint(a, pltpu.HBM) for a in given],
        in_specs=[in_hbm] * 3,
        scratch_shapes=[pltpu.SemaphoreType.DMA((6 * SPECIES + 2,))],
    )
    x_halos = exchange("gx", low, high)
    kept.append(reaction)
    face = (PLANES // 2, 8, span_z)
    y_halos = exchange("gy", *call(y_faces, [face, face], 1 << 20, *kept, *x_halos))
    face = (BLOCKS, ROWS, span_z)
    whole = (PLANES, ROWS, span_z)
    main, low, high = call(z_faces, [whole, face, face], 1 << 20, *kept, *x_halos, *y_halos)
    z_halos = exchange("gz", low, high)
    basis = earlier_basis.reshape(EARLIER, tiles, 8, span_z)
    (sums,) = call(earlier_products, [(8, span_z)], 4 << 20, basis)
    own = (tiles, 8, span_z)
    scratch = [pltpu.VMEM((D_BASE, ROWS, span_z), jnp.float32)] * 2
    several = [
        (count, ROWS, span_z)
        for count in (SPECIES * span_x, HALVES, SPECIES * WIDE + 1, SPECIES * WIDE + 1, SIDES, CONDUCTS, 3 * HALVES)
    ]
    v1, v2, wide, wide_side, low, high, side, conducts, side_conducts = call(
        first_steps,
        [own, own] + several,
        1 << 20,
        main,
        *z_halos,
        scratch_shapes=scratch,
    )
    halos = exchange("gx", low, high)
    (sums,) = call(middle_products, [(8, span_z)], 4 << 20, basis, v1, v2, sums)
    v3, v4, rows = call(
        last_steps,
        [own, own, (devices, span_z)],
        1 << 20,
        main,
        side,
        conducts,
        side_conducts,
        wide,
        wide_side,
        *halos,
        basis,
        v1,
        v2,
        sums,
        scratch_shapes=scratch,
    )
    rows = lax.all_to_all(rows.reshape(devices, 1, span_z), AXES, 0, 0)
    new, coeff, triangle = call(
        functools.partial(finish_kernel, entries),
        [(STEPS, tiles, 8, span_z), (STEPS, EARLIER), (STEPS, STEPS)],
        1 << 20,
        rows.reshape(devices // 8, 8, span_z),
        basis,
        v1,
        v2,
        v3,
        v4,
    )
    return new.reshape((STEPS, SPECIES, span_x, span_y, span_z)), coeff.T, triangle


def solution(mesh):
    in_specs = (
        P(None, None, "gx", "gy", "gz"),
        P(None, "gx", "gy", "gz"),
        P(None, None, "gx", "gy", "gz"),
    )
    out_specs = (P(None, None, "gx", "gy", "gz"), P(), P())
    return jax.shard_map(
        on_device, mesh=mesh, in_specs=in_specs, out_specs=out_specs, check_vma=False
    )
```

```python
import functools

import jax
import jax.numpy as jnp
from jax import lax
from jax.experimental import pallas as pl
from jax.experimental.pallas import tpu as pltpu
from jax.sharding import PartitionSpec as P

SPECIES = 4
STEPS = 4
EARLIER = 8
SHIFTS = (6.0, 9.0, 14.0, 17.0)
DAMPING = 0.2
AXES = ("gx", "gy", "gz")

VECTORS = EARLIER + STEPS
SLOT = {}
for _b in range(VECTORS):
    for _a in range(_b + 1):
        SLOT[(_a, _b)] = len(SLOT)

WIDE = 2
DEEP = 4
ROWS = 24
V_PLANES = tuple(range(-WIDE, 4 + WIDE))
R_PLANES = tuple(range(-1, 5))
V_BASE = 0
D_BASE = SPECIES * len(V_PLANES)
R_BASE = 2 * D_BASE
PLANES = R_BASE + SPECIES * SPECIES * len(R_PLANES)
HALVES = SPECIES // 2
SIDES = 2 * HALVES + HALVES * SPECIES
BLOCKS = SIDES // 2


def v_at(s, x):
    return V_BASE + s * len(V_PLANES) + x + WIDE


def d_at(s, x):
    return D_BASE + s * len(V_PLANES) + x + WIDE


def r_at(s, t, x):
    return R_BASE + (s * SPECIES + t) * len(R_PLANES) + x + 1


def iota(shape, dim):
    return lax.broadcasted_iota(jnp.int32, shape, dim)


def roll(value, shift, axis):
    shift %= value.shape[axis]
    return pltpu.roll(value, shift, axis) if shift else value


def x_faces(q_ref, d_ref, r_ref, low_ref, high_ref, v_out, d_out, sems):
    copies = [(q_ref.at[EARLIER - 1], v_out), (d_ref, d_out)]
    for face, planes, plane in ((low_ref, pl.ds(0, WIDE), 0), (high_ref, pl.ds(4 - WIDE, WIDE), 3)):
        for s in range(SPECIES):
            copies.append((q_ref.at[EARLIER - 1, s, planes], face.at[pl.ds(s * WIDE, WIDE)]))
            copies.append((d_ref.at[s, planes], face.at[pl.ds((SPECIES + s) * WIDE, WIDE)]))
            start = 2 * SPECIES * WIDE + s * SPECIES
            copies.append((r_ref.at[s, :, plane], face.at[pl.ds(start, SPECIES)]))
    started = [pltpu.make_async_copy(a, b, sems.at[n]) for n, (a, b) in enumerate(copies)]
    for copy in started:
        copy.start()
    for copy in started:
        copy.wait()


def own_planes(v_ref, d_ref, r_ref, before_ref, after_ref):
    def pick(own, slot, width, x):
        if x < 0:
            return lambda rows: before_ref[slot + x + width, rows]
        if x > 3:
            return lambda rows: after_ref[slot + x - 4, rows]
        return lambda rows: own(x, rows)

    planes = []
    for s in range(SPECIES):
        for x in V_PLANES:
            planes.append(pick(lambda x, rows, s=s: v_ref[s, x, rows], s * WIDE, WIDE, x))
    for s in range(SPECIES):
        for x in V_PLANES:
            planes.append(pick(lambda x, rows, s=s: d_ref[s, x, rows], (SPECIES + s) * WIDE, WIDE, x))
    for s in range(SPECIES):
        for t in range(SPECIES):
            slot = 2 * SPECIES * WIDE + s * SPECIES + t
            for x in R_PLANES:
                planes.append(pick(lambda x, rows, s=s, t=t: r_ref[s, t, x, rows], slot, 1, x))
    return planes


def y_faces(v_ref, d_ref, r_ref, before_ref, after_ref, low_ref, high_ref):
    planes = own_planes(v_ref, d_ref, r_ref, before_ref, after_ref)
    top = iota((8, 128), 0) < DEEP
    for m in range(PLANES // 2):
        a, b = planes[2 * m], planes[2 * m + 1]
        low_ref[m] = jnp.where(top, a(pl.ds(0, 8)), roll(b(pl.ds(0, 8)), DEEP, 0))
        high_ref[m] = jnp.where(top, roll(a(pl.ds(8, 8)), DEEP, 0), b(pl.ds(8, 8)))


def side_planes(side):
    found = []
    for half in range(2):
        for x in V_PLANES:
            if side < 2 * HALVES:
                s = side % HALVES * 2 + half
                found.append(v_at(s, x) if side < HALVES else d_at(s, x))
            else:
                pair, t = divmod(side - 2 * HALVES, SPECIES)
                found.append(r_at(2 * pair + half, t, x) if x in R_PLANES else None)
    return found


def z_faces(v_ref, d_ref, r_ref, before_ref, after_ref, y_before_ref, y_after_ref, main_ref, low_ref, high_ref):
    planes = own_planes(v_ref, d_ref, r_ref, before_ref, after_ref)
    top = iota((8, 128), 0) < DEEP
    group = iota((ROWS, 128), 1) // DEEP
    for block in range(BLOCKS):
        low = high = jnp.zeros((ROWS, 128), jnp.float32)
        for part in range(2):
            for slot, plane in enumerate(side_planes(2 * block + part)):
                if plane is None:
                    continue
                before, after = y_before_ref[plane // 2], y_after_ref[plane // 2]
                if plane % 2:
                    halo = jnp.where(top, roll(after, DEEP, 0), before)
                else:
                    halo = jnp.where(top, after, roll(before, DEEP, 0))
                value = jnp.concatenate([planes[plane](pl.ds(0, 16)), halo], 0)
                main_ref[plane] = value
                k = 2 * slot + part
                low = jnp.where(group == k, roll(value, DEEP * k, 1), low)
                high = jnp.where(group == k, roll(value, DEEP * k + DEEP, 1), high)
        low_ref[block] = low
        high_ref[block] = high


def masks():
    first = {axis: lax.axis_index(axis) == 0 for axis in AXES}
    final = {axis: lax.axis_index(axis) == lax.axis_size(axis) - 1 for axis in AXES}

    def keep(flag):
        return jnp.where(flag, 0.0, 1.0).astype(jnp.float32)

    row, lane = iota((ROWS, 128), 0), iota((ROWS, 128), 1)
    main = jnp.where(row < 16, 1.0, jnp.where(row < 16 + DEEP, keep(final["gy"]), keep(first["gy"])))
    slot = lane // 8 % 8
    side = main * jnp.where(lane % 8 < DEEP, keep(first["gz"]), keep(final["gz"]))
    before, after = keep(first["gx"]), keep(final["gx"])
    side = side * jnp.where(slot < WIDE, before, jnp.where(slot < WIDE + 4, 1.0, after))
    return main, side, before, after


def mask_of(x, main, before, after):
    if 0 <= x < 4:
        return main
    return main * (before if x < 0 else after)


def next_y(value):
    return roll(value, -1, 0)


def slot_of(s, x):
    return 64 * (s % 2) + 8 * (x + WIDE)


def column(planes, value_of, source, target):
    lane = iota((ROWS, 128), 1)
    found = []
    for half in range(HALVES):
        value = jnp.zeros((ROWS, 128), jnp.float32)
        for s in (2 * half, 2 * half + 1):
            for x in planes:
                place = slot_of(s, x) + target
                value = jnp.where(lane == place, roll(value_of(s, x), place - source, 1), value)
        found.append(value)
    return found


def next_z(value, side, place):
    lane = iota((ROWS, 128), 1)
    return jnp.where(lane == 127, roll(side, 127 - place - DEEP, 1), roll(value, -1, 1))


def previous_z(value, side, place):
    lane = iota((ROWS, 128), 1)
    return jnp.where(lane == 0, roll(side, -(place + DEEP - 1), 1), roll(value, 1, 1))


def side_next_z(side, edge):
    return jnp.where(iota((ROWS, 128), 1) % 8 == DEEP - 1, edge, roll(side, -1, 1))


def side_previous_z(side, edge):
    return jnp.where(iota((ROWS, 128), 1) % 8 == DEEP, edge, roll(side, 1, 1))


def cx_at(s, x):
    return s * 7 + x + 2


def cy_at(s, x):
    return SPECIES * 7 + s * 6 + x + 1


def cz_at(s, x):
    return SPECIES * 13 + s * 6 + x + 1


def back_at(s, x):
    return SPECIES * 19 + s * 6 + x + 1


CONDUCTS = SPECIES * 25


def conduct(d_of, d_side, c_ref, c_side):
    for s in range(SPECIES):
        for x in V_PLANES:
            d = d_of(s, x)
            if x < V_PLANES[-1]:
                c_ref[cx_at(s, x)] = 0.5 * (d + d_of(s, x + 1))
            if x in R_PLANES:
                c_ref[cy_at(s, x)] = 0.5 * (d + next_y(d))
                c_ref[cz_at(s, x)] = 0.5 * (d + next_z(d, d_side[s // 2], slot_of(s, x)))
                c_ref[back_at(s, x)] = 0.5 * (d + previous_z(d, d_side[s // 2], slot_of(s, x)))
    edges = column(R_PLANES, d_of, 0, DEEP - 1)
    ends = column(R_PLANES, d_of, 127, DEEP)
    for half in range(HALVES):
        d = d_side[half]
        c_side[4 * half] = 0.5 * (d + roll(d, -8, 1))
        c_side[4 * half + 1] = 0.5 * (d + next_y(d))
        c_side[4 * half + 2] = 0.5 * (d + side_next_z(d, edges[half]))
        c_side[4 * half + 3] = 0.5 * (d + side_previous_z(d, ends[half]))


def step(degree, planes, v_of, v_side, main_ref, side_ref, c_ref, c_side, mask, store, sides=True):
    lane = iota((ROWS, 128), 1)
    for x in planes:
        factor = DAMPING * mask_of(x, mask[0], *mask[2:])
        here = [v_of(t, x) for t in range(SPECIES)]
        for s in range(SPECIES):
            half, place, v = s // 2, slot_of(s, x), here[s]
            value = v * (1.0 - SHIFTS[degree])
            value = value + c_ref[cz_at(s, x)] * (v - next_z(v, v_side[half], place))
            value = value + c_ref[back_at(s, x)] * (v - previous_z(v, v_side[half], place))
            for t in range(SPECIES):
                value = value + main_ref[r_at(s, t, x)] * here[t]
            value = value + c_ref[cx_at(s, x)] * (v - v_of(s, x + 1))
            value = value + c_ref[cx_at(s, x - 1)] * (v - v_of(s, x - 1))
            along = c_ref[cy_at(s, x)] * (v - next_y(v))
            value = value + (along - roll(along, 1, 0))
            store(s, x, value * factor)
    if not sides:
        return None
    edges = column(planes, v_of, 0, DEEP - 1)
    ends = column(planes, v_of, 127, DEEP)
    both = []
    for half in range(HALVES):
        other = roll(v_side[half], 64, 1)
        both.append(jnp.where(lane < 64, v_side[half], other))
        both.append(jnp.where(lane < 64, other, v_side[half]))
    result = []
    for half in range(HALVES):
        v = v_side[half]
        value = v * (1.0 - SHIFTS[degree])
        value = value + c_side[4 * half + 2] * (v - side_next_z(v, edges[half]))
        value = value + c_side[4 * half + 3] * (v - side_previous_z(v, ends[half]))
        for t in range(SPECIES):
            value = value + side_ref[2 * HALVES + SPECIES * half + t] * both[t]
        across = c_side[4 * half] * (v - roll(v, -8, 1))
        value = value + (across - roll(across, 8, 1))
        along = c_side[4 * half + 1] * (v - next_y(v))
        value = value + (along - roll(along, 1, 0))
        result.append(value * (DAMPING * mask[1]))
    return result


def put_own(out_ref, s, x, value):
    out_ref[8 * s + 2 * x] = value[:8]
    out_ref[8 * s + 2 * x + 1] = value[8:16]


def first_steps(main_ref, before_ref, after_ref, v1_ref, v2_ref, wide_ref, wide_side, low_ref, high_ref, side_ref, c_ref, c_side, v_in, v_mid):
    lane = iota((ROWS, 128), 1)
    early = lane % 8 < DEEP
    for block in range(BLOCKS):
        before, after = before_ref[block], after_ref[block]
        side_ref[2 * block] = jnp.where(early, before, roll(after, DEEP, 1))
        side_ref[2 * block + 1] = jnp.where(early, roll(before, -DEEP, 1), after)
    mask = masks()

    def inside(plane, x):
        return main_ref[plane] * mask_of(x, mask[0], *mask[2:])

    v_side = [side_ref[half] * mask[1] for half in range(HALVES)]
    d_side = [side_ref[HALVES + half] * mask[1] for half in range(HALVES)]
    for s in range(SPECIES):
        for x in V_PLANES:
            v_mid[v_at(s, x)] = inside(d_at(s, x), x)
            v_in[v_at(s, x)] = inside(v_at(s, x), x)
    conduct(lambda s, x: v_mid[v_at(s, x)], d_side, c_ref, c_side)

    def store_mid(s, x, value):
        v_mid[v_at(s, x)] = value
        if 0 <= x < 4:
            put_own(v1_ref, s, x, value)

    def store_wide(s, x, value):
        wide_ref[4 * s + x] = value
        put_own(v2_ref, s, x, value)

    more = (main_ref, side_ref, c_ref, c_side, mask)
    v_side = step(0, R_PLANES, lambda s, x: v_in[v_at(s, x)], v_side, *more, store_mid)
    v_side = step(1, range(4), lambda s, x: v_mid[v_at(s, x)], v_side, *more, store_wide)
    for half in range(HALVES):
        wide_side[half] = v_side[half]
    slot = lane // 8 % 8
    for face, start, shift in ((low_ref, 0, -16), (high_ref, 4 - WIDE, 16)):
        for s in range(SPECIES):
            for n in range(WIDE):
                face[s * WIDE + n] = wide_ref[4 * s + start + n]
        kept = (slot >= start + WIDE) & (slot < start + 2 * WIDE)
        face[SPECIES * WIDE] = jnp.where(kept, v_side[0], roll(v_side[1], shift, 1))


def last_steps(main_ref, side_ref, c_ref, c_side, wide_ref, wide_side, before_ref, after_ref, q_ref, v1_ref, v2_ref, sums_in, v3_ref, v4_ref, sums_ref, v_in, v_mid):
    mask = masks()
    for s in range(SPECIES):
        for face, start, factor in ((before_ref, -WIDE, mask[2]), (after_ref, 4, mask[3])):
            for n in range(WIDE):
                v_in[v_at(s, start + n)] = face[s * WIDE + n] * factor
    slot = iota((ROWS, 128), 1) // 8 % 8
    before, after = before_ref[SPECIES * WIDE] * mask[2], after_ref[SPECIES * WIDE] * mask[3]
    v_side = []
    for half in range(HALVES):
        value = jnp.where(slot < WIDE, roll(before, -32 - 16 * half, 1), wide_side[half])
        v_side.append(jnp.where(slot >= WIDE + 4, roll(after, 32 + 16 * half, 1), value))

    def first(s, x):
        return wide_ref[4 * s + x] if 0 <= x < 4 else v_in[v_at(s, x)]

    def store_mid(s, x, value):
        v_mid[v_at(s, x)] = value
        if 0 <= x < 4:
            put_own(v3_ref, s, x, value)

    def store_last(s, x, value):
        put_own(v4_ref, s, x, value)

    more = (main_ref, side_ref, c_ref, c_side, mask)
    v_side = step(2, R_PLANES, first, v_side, *more, store_mid)
    step(3, range(4), lambda s, x: v_mid[v_at(s, x)], v_side, *more, store_last, sides=False)

    def load(i):
        return [q_ref[a, i] for a in range(EARLIER)] + [v1_ref[i], v2_ref[i], v3_ref[i], v4_ref[i]]

    row = sums_in[...] + products(new_pairs(2) + new_pairs(3), load, q_ref.shape[1])
    sums_ref[...] = jnp.broadcast_to(jnp.sum(row, 0, keepdims=True), sums_ref.shape)


def middle_products(q_ref, v1_ref, v2_ref, before_ref, out_ref):
    def load(i):
        return [q_ref[a, i] for a in range(EARLIER)] + [v1_ref[i], v2_ref[i]]

    out_ref[...] = before_ref[...] + products(new_pairs(0) + new_pairs(1), load, q_ref.shape[1])


def products(pairs, load, count):
    def body(i, sums):
        values = load(i)
        return tuple(total + values[a] * values[b] for total, (a, b) in zip(sums, pairs))

    zero = jnp.zeros((8, 128), jnp.float32)
    sums = lax.fori_loop(0, count, body, (zero,) * len(pairs))
    lane = lax.broadcasted_iota(jnp.int32, (8, 128), 1)
    row = zero
    for total, pair in zip(sums, pairs):
        row = jnp.where(lane == SLOT[pair], jnp.sum(total, 1, keepdims=True), row)
    return row


def earlier_products(q_ref, out_ref):
    pairs = [(a, b) for b in range(EARLIER) for a in range(b + 1)]
    out_ref[...] = products(pairs, lambda i: [q_ref[a, i] for a in range(EARLIER)], q_ref.shape[1])


def new_pairs(number):
    return [(a, EARLIER + number) for a in range(EARLIER + number + 1)]


def finish_kernel(entries, sums_ref, q_ref, *refs):
    v_refs, (new_ref, coeff_ref, triangle_ref) = refs[:STEPS], refs[STEPS:]
    total = sums_ref[0]
    for i in range(1, sums_ref.shape[0]):
        total = total + sums_ref[i]
    total = jnp.broadcast_to(jnp.sum(total, 0, keepdims=True), total.shape) * (1.0 / entries)

    def entry(a, b):
        k = SLOT[(min(a, b), max(a, b))]
        return jnp.broadcast_to(total[:, k : k + 1], total.shape)

    coeff = [[entry(i, EARLIER + j) for j in range(STEPS)] for i in range(EARLIER)]
    overlap = {(a, b): entry(a, b) for b in range(EARLIER) for a in range(b + 1)}
    gram = {}
    for k in range(STEPS):
        mixed = []
        for i in range(EARLIER):
            term = -2.0 * coeff[i][k]
            for m in range(EARLIER):
                term = term + overlap[(min(i, m), max(i, m))] * coeff[m][k]
            mixed.append(term)
        for j in range(k, STEPS):
            value = entry(EARLIER + k, EARLIER + j)
            for i in range(EARLIER):
                value = value + coeff[i][j] * mixed[i]
            gram[(j, k)] = value
    factor, inverse = {}, []
    for k in range(STEPS):
        pivot = gram[(k, k)]
        for m in range(k):
            pivot = pivot - factor[(k, m)] * factor[(k, m)]
        factor[(k, k)] = jnp.sqrt(pivot)
        inverse.append(1.0 / factor[(k, k)])
        for j in range(k + 1, STEPS):
            value = gram[(j, k)]
            for m in range(k):
                value = value - factor[(j, m)] * factor[(k, m)]
            factor[(j, k)] = value * inverse[k]
    row = lax.broadcasted_iota(jnp.int32, total.shape, 0)
    lane = lax.broadcasted_iota(jnp.int32, total.shape, 1)
    table = jnp.zeros_like(total)
    for i in range(EARLIER):
        for j in range(STEPS):
            table = jnp.where((row == j) & (lane == i), coeff[i][j], table)
    coeff_ref[...] = table[:STEPS, :EARLIER]
    table = jnp.zeros_like(total)
    for (j, k), value in factor.items():
        table = jnp.where((row == k) & (lane == j), value, table)
    triangle_ref[...] = table[:STEPS, :STEPS]

    def body(n, carry):
        earlier = [q_ref[i, n] for i in range(EARLIER)]
        done = []
        for j in range(STEPS):
            value = v_refs[j][n]
            for i in range(EARLIER):
                value = value - coeff[i][j] * earlier[i]
            for k in range(j):
                value = value - factor[(j, k)] * done[k]
            done.append(value * inverse[j])
            new_ref[j, n] = done[j]
        return carry

    lax.fori_loop(0, q_ref.shape[1], body, 0)


def call(body, outs, cost, *args, **more):
    return pl.pallas_call(
        body,
        out_shape=[jax.ShapeDtypeStruct(shape, jnp.float32) for shape in outs],
        cost_estimate=pl.CostEstimate(flops=cost, bytes_accessed=cost, transcendentals=0),
        compiler_params=pltpu.CompilerParams(vmem_limit_bytes=24 << 20),
        **more,
    )(*args)


def exchange(axis, low, high):
    count = lax.axis_size(axis)
    up = [(i, (i + 1) % count) for i in range(count)]
    down = [(target, source) for source, target in up]
    return lax.ppermute(high, axis, up), lax.ppermute(low, axis, down)


def on_device(earlier_basis, diffusivity, reaction):
    span_x, span_y, span_z = diffusivity.shape[1:]
    tiles = SPECIES * span_x * span_y // 8
    devices = 1
    for axis in AXES:
        devices *= lax.axis_size(axis)
    entries = tiles * 8 * span_z * devices
    in_hbm = pl.BlockSpec(memory_space=pltpu.HBM)
    given = (earlier_basis, diffusivity, reaction)
    face = (2 * SPECIES * WIDE + SPECIES * SPECIES, span_y, span_z)
    field = diffusivity.shape
    low, high, *kept = call(
        x_faces,
        [face, face, field, field],
        1 << 20,
        *[pltpu.with_memory_space_constraint(a, pltpu.HBM) for a in given],
        in_specs=[in_hbm] * 3,
        scratch_shapes=[pltpu.SemaphoreType.DMA((6 * SPECIES + 2,))],
    )
    x_halos = exchange("gx", low, high)
    kept.append(reaction)
    face = (PLANES // 2, 8, span_z)
    y_halos = exchange("gy", *call(y_faces, [face, face], 1 << 20, *kept, *x_halos))
    face = (BLOCKS, ROWS, span_z)
    whole = (PLANES, ROWS, span_z)
    main, low, high = call(z_faces, [whole, face, face], 1 << 20, *kept, *x_halos, *y_halos)
    z_halos = exchange("gz", low, high)
    basis = earlier_basis.reshape(EARLIER, tiles, 8, span_z)
    (sums,) = call(earlier_products, [(8, span_z)], 4 << 20, basis)
    own = (tiles, 8, span_z)
    scratch = [pltpu.VMEM((D_BASE, ROWS, span_z), jnp.float32)] * 2
    several = [
        (count, ROWS, span_z)
        for count in (SPECIES * span_x, HALVES, SPECIES * WIDE + 1, SPECIES * WIDE + 1, SIDES, CONDUCTS, 4 * HALVES)
    ]
    v1, v2, wide, wide_side, low, high, side, conducts, side_conducts = call(
        first_steps,
        [own, own] + several,
        1 << 20,
        main,
        *z_halos,
        scratch_shapes=scratch,
    )
    halos = exchange("gx", low, high)
    (sums,) = call(middle_products, [(8, span_z)], 4 << 20, basis, v1, v2, sums)
    v3, v4, rows = call(
        last_steps,
        [own, own, (devices, span_z)],
        1 << 20,
        main,
        side,
        conducts,
        side_conducts,
        wide,
        wide_side,
        *halos,
        basis,
        v1,
        v2,
        sums,
        scratch_shapes=scratch,
    )
    rows = lax.all_to_all(rows.reshape(devices, 1, span_z), AXES, 0, 0)
    new, coeff, triangle = call(
        functools.partial(finish_kernel, entries),
        [(STEPS, tiles, 8, span_z), (STEPS, EARLIER), (STEPS, STEPS)],
        1 << 20,
        rows.reshape(devices // 8, 8, span_z),
        basis,
        v1,
        v2,
        v3,
        v4,
    )
    return new.reshape((STEPS, SPECIES, span_x, span_y, span_z)), coeff.T, triangle


def solution(mesh):
    in_specs = (
        P(None, None, "gx", "gy", "gz"),
        P(None, "gx", "gy", "gz"),
        P(None, None, "gx", "gy", "gz"),
    )
    out_specs = (P(None, None, "gx", "gy", "gz"), P(), P())
    return jax.shard_map(
        on_device, mesh=mesh, in_specs=in_specs, out_specs=out_specs, check_vma=False
    )
```

```python
import functools

import jax
import jax.numpy as jnp
from jax import lax
from jax.experimental import pallas as pl
from jax.experimental.pallas import tpu as pltpu
from jax.sharding import PartitionSpec as P

SPECIES = 4
STEPS = 4
EARLIER = 8
SHIFTS = (6.0, 9.0, 14.0, 17.0)
DAMPING = 0.2
AXES = ("gx", "gy", "gz")

VECTORS = EARLIER + STEPS
SLOT = {}
for _b in range(VECTORS):
    for _a in range(_b + 1):
        SLOT[(_a, _b)] = len(SLOT)

WIDE = 2
DEEP = 4
ROWS = 24
V_PLANES = tuple(range(-WIDE, 4 + WIDE))
R_PLANES = tuple(range(-1, 5))
V_BASE = 0
D_BASE = SPECIES * len(V_PLANES)
R_BASE = 2 * D_BASE
PLANES = R_BASE + SPECIES * SPECIES * len(R_PLANES)
HALVES = SPECIES // 2
SIDES = 2 * HALVES + HALVES * SPECIES
BLOCKS = SIDES // 2


def v_at(s, x):
    return V_BASE + s * len(V_PLANES) + x + WIDE


def d_at(s, x):
    return D_BASE + s * len(V_PLANES) + x + WIDE


def r_at(s, t, x):
    return R_BASE + (s * SPECIES + t) * len(R_PLANES) + x + 1


def iota(shape, dim):
    return lax.broadcasted_iota(jnp.int32, shape, dim)


def roll(value, shift, axis):
    shift %= value.shape[axis]
    return pltpu.roll(value, shift, axis) if shift else value


def x_faces(q_ref, d_ref, r_ref, low_ref, high_ref, v_out, d_out, sems):
    copies = []
    for face, planes, plane in ((low_ref, pl.ds(0, WIDE), 0), (high_ref, pl.ds(4 - WIDE, WIDE), 3)):
        for n, source in enumerate((q_ref.at[EARLIER - 1, :, planes], d_ref.at[:, planes])):
            target = face.at[pl.ds(n * SPECIES * WIDE, SPECIES * WIDE)]
            copies.append((source, target.reshape((SPECIES, WIDE) + face.shape[1:])))
        target = face.at[pl.ds(2 * SPECIES * WIDE, SPECIES * SPECIES)]
        copies.append((r_ref.at[:, :, plane], target.reshape((SPECIES, SPECIES) + face.shape[1:])))
    copies += [(q_ref.at[EARLIER - 1], v_out), (d_ref, d_out)]
    started = [pltpu.make_async_copy(a, b, sems.at[n]) for n, (a, b) in enumerate(copies)]
    for copy in started:
        copy.start()
    for copy in started:
        copy.wait()


def own_planes(v_ref, d_ref, r_ref, before_ref, after_ref):
    def pick(own, slot, width, x):
        if x < 0:
            return lambda rows: before_ref[slot + x + width, rows]
        if x > 3:
            return lambda rows: after_ref[slot + x - 4, rows]
        return lambda rows: own(x, rows)

    planes = []
    for s in range(SPECIES):
        for x in V_PLANES:
            planes.append(pick(lambda x, rows, s=s: v_ref[s, x, rows], s * WIDE, WIDE, x))
    for s in range(SPECIES):
        for x in V_PLANES:
            planes.append(pick(lambda x, rows, s=s: d_ref[s, x, rows], (SPECIES + s) * WIDE, WIDE, x))
    for s in range(SPECIES):
        for t in range(SPECIES):
            slot = 2 * SPECIES * WIDE + s * SPECIES + t
            for x in R_PLANES:
                planes.append(pick(lambda x, rows, s=s, t=t: r_ref[s, t, x, rows], slot, 1, x))
    return planes


def y_places():
    places, used = {}, [0, 0]

    def put(message, planes, rows):
        per = 8 // rows
        for n, plane in enumerate(planes):
            places[plane] = (message, used[message] + n // per, n % per, rows)
        used[message] += len(planes) // per

    near, far, own = [], [], []
    for base in (v_at, d_at):
        for s in range(SPECIES):
            for x in V_PLANES:
                (own if 0 <= x < 4 else near if -1 <= x < 5 else far).append(base(s, x))
    for s in range(SPECIES):
        for t in range(SPECIES):
            for x in R_PLANES:
                (own if 0 <= x < 4 else far).append(r_at(s, t, x))
    put(0, own, DEEP)
    put(1, near, DEEP)
    put(1, far, 2)
    return places, used


Y_PLACES, Y_TILES = y_places()


def y_faces(message, planes, low_ref, high_ref):
    row = iota((8, 128), 0)
    low, high = [None] * Y_TILES[message], [None] * Y_TILES[message]
    for plane, (number, tile, place, rows) in Y_PLACES.items():
        if number != message:
            continue
        first = roll(planes[plane](pl.ds(0, 8)), rows * place, 0)
        final = roll(planes[plane](pl.ds(8, 8)), rows * place + rows, 0)
        here = row // rows == place
        low[tile] = first if low[tile] is None else jnp.where(here, first, low[tile])
        high[tile] = final if high[tile] is None else jnp.where(here, final, high[tile])
    for tile in range(Y_TILES[message]):
        low_ref[tile] = low[tile]
        high_ref[tile] = high[tile]


def own_y_faces(v_ref, d_ref, r_ref, low_ref, high_ref):
    y_faces(0, own_planes(v_ref, d_ref, r_ref, None, None), low_ref, high_ref)


def more_y_faces(before_ref, after_ref, low_ref, high_ref):
    y_faces(1, own_planes(None, None, None, before_ref, after_ref), low_ref, high_ref)


def side_planes(side):
    found = []
    for half in range(2):
        for x in V_PLANES:
            if side < 2 * HALVES:
                s = side % HALVES * 2 + half
                found.append(v_at(s, x) if side < HALVES else d_at(s, x))
            else:
                pair, t = divmod(side - 2 * HALVES, SPECIES)
                found.append(r_at(2 * pair + half, t, x) if x in R_PLANES else None)
    return found


def z_faces(value_of, out_ref, low_ref, high_ref):
    shape = low_ref.shape[1:]
    group = iota(shape, 1) // DEEP
    for block in range(BLOCKS):
        low = high = jnp.zeros(shape, jnp.float32)
        for part in range(2):
            for slot, plane in enumerate(side_planes(2 * block + part)):
                if plane is None:
                    continue
                value = value_of(plane)
                out_ref[plane] = value
                k = 2 * slot + part
                low = jnp.where(group == k, roll(value, DEEP * k, 1), low)
                high = jnp.where(group == k, roll(value, DEEP * k + DEEP, 1), high)
        low_ref[block] = low
        high_ref[block] = high


def own_z_faces(v_ref, d_ref, r_ref, before_ref, after_ref, rows_ref, low_ref, high_ref):
    planes = own_planes(v_ref, d_ref, r_ref, before_ref, after_ref)
    z_faces(lambda plane: planes[plane](pl.ds(0, 16)), rows_ref, low_ref, high_ref)


def more_z_faces(own_before, own_after, more_before, more_after, edge_ref, low_ref, high_ref):
    top = iota((8, 128), 0) < DEEP
    befores, afters = (own_before, more_before), (own_after, more_after)

    def value_of(plane):
        message, tile, place, rows = Y_PLACES[plane]
        after = roll(afters[message][tile], -rows * place, 0)
        before = roll(befores[message][tile], 8 - rows - rows * place, 0)
        return jnp.where(top, after, before)

    z_faces(value_of, edge_ref, low_ref, high_ref)


class Planes:
    def __init__(self, rows_ref, edge_ref):
        self.refs = (rows_ref, edge_ref)

    def __getitem__(self, plane):
        return jnp.concatenate([ref[plane] for ref in self.refs], 0)


def masks():
    first = {axis: lax.axis_index(axis) == 0 for axis in AXES}
    final = {axis: lax.axis_index(axis) == lax.axis_size(axis) - 1 for axis in AXES}

    def keep(flag):
        return jnp.where(flag, 0.0, 1.0).astype(jnp.float32)

    row, lane = iota((ROWS, 128), 0), iota((ROWS, 128), 1)
    main = jnp.where(row < 16, 1.0, jnp.where(row < 16 + DEEP, keep(final["gy"]), keep(first["gy"])))
    slot = lane // 8 % 8
    side = main * jnp.where(lane % 8 < DEEP, keep(first["gz"]), keep(final["gz"]))
    before, after = keep(first["gx"]), keep(final["gx"])
    side = side * jnp.where(slot < WIDE, before, jnp.where(slot < WIDE + 4, 1.0, after))
    return main, side, before, after


def mask_of(x, main, before, after):
    if 0 <= x < 4:
        return main
    return main * (before if x < 0 else after)


def next_y(value):
    return roll(value, -1, 0)


def slot_of(s, x):
    return 64 * (s % 2) + 8 * (x + WIDE)


def column(planes, value_of, source, target):
    lane = iota((ROWS, 128), 1)
    found = []
    for half in range(HALVES):
        value = jnp.zeros((ROWS, 128), jnp.float32)
        for s in (2 * half, 2 * half + 1):
            for x in planes:
                place = slot_of(s, x) + target
                value = jnp.where(lane == place, roll(value_of(s, x), place - source, 1), value)
        found.append(value)
    return found


def next_z(value, side, place):
    lane = iota((ROWS, 128), 1)
    return jnp.where(lane == 127, roll(side, 127 - place - DEEP, 1), roll(value, -1, 1))


def previous_z(value, side, place):
    lane = iota((ROWS, 128), 1)
    return jnp.where(lane == 0, roll(side, -(place + DEEP - 1), 1), roll(value, 1, 1))


def side_next_z(side, edge):
    return jnp.where(iota((ROWS, 128), 1) % 8 == DEEP - 1, edge, roll(side, -1, 1))


def side_previous_z(side, edge):
    return jnp.where(iota((ROWS, 128), 1) % 8 == DEEP, edge, roll(side, 1, 1))


def cx_at(s, x):
    return s * 7 + x + 2


def cy_at(s, x):
    return SPECIES * 7 + s * 6 + x + 1


def cz_at(s, x):
    return SPECIES * 13 + s * 6 + x + 1


def back_at(s, x):
    return SPECIES * 19 + s * 6 + x + 1


CONDUCTS = SPECIES * 25


def conduct(d_of, d_side, c_ref, c_side):
    for s in range(SPECIES):
        for x in V_PLANES:
            d = d_of(s, x)
            if x < V_PLANES[-1]:
                c_ref[cx_at(s, x)] = 0.5 * (d + d_of(s, x + 1))
            if x in R_PLANES:
                c_ref[cy_at(s, x)] = 0.5 * (d + next_y(d))
                c_ref[cz_at(s, x)] = 0.5 * (d + next_z(d, d_side[s // 2], slot_of(s, x)))
                c_ref[back_at(s, x)] = 0.5 * (d + previous_z(d, d_side[s // 2], slot_of(s, x)))
    edges = column(R_PLANES, d_of, 0, DEEP - 1)
    ends = column(R_PLANES, d_of, 127, DEEP)
    for half in range(HALVES):
        d = d_side[half]
        c_side[4 * half] = 0.5 * (d + roll(d, -8, 1))
        c_side[4 * half + 1] = 0.5 * (d + next_y(d))
        c_side[4 * half + 2] = 0.5 * (d + side_next_z(d, edges[half]))
        c_side[4 * half + 3] = 0.5 * (d + side_previous_z(d, ends[half]))


def step(degree, planes, v_of, v_side, main_ref, side_ref, c_ref, c_side, mask, store, sides=True):
    lane = iota((ROWS, 128), 1)
    for x in planes:
        factor = DAMPING * mask_of(x, mask[0], *mask[2:])
        here = [v_of(t, x) for t in range(SPECIES)]
        for s in range(SPECIES):
            half, place, v = s // 2, slot_of(s, x), here[s]
            value = v * (1.0 - SHIFTS[degree])
            value = value + c_ref[cz_at(s, x)] * (v - next_z(v, v_side[half], place))
            value = value + c_ref[back_at(s, x)] * (v - previous_z(v, v_side[half], place))
            for t in range(SPECIES):
                value = value + main_ref[r_at(s, t, x)] * here[t]
            value = value + c_ref[cx_at(s, x)] * (v - v_of(s, x + 1))
            value = value + c_ref[cx_at(s, x - 1)] * (v - v_of(s, x - 1))
            along = c_ref[cy_at(s, x)] * (v - next_y(v))
            value = value + (along - roll(along, 1, 0))
            store(s, x, value * factor)
    if not sides:
        return None
    edges = column(planes, v_of, 0, DEEP - 1)
    ends = column(planes, v_of, 127, DEEP)
    both = []
    for half in range(HALVES):
        other = roll(v_side[half], 64, 1)
        both.append(jnp.where(lane < 64, v_side[half], other))
        both.append(jnp.where(lane < 64, other, v_side[half]))
    result = []
    for half in range(HALVES):
        v = v_side[half]
        value = v * (1.0 - SHIFTS[degree])
        value = value + c_side[4 * half + 2] * (v - side_next_z(v, edges[half]))
        value = value + c_side[4 * half + 3] * (v - side_previous_z(v, ends[half]))
        for t in range(SPECIES):
            value = value + side_ref[2 * HALVES + SPECIES * half + t] * both[t]
        across = c_side[4 * half] * (v - roll(v, -8, 1))
        value = value + (across - roll(across, 8, 1))
        along = c_side[4 * half + 1] * (v - next_y(v))
        value = value + (along - roll(along, 1, 0))
        result.append(value * (DAMPING * mask[1]))
    return result


def put_own(out_ref, s, x, value):
    out_ref[8 * s + 2 * x] = value[:8]
    out_ref[8 * s + 2 * x + 1] = value[8:16]


def first_steps(rows_ref, edge_ref, before_rows, after_rows, before_edge, after_edge, v1_ref, v2_ref, wide_ref, wide_side, low_ref, high_ref, side_ref, c_ref, c_side, v_in, v_mid):
    main_ref = Planes(rows_ref, edge_ref)
    before_ref, after_ref = Planes(before_rows, before_edge), Planes(after_rows, after_edge)
    lane = iota((ROWS, 128), 1)
    early = lane % 8 < DEEP
    for block in range(BLOCKS):
        before, after = before_ref[block], after_ref[block]
        side_ref[2 * block] = jnp.where(early, before, roll(after, DEEP, 1))
        side_ref[2 * block + 1] = jnp.where(early, roll(before, -DEEP, 1), after)
    mask = masks()

    def inside(plane, x):
        return main_ref[plane] * mask_of(x, mask[0], *mask[2:])

    v_side = [side_ref[half] * mask[1] for half in range(HALVES)]
    d_side = [side_ref[HALVES + half] * mask[1] for half in range(HALVES)]
    for s in range(SPECIES):
        for x in V_PLANES:
            v_mid[v_at(s, x)] = inside(d_at(s, x), x)
            v_in[v_at(s, x)] = inside(v_at(s, x), x)
    conduct(lambda s, x: v_mid[v_at(s, x)], d_side, c_ref, c_side)

    def store_mid(s, x, value):
        v_mid[v_at(s, x)] = value
        if 0 <= x < 4:
            put_own(v1_ref, s, x, value)

    def store_wide(s, x, value):
        wide_ref[4 * s + x] = value
        put_own(v2_ref, s, x, value)

    more = (main_ref, side_ref, c_ref, c_side, mask)
    v_side = step(0, R_PLANES, lambda s, x: v_in[v_at(s, x)], v_side, *more, store_mid)
    v_side = step(1, range(4), lambda s, x: v_mid[v_at(s, x)], v_side, *more, store_wide)
    for half in range(HALVES):
        wide_side[half] = v_side[half]
    slot = lane // 8 % 8
    for face, start, shift in ((low_ref, 0, -16), (high_ref, 4 - WIDE, 16)):
        for s in range(SPECIES):
            for n in range(WIDE):
                face[s * WIDE + n] = wide_ref[4 * s + start + n]
        kept = (slot >= start + WIDE) & (slot < start + 2 * WIDE)
        face[SPECIES * WIDE] = jnp.where(kept, v_side[0], roll(v_side[1], shift, 1))


def last_steps(rows_ref, edge_ref, side_ref, c_ref, c_side, wide_ref, wide_side, before_ref, after_ref, q_ref, v1_ref, v2_ref, sums_in, v3_ref, v4_ref, sums_ref, v_in, v_mid):
    main_ref = Planes(rows_ref, edge_ref)
    mask = masks()
    for s in range(SPECIES):
        for face, start, factor in ((before_ref, -WIDE, mask[2]), (after_ref, 4, mask[3])):
            for n in range(WIDE):
                v_in[v_at(s, start + n)] = face[s * WIDE + n] * factor
    slot = iota((ROWS, 128), 1) // 8 % 8
    before, after = before_ref[SPECIES * WIDE] * mask[2], after_ref[SPECIES * WIDE] * mask[3]
    v_side = []
    for half in range(HALVES):
        value = jnp.where(slot < WIDE, roll(before, -32 - 16 * half, 1), wide_side[half])
        v_side.append(jnp.where(slot >= WIDE + 4, roll(after, 32 + 16 * half, 1), value))

    def first(s, x):
        return wide_ref[4 * s + x] if 0 <= x < 4 else v_in[v_at(s, x)]

    def store_mid(s, x, value):
        v_mid[v_at(s, x)] = value
        if 0 <= x < 4:
            put_own(v3_ref, s, x, value)

    def store_last(s, x, value):
        put_own(v4_ref, s, x, value)

    more = (main_ref, side_ref, c_ref, c_side, mask)
    v_side = step(2, R_PLANES, first, v_side, *more, store_mid)
    step(3, range(4), lambda s, x: v_mid[v_at(s, x)], v_side, *more, store_last, sides=False)

    def load(i):
        return [q_ref[a, i] for a in range(EARLIER)] + [v1_ref[i], v2_ref[i], v3_ref[i], v4_ref[i]]

    row = sums_in[...] + products(new_pairs(2) + new_pairs(3), load, q_ref.shape[1])
    sums_ref[...] = jnp.broadcast_to(jnp.sum(row, 0, keepdims=True), sums_ref.shape)


def middle_products(q_ref, v1_ref, v2_ref, before_ref, out_ref):
    def load(i):
        return [q_ref[a, i] for a in range(EARLIER)] + [v1_ref[i], v2_ref[i]]

    out_ref[...] = before_ref[...] + products(new_pairs(0) + new_pairs(1), load, q_ref.shape[1])


def products(pairs, load, count):
    def body(i, sums):
        values = load(i)
        return tuple(total + values[a] * values[b] for total, (a, b) in zip(sums, pairs))

    zero = jnp.zeros((8, 128), jnp.float32)
    sums = lax.fori_loop(0, count, body, (zero,) * len(pairs))
    lane = lax.broadcasted_iota(jnp.int32, (8, 128), 1)
    row = zero
    for total, pair in zip(sums, pairs):
        row = jnp.where(lane == SLOT[pair], jnp.sum(total, 1, keepdims=True), row)
    return row


def earlier_products(q_ref, out_ref):
    pairs = [(a, b) for b in range(EARLIER) for a in range(b + 1)]
    out_ref[...] = products(pairs, lambda i: [q_ref[a, i] for a in range(EARLIER)], q_ref.shape[1])


def new_pairs(number):
    return [(a, EARLIER + number) for a in range(EARLIER + number + 1)]


def finish_kernel(entries, sums_ref, q_ref, *refs):
    v_refs, (new_ref, coeff_ref, triangle_ref) = refs[:STEPS], refs[STEPS:]
    total = sums_ref[0]
    for i in range(1, sums_ref.shape[0]):
        total = total + sums_ref[i]
    total = jnp.broadcast_to(jnp.sum(total, 0, keepdims=True), total.shape) * (1.0 / entries)

    def entry(a, b):
        k = SLOT[(min(a, b), max(a, b))]
        return jnp.broadcast_to(total[:, k : k + 1], total.shape)

    coeff = [[entry(i, EARLIER + j) for j in range(STEPS)] for i in range(EARLIER)]
    overlap = {(a, b): entry(a, b) for b in range(EARLIER) for a in range(b + 1)}
    gram = {}
    for k in range(STEPS):
        mixed = []
        for i in range(EARLIER):
            term = -2.0 * coeff[i][k]
            for m in range(EARLIER):
                term = term + overlap[(min(i, m), max(i, m))] * coeff[m][k]
            mixed.append(term)
        for j in range(k, STEPS):
            value = entry(EARLIER + k, EARLIER + j)
            for i in range(EARLIER):
                value = value + coeff[i][j] * mixed[i]
            gram[(j, k)] = value
    factor, inverse = {}, []
    for k in range(STEPS):
        pivot = gram[(k, k)]
        for m in range(k):
            pivot = pivot - factor[(k, m)] * factor[(k, m)]
        factor[(k, k)] = jnp.sqrt(pivot)
        inverse.append(1.0 / factor[(k, k)])
        for j in range(k + 1, STEPS):
            value = gram[(j, k)]
            for m in range(k):
                value = value - factor[(j, m)] * factor[(k, m)]
            factor[(j, k)] = value * inverse[k]
    row = lax.broadcasted_iota(jnp.int32, total.shape, 0)
    lane = lax.broadcasted_iota(jnp.int32, total.shape, 1)
    table = jnp.zeros_like(total)
    for i in range(EARLIER):
        for j in range(STEPS):
            table = jnp.where((row == j) & (lane == i), coeff[i][j], table)
    coeff_ref[...] = table[:STEPS, :EARLIER]
    table = jnp.zeros_like(total)
    for (j, k), value in factor.items():
        table = jnp.where((row == k) & (lane == j), value, table)
    triangle_ref[...] = table[:STEPS, :STEPS]

    def body(n, carry):
        earlier = [q_ref[i, n] for i in range(EARLIER)]
        done = []
        for j in range(STEPS):
            value = v_refs[j][n]
            for i in range(EARLIER):
                value = value - coeff[i][j] * earlier[i]
            for k in range(j):
                value = value - factor[(j, k)] * done[k]
            done.append(value * inverse[j])
            new_ref[j, n] = done[j]
        return carry

    lax.fori_loop(0, q_ref.shape[1], body, 0)


def call(body, outs, cost, *args, **more):
    return pl.pallas_call(
        body,
        out_shape=[jax.ShapeDtypeStruct(shape, jnp.float32) for shape in outs],
        cost_estimate=pl.CostEstimate(flops=cost, bytes_accessed=cost, transcendentals=0),
        compiler_params=pltpu.CompilerParams(vmem_limit_bytes=24 << 20),
        **more,
    )(*args)


def exchange(axis, low, high):
    count = lax.axis_size(axis)
    up = [(i, (i + 1) % count) for i in range(count)]
    down = [(target, source) for source, target in up]
    return lax.ppermute(high, axis, up), lax.ppermute(low, axis, down)


def on_device(earlier_basis, diffusivity, reaction):
    span_x, span_y, span_z = diffusivity.shape[1:]
    tiles = SPECIES * span_x * span_y // 8
    devices = 1
    for axis in AXES:
        devices *= lax.axis_size(axis)
    entries = tiles * 8 * span_z * devices
    in_hbm = pl.BlockSpec(memory_space=pltpu.HBM)
    given = (earlier_basis, diffusivity, reaction)
    face = (2 * SPECIES * WIDE + SPECIES * SPECIES, span_y, span_z)
    field = diffusivity.shape
    low, high, *kept = call(
        x_faces,
        [face, face, field, field],
        1 << 20,
        *[pltpu.with_memory_space_constraint(a, pltpu.HBM) for a in given],
        in_specs=[in_hbm] * 3,
        scratch_shapes=[pltpu.SemaphoreType.DMA((8,))],
    )
    x_halos = exchange("gx", low, high)
    kept.append(reaction)
    face = (Y_TILES[0], 8, span_z)
    y_own = exchange("gy", *call(own_y_faces, [face, face], 1 << 20, *kept))
    face = (Y_TILES[1], 8, span_z)
    y_more = exchange("gy", *call(more_y_faces, [face, face], 1 << 20, *x_halos))
    face = (BLOCKS, 16, span_z)
    rows, low, high = call(own_z_faces, [(PLANES, 16, span_z), face, face], 1 << 20, *kept, *x_halos)
    z_own = exchange("gz", low, high)
    face = (BLOCKS, 8, span_z)
    edge, low, high = call(more_z_faces, [(PLANES, 8, span_z), face, face], 1 << 20, *y_own, *y_more)
    z_more = exchange("gz", low, high)
    main = (rows, edge)
    basis = earlier_basis.reshape(EARLIER, tiles, 8, span_z)
    (sums,) = call(earlier_products, [(8, span_z)], 4 << 20, basis)
    own = (tiles, 8, span_z)
    scratch = [pltpu.VMEM((D_BASE, ROWS, span_z), jnp.float32)] * 2
    several = [
        (count, ROWS, span_z)
        for count in (SPECIES * span_x, HALVES, SPECIES * WIDE + 1, SPECIES * WIDE + 1, SIDES, CONDUCTS, 4 * HALVES)
    ]
    v1, v2, wide, wide_side, low, high, side, conducts, side_conducts = call(
        first_steps,
        [own, own] + several,
        1 << 20,
        *main,
        *z_own,
        *z_more,
        scratch_shapes=scratch,
    )
    halos = exchange("gx", low, high)
    (sums,) = call(middle_products, [(8, span_z)], 4 << 20, basis, v1, v2, sums)
    v3, v4, rows = call(
        last_steps,
        [own, own, (devices, span_z)],
        1 << 20,
        *main,
        side,
        conducts,
        side_conducts,
        wide,
        wide_side,
        *halos,
        basis,
        v1,
        v2,
        sums,
        scratch_shapes=scratch,
    )
    rows = lax.all_to_all(rows.reshape(devices, 1, span_z), AXES, 0, 0)
    new, coeff, triangle = call(
        functools.partial(finish_kernel, entries),
        [(STEPS, tiles, 8, span_z), (STEPS, EARLIER), (STEPS, STEPS)],
        1 << 20,
        rows.reshape(devices // 8, 8, span_z),
        basis,
        v1,
        v2,
        v3,
        v4,
    )
    return new.reshape((STEPS, SPECIES, span_x, span_y, span_z)), coeff.T, triangle


def solution(mesh):
    in_specs = (
        P(None, None, "gx", "gy", "gz"),
        P(None, "gx", "gy", "gz"),
        P(None, None, "gx", "gy", "gz"),
    )
    out_specs = (P(None, None, "gx", "gy", "gz"), P(), P())
    return jax.shard_map(
        on_device, mesh=mesh, in_specs=in_specs, out_specs=out_specs, check_vma=False
    )
```

```python
import functools

import jax
import jax.numpy as jnp
from jax import lax
from jax.experimental import pallas as pl
from jax.experimental.pallas import tpu as pltpu
from jax.sharding import PartitionSpec as P

SPECIES = 4
STEPS = 4
EARLIER = 8
SHIFTS = (6.0, 9.0, 14.0, 17.0)
DAMPING = 0.2
AXES = ("gx", "gy", "gz")

VECTORS = EARLIER + STEPS
SLOT = {}
for _b in range(VECTORS):
    for _a in range(_b + 1):
        SLOT[(_a, _b)] = len(SLOT)

WIDE = 2
DEEP = 4
ROWS = 24
V_PLANES = tuple(range(-WIDE, 4 + WIDE))
R_PLANES = tuple(range(-1, 5))
V_BASE = 0
D_BASE = SPECIES * len(V_PLANES)
R_BASE = 2 * D_BASE
PLANES = R_BASE + SPECIES * SPECIES * len(R_PLANES)
HALVES = SPECIES // 2
SIDES = 2 * HALVES + HALVES * SPECIES
BLOCKS = SIDES // 2


def v_at(s, x):
    return V_BASE + s * len(V_PLANES) + x + WIDE


def d_at(s, x):
    return D_BASE + s * len(V_PLANES) + x + WIDE


def r_at(s, t, x):
    return R_BASE + (s * SPECIES + t) * len(R_PLANES) + x + 1


def iota(shape, dim):
    return lax.broadcasted_iota(jnp.int32, shape, dim)


def roll(value, shift, axis):
    shift %= value.shape[axis]
    return pltpu.roll(value, shift, axis) if shift else value


def x_faces(q_ref, d_ref, r_ref, low_ref, high_ref, v_out, d_out, sems):
    copies = []
    for face, planes, plane in ((low_ref, pl.ds(0, WIDE), 0), (high_ref, pl.ds(4 - WIDE, WIDE), 3)):
        for n, source in enumerate((q_ref.at[EARLIER - 1, :, planes], d_ref.at[:, planes])):
            target = face.at[pl.ds(n * SPECIES * WIDE, SPECIES * WIDE)]
            copies.append((source, target.reshape((SPECIES, WIDE) + face.shape[1:])))
        target = face.at[pl.ds(2 * SPECIES * WIDE, SPECIES * SPECIES)]
        copies.append((r_ref.at[:, :, plane], target.reshape((SPECIES, SPECIES) + face.shape[1:])))
    copies += [(q_ref.at[EARLIER - 1], v_out), (d_ref, d_out)]
    started = [pltpu.make_async_copy(a, b, sems.at[n]) for n, (a, b) in enumerate(copies)]
    for copy in started:
        copy.start()
    for copy in started:
        copy.wait()


def own_planes(v_ref, d_ref, r_ref, before_ref, after_ref):
    def pick(own, slot, width, x):
        if x < 0:
            return lambda rows: before_ref[slot + x + width, rows]
        if x > 3:
            return lambda rows: after_ref[slot + x - 4, rows]
        return lambda rows: own(x, rows)

    planes = []
    for s in range(SPECIES):
        for x in V_PLANES:
            planes.append(pick(lambda x, rows, s=s: v_ref[s, x, rows], s * WIDE, WIDE, x))
    for s in range(SPECIES):
        for x in V_PLANES:
            planes.append(pick(lambda x, rows, s=s: d_ref[s, x, rows], (SPECIES + s) * WIDE, WIDE, x))
    for s in range(SPECIES):
        for t in range(SPECIES):
            slot = 2 * SPECIES * WIDE + s * SPECIES + t
            for x in R_PLANES:
                planes.append(pick(lambda x, rows, s=s, t=t: r_ref[s, t, x, rows], slot, 1, x))
    return planes


def y_places():
    places, used = {}, [0, 0]

    def put(message, planes, rows):
        per = 8 // rows
        for n, plane in enumerate(planes):
            places[plane] = (message, used[message] + n // per, n % per, rows)
        used[message] += len(planes) // per

    near, far, own = [], [], []
    for base in (v_at, d_at):
        for s in range(SPECIES):
            for x in V_PLANES:
                (own if 0 <= x < 4 else near if -1 <= x < 5 else far).append(base(s, x))
    for s in range(SPECIES):
        for t in range(SPECIES):
            for x in R_PLANES:
                (own if 0 <= x < 4 else far).append(r_at(s, t, x))
    put(0, own, DEEP)
    put(1, near, DEEP)
    put(1, far, 2)
    return places, used


Y_PLACES, Y_TILES = y_places()


def y_faces(message, planes, low_ref, high_ref):
    row = iota((8, 128), 0)
    low, high = [None] * Y_TILES[message], [None] * Y_TILES[message]
    for plane, (number, tile, place, rows) in Y_PLACES.items():
        if number != message:
            continue
        first = roll(planes[plane](pl.ds(0, 8)), rows * place, 0)
        final = roll(planes[plane](pl.ds(8, 8)), rows * place + rows, 0)
        here = row // rows == place
        low[tile] = first if low[tile] is None else jnp.where(here, first, low[tile])
        high[tile] = final if high[tile] is None else jnp.where(here, final, high[tile])
    for tile in range(Y_TILES[message]):
        low_ref[tile] = low[tile]
        high_ref[tile] = high[tile]


def own_faces(v_ref, d_ref, r_ref, y_low, y_high, z_low, z_high):
    planes = own_planes(v_ref, d_ref, r_ref, None, None)
    y_faces(0, planes, y_low, y_high)
    for block, found in enumerate(z_groups(True)):
        z_low[block], z_high[block] = pack_z(found, lambda plane: planes[plane](pl.ds(0, 16)), 16)


def more_y_faces(before_ref, after_ref, z_before, z_after, low_ref, high_ref):
    del z_before, z_after
    y_faces(1, own_planes(None, None, None, before_ref, after_ref), low_ref, high_ref)


def side_planes(side):
    found = []
    for half in range(2):
        for x in V_PLANES:
            if side < 2 * HALVES:
                s = side % HALVES * 2 + half
                found.append(v_at(s, x) if side < HALVES else d_at(s, x))
            else:
                pair, t = divmod(side - 2 * HALVES, SPECIES)
                found.append(r_at(2 * pair + half, t, x) if x in R_PLANES else None)
    return found


def z_groups(own):
    blocks = [[] for _ in range(SIDES // 4)]
    for side in range(SIDES):
        for slot, plane in enumerate(side_planes(side)):
            if plane is not None and own == (WIDE <= slot % 8 < WIDE + 4):
                group = (2 * slot + 8 * (side % 4 // 2) + side % 2) % 32
                blocks[side // 4].append((plane, group))
    return blocks


def z_edge_groups():
    blocks = [[] for _ in range(BLOCKS)]
    for side in range(SIDES):
        for slot, plane in enumerate(side_planes(side)):
            if plane is not None:
                blocks[side // 2].append((plane, 2 * slot + side % 2))
    return blocks


def pack_z(planes, value_of, rows):
    group = iota((rows, 128), 1) // DEEP
    low = high = jnp.zeros((rows, 128), jnp.float32)
    for plane, k in planes:
        value = value_of(plane)
        low = jnp.where(group == k, roll(value, DEEP * k, 1), low)
        high = jnp.where(group == k, roll(value, DEEP * k + DEEP, 1), high)
    return low, high


def more_z_faces(x_before, x_after, own_before, own_after, more_before, more_after, edge_ref, low_ref, high_ref):
    planes = own_planes(None, None, None, x_before, x_after)
    top = iota((8, 128), 0) < DEEP
    befores, afters = (own_before, more_before), (own_after, more_after)
    for block, found in enumerate(z_groups(False)):
        low, high = pack_z(found, lambda plane: planes[plane](pl.ds(0, 16)), 16)
        for half in range(2):
            low_ref[2 * block + half] = low[8 * half : 8 * half + 8]
            high_ref[2 * block + half] = high[8 * half : 8 * half + 8]

    def value_of(plane):
        message, tile, place, rows = Y_PLACES[plane]
        after = roll(afters[message][tile], -rows * place, 0)
        before = roll(befores[message][tile], 8 - rows - rows * place, 0)
        edge_ref[plane] = jnp.where(top, after, before)
        return edge_ref[plane]

    for block, found in enumerate(z_edge_groups()):
        low_ref[BLOCKS + block], high_ref[BLOCKS + block] = pack_z(found, value_of, 8)


def unpack_z(side, own_before, own_after, more_before, more_after):
    lane = iota((16, 128), 1)
    block, turned, part = side // 4, side % 4 // 2, side % 2
    own = (lane // 8 % 8 >= WIDE) & (lane // 8 % 8 < WIDE + 4)
    if turned:
        own = ~own

    def rows(own_ref, more_ref):
        more = jnp.concatenate([more_ref[2 * block], more_ref[2 * block + 1]], 0)
        return jnp.where(own, own_ref[block], more)

    def join(before, after, shift):
        early = iota(before.shape, 1) % 8 < DEEP
        return jnp.where(early, roll(before, -shift - DEEP * part, 1), roll(after, DEEP - shift - DEEP * part, 1))

    main = join(rows(own_before, more_before), rows(own_after, more_after), 32 * turned)
    edge = join(more_before[BLOCKS + side // 2], more_after[BLOCKS + side // 2], 0)
    return jnp.concatenate([main, edge], 0)


class Planes:
    def __init__(self, planes, edge_ref):
        self.planes, self.edge_ref = planes, edge_ref

    def __getitem__(self, plane):
        return jnp.concatenate([self.planes[plane](pl.ds(0, 16)), self.edge_ref[plane]], 0)


def masks():
    first = {axis: lax.axis_index(axis) == 0 for axis in AXES}
    final = {axis: lax.axis_index(axis) == lax.axis_size(axis) - 1 for axis in AXES}

    def keep(flag):
        return jnp.where(flag, 0.0, 1.0).astype(jnp.float32)

    row, lane = iota((ROWS, 128), 0), iota((ROWS, 128), 1)
    main = jnp.where(row < 16, 1.0, jnp.where(row < 16 + DEEP, keep(final["gy"]), keep(first["gy"])))
    slot = lane // 8 % 8
    side = main * jnp.where(lane % 8 < DEEP, keep(first["gz"]), keep(final["gz"]))
    before, after = keep(first["gx"]), keep(final["gx"])
    side = side * jnp.where(slot < WIDE, before, jnp.where(slot < WIDE + 4, 1.0, after))
    return main, side, before, after


def mask_of(x, main, before, after):
    if 0 <= x < 4:
        return main
    return main * (before if x < 0 else after)


def next_y(value):
    return roll(value, -1, 0)


def slot_of(s, x):
    return 64 * (s % 2) + 8 * (x + WIDE)


def columns(planes, value_of):
    group = iota((ROWS, 128), 1) // 8
    found = []
    for half in range(HALVES):
        value = jnp.zeros((ROWS, 128), jnp.float32)
        for s in (2 * half, 2 * half + 1):
            for x in planes:
                place = slot_of(s, x)
                value = jnp.where(group == place // 8, roll(value_of(s, x), place + DEEP, 1), value)
        found.append(value)
    return found


def next_z(value, side, place):
    lane = iota((ROWS, 128), 1)
    return jnp.where(lane == 127, roll(side, 127 - place - DEEP, 1), roll(value, -1, 1))


def previous_z(value, side, place):
    lane = iota((ROWS, 128), 1)
    return jnp.where(lane == 0, roll(side, -(place + DEEP - 1), 1), roll(value, 1, 1))


def side_next_z(side, edge):
    return roll(jnp.where(iota((ROWS, 128), 1) % 8 == DEEP, edge, side), -1, 1)


def side_previous_z(side, edge):
    return roll(jnp.where(iota((ROWS, 128), 1) % 8 == DEEP - 1, edge, side), 1, 1)


def cx_at(s, x):
    return s * 7 + x + 2


def cy_at(s, x):
    return SPECIES * 7 + s * 6 + x + 1


def cz_at(s, x):
    return SPECIES * 13 + s * 6 + x + 1


def back_at(s, x):
    return SPECIES * 19 + s * 6 + x + 1


CONDUCTS = SPECIES * 25


def conduct(d_of, d_side, c_ref, c_side):
    for s in range(SPECIES):
        for x in V_PLANES:
            d = d_of(s, x)
            if x < V_PLANES[-1]:
                c_ref[cx_at(s, x)] = 0.5 * (d + d_of(s, x + 1))
            if x in R_PLANES:
                c_ref[cy_at(s, x)] = 0.5 * (d + next_y(d))
                c_ref[cz_at(s, x)] = 0.5 * (d + next_z(d, d_side[s // 2], slot_of(s, x)))
                c_ref[back_at(s, x)] = 0.5 * (d + previous_z(d, d_side[s // 2], slot_of(s, x)))
    edges = columns(R_PLANES, d_of)
    for half in range(HALVES):
        d = d_side[half]
        c_side[4 * half] = 0.5 * (d + roll(d, -8, 1))
        c_side[4 * half + 1] = 0.5 * (d + next_y(d))
        c_side[4 * half + 2] = 0.5 * (d + side_next_z(d, edges[half]))
        c_side[4 * half + 3] = 0.5 * (d + side_previous_z(d, edges[half]))


def step(degree, planes, v_of, v_side, main_ref, side_ref, c_ref, c_side, mask, store, sides=True):
    lane = iota((ROWS, 128), 1)
    for x in planes:
        factor = DAMPING * mask_of(x, mask[0], *mask[2:])
        here = [v_of(t, x) for t in range(SPECIES)]
        for s in range(SPECIES):
            half, place, v = s // 2, slot_of(s, x), here[s]
            value = v * (1.0 - SHIFTS[degree])
            value = value + c_ref[cz_at(s, x)] * (v - next_z(v, v_side[half], place))
            value = value + c_ref[back_at(s, x)] * (v - previous_z(v, v_side[half], place))
            for t in range(SPECIES):
                value = value + main_ref[r_at(s, t, x)] * here[t]
            value = value + c_ref[cx_at(s, x)] * (v - v_of(s, x + 1))
            value = value + c_ref[cx_at(s, x - 1)] * (v - v_of(s, x - 1))
            along = c_ref[cy_at(s, x)] * (v - next_y(v))
            value = value + (along - roll(along, 1, 0))
            store(s, x, value * factor)
    if not sides:
        return None
    edges = columns(planes, v_of)
    both = []
    for half in range(HALVES):
        other = roll(v_side[half], 64, 1)
        both.append(jnp.where(lane < 64, v_side[half], other))
        both.append(jnp.where(lane < 64, other, v_side[half]))
    result = []
    for half in range(HALVES):
        v = v_side[half]
        value = v * (1.0 - SHIFTS[degree])
        value = value + c_side[4 * half + 2] * (v - side_next_z(v, edges[half]))
        value = value + c_side[4 * half + 3] * (v - side_previous_z(v, edges[half]))
        for t in range(SPECIES):
            value = value + side_ref[2 * HALVES + SPECIES * half + t] * both[t]
        across = c_side[4 * half] * (v - roll(v, -8, 1))
        value = value + (across - roll(across, 8, 1))
        along = c_side[4 * half + 1] * (v - next_y(v))
        value = value + (along - roll(along, 1, 0))
        result.append(value * (DAMPING * mask[1]))
    return result


def put_own(out_ref, s, x, value):
    out_ref[8 * s + 2 * x] = value[:8]
    out_ref[8 * s + 2 * x + 1] = value[8:16]


def first_steps(v_ref, d_ref, r_ref, x_before, x_after, edge_ref, own_before, own_after, more_before, more_after, v1_ref, v2_ref, wide_ref, wide_side, low_ref, high_ref, side_ref, c_ref, c_side, v_in, v_mid):
    main_ref = Planes(own_planes(v_ref, d_ref, r_ref, x_before, x_after), edge_ref)
    lane = iota((ROWS, 128), 1)
    for side in range(SIDES):
        side_ref[side] = unpack_z(side, own_before, own_after, more_before, more_after)
    mask = masks()

    def inside(plane, x):
        return main_ref[plane] * mask_of(x, mask[0], *mask[2:])

    v_side = [side_ref[half] * mask[1] for half in range(HALVES)]
    d_side = [side_ref[HALVES + half] * mask[1] for half in range(HALVES)]
    for s in range(SPECIES):
        for x in V_PLANES:
            v_mid[v_at(s, x)] = inside(d_at(s, x), x)
            v_in[v_at(s, x)] = inside(v_at(s, x), x)
    conduct(lambda s, x: v_mid[v_at(s, x)], d_side, c_ref, c_side)

    def store_mid(s, x, value):
        v_mid[v_at(s, x)] = value
        if 0 <= x < 4:
            put_own(v1_ref, s, x, value)

    def store_wide(s, x, value):
        wide_ref[4 * s + x] = value
        put_own(v2_ref, s, x, value)

    more = (main_ref, side_ref, c_ref, c_side, mask)
    v_side = step(0, R_PLANES, lambda s, x: v_in[v_at(s, x)], v_side, *more, store_mid)
    v_side = step(1, range(4), lambda s, x: v_mid[v_at(s, x)], v_side, *more, store_wide)
    for half in range(HALVES):
        wide_side[half] = v_side[half]
    slot = lane // 8 % 8
    for face, start, shift in ((low_ref, 0, -16), (high_ref, 4 - WIDE, 16)):
        for s in range(SPECIES):
            for n in range(WIDE):
                face[s * WIDE + n] = wide_ref[4 * s + start + n]
        kept = (slot >= start + WIDE) & (slot < start + 2 * WIDE)
        face[SPECIES * WIDE] = jnp.where(kept, v_side[0], roll(v_side[1], shift, 1))


def last_steps(r_ref, x_before, x_after, edge_ref, side_ref, c_ref, c_side, wide_ref, wide_side, before_ref, after_ref, q_ref, v1_ref, v2_ref, sums_in, v3_ref, v4_ref, sums_ref, v_in, v_mid):
    main_ref = Planes(own_planes(None, None, r_ref, x_before, x_after), edge_ref)
    mask = masks()
    for s in range(SPECIES):
        for face, start, factor in ((before_ref, -WIDE, mask[2]), (after_ref, 4, mask[3])):
            for n in range(WIDE):
                v_in[v_at(s, start + n)] = face[s * WIDE + n] * factor
    slot = iota((ROWS, 128), 1) // 8 % 8
    before, after = before_ref[SPECIES * WIDE] * mask[2], after_ref[SPECIES * WIDE] * mask[3]
    v_side = []
    for half in range(HALVES):
        value = jnp.where(slot < WIDE, roll(before, -32 - 16 * half, 1), wide_side[half])
        v_side.append(jnp.where(slot >= WIDE + 4, roll(after, 32 + 16 * half, 1), value))

    def first(s, x):
        return wide_ref[4 * s + x] if 0 <= x < 4 else v_in[v_at(s, x)]

    def store_mid(s, x, value):
        v_mid[v_at(s, x)] = value
        if 0 <= x < 4:
            put_own(v3_ref, s, x, value)

    def store_last(s, x, value):
        put_own(v4_ref, s, x, value)

    more = (main_ref, side_ref, c_ref, c_side, mask)
    v_side = step(2, R_PLANES, first, v_side, *more, store_mid)
    step(3, range(4), lambda s, x: v_mid[v_at(s, x)], v_side, *more, store_last, sides=False)

    def load(i):
        return [q_ref[a, i] for a in range(EARLIER)] + [v1_ref[i], v2_ref[i], v3_ref[i], v4_ref[i]]

    row = sums_in[...] + products(new_pairs(2) + new_pairs(3), load, q_ref.shape[1])
    sums_ref[...] = jnp.broadcast_to(jnp.sum(row, 0, keepdims=True), sums_ref.shape)


def middle_products(q_ref, v1_ref, v2_ref, before_ref, out_ref):
    def load(i):
        return [q_ref[a, i] for a in range(EARLIER)] + [v1_ref[i], v2_ref[i]]

    out_ref[...] = before_ref[...] + products(new_pairs(0) + new_pairs(1), load, q_ref.shape[1])


def products(pairs, load, count):
    def body(i, sums):
        values = load(i)
        return tuple(total + values[a] * values[b] for total, (a, b) in zip(sums, pairs))

    zero = jnp.zeros((8, 128), jnp.float32)
    sums = lax.fori_loop(0, count, body, (zero,) * len(pairs))
    lane = lax.broadcasted_iota(jnp.int32, (8, 128), 1)
    row = zero
    for total, pair in zip(sums, pairs):
        row = jnp.where(lane == SLOT[pair], jnp.sum(total, 1, keepdims=True), row)
    return row


def earlier_products(q_ref, out_ref):
    pairs = [(a, b) for b in range(EARLIER) for a in range(b + 1)]
    out_ref[...] = products(pairs, lambda i: [q_ref[a, i] for a in range(EARLIER)], q_ref.shape[1])


def new_pairs(number):
    return [(a, EARLIER + number) for a in range(EARLIER + number + 1)]


def finish_kernel(entries, sums_ref, q_ref, *refs):
    v_refs, (new_ref, coeff_ref, triangle_ref) = refs[:STEPS], refs[STEPS:]
    total = sums_ref[0]
    for i in range(1, sums_ref.shape[0]):
        total = total + sums_ref[i]
    total = jnp.broadcast_to(jnp.sum(total, 0, keepdims=True), total.shape) * (1.0 / entries)

    def entry(a, b):
        k = SLOT[(min(a, b), max(a, b))]
        return jnp.broadcast_to(total[:, k : k + 1], total.shape)

    coeff = [[entry(i, EARLIER + j) for j in range(STEPS)] for i in range(EARLIER)]
    overlap = {(a, b): entry(a, b) for b in range(EARLIER) for a in range(b + 1)}
    gram = {}
    for k in range(STEPS):
        mixed = []
        for i in range(EARLIER):
            term = -2.0 * coeff[i][k]
            for m in range(EARLIER):
                term = term + overlap[(min(i, m), max(i, m))] * coeff[m][k]
            mixed.append(term)
        for j in range(k, STEPS):
            value = entry(EARLIER + k, EARLIER + j)
            for i in range(EARLIER):
                value = value + coeff[i][j] * mixed[i]
            gram[(j, k)] = value
    factor, inverse = {}, []
    for k in range(STEPS):
        pivot = gram[(k, k)]
        for m in range(k):
            pivot = pivot - factor[(k, m)] * factor[(k, m)]
        factor[(k, k)] = jnp.sqrt(pivot)
        inverse.append(1.0 / factor[(k, k)])
        for j in range(k + 1, STEPS):
            value = gram[(j, k)]
            for m in range(k):
                value = value - factor[(j, m)] * factor[(k, m)]
            factor[(j, k)] = value * inverse[k]
    row = lax.broadcasted_iota(jnp.int32, total.shape, 0)
    lane = lax.broadcasted_iota(jnp.int32, total.shape, 1)
    table = jnp.zeros_like(total)
    for i in range(EARLIER):
        for j in range(STEPS):
            table = jnp.where((row == j) & (lane == i), coeff[i][j], table)
    coeff_ref[...] = table[:STEPS, :EARLIER]
    table = jnp.zeros_like(total)
    for (j, k), value in factor.items():
        table = jnp.where((row == k) & (lane == j), value, table)
    triangle_ref[...] = table[:STEPS, :STEPS]

    def body(n, carry):
        earlier = [q_ref[i, n] for i in range(EARLIER)]
        done = []
        for j in range(STEPS):
            value = v_refs[j][n]
            for i in range(EARLIER):
                value = value - coeff[i][j] * earlier[i]
            for k in range(j):
                value = value - factor[(j, k)] * done[k]
            done.append(value * inverse[j])
            new_ref[j, n] = done[j]
        return carry

    lax.fori_loop(0, q_ref.shape[1], body, 0)


def call(body, outs, cost, *args, **more):
    return pl.pallas_call(
        body,
        out_shape=[jax.ShapeDtypeStruct(shape, jnp.float32) for shape in outs],
        cost_estimate=pl.CostEstimate(flops=cost, bytes_accessed=cost, transcendentals=0),
        compiler_params=pltpu.CompilerParams(vmem_limit_bytes=24 << 20),
        **more,
    )(*args)


def exchange(axis, low, high):
    count = lax.axis_size(axis)
    up = [(i, (i + 1) % count) for i in range(count)]
    down = [(target, source) for source, target in up]
    return lax.ppermute(high, axis, up), lax.ppermute(low, axis, down)


def on_device(earlier_basis, diffusivity, reaction):
    span_x, span_y, span_z = diffusivity.shape[1:]
    tiles = SPECIES * span_x * span_y // 8
    devices = 1
    for axis in AXES:
        devices *= lax.axis_size(axis)
    entries = tiles * 8 * span_z * devices
    in_hbm = pl.BlockSpec(memory_space=pltpu.HBM)
    given = (earlier_basis, diffusivity, reaction)
    face = (2 * SPECIES * WIDE + SPECIES * SPECIES, span_y, span_z)
    field = diffusivity.shape
    low, high, *kept = call(
        x_faces,
        [face, face, field, field],
        1 << 20,
        *[pltpu.with_memory_space_constraint(a, pltpu.HBM) for a in given],
        in_specs=[in_hbm] * 3,
        scratch_shapes=[pltpu.SemaphoreType.DMA((8,))],
    )
    x_halos = exchange("gx", low, high)
    kept.append(reaction)
    face = (Y_TILES[0], 8, span_z)
    z_face = (SIDES // 4, 16, span_z)
    own = call(own_faces, [face, face, z_face, z_face], 1 << 20, *kept)
    y_own, z_own = exchange("gy", *own[:2]), exchange("gz", *own[2:])
    face = (Y_TILES[1], 8, span_z)
    y_more = exchange("gy", *call(more_y_faces, [face, face], 1 << 20, *x_halos, *z_own))
    face = (2 * BLOCKS, 8, span_z)
    edge, low, high = call(more_z_faces, [(PLANES, 8, span_z), face, face], 1 << 20, *x_halos, *y_own, *y_more)
    z_more = exchange("gz", low, high)
    basis = earlier_basis.reshape(EARLIER, tiles, 8, span_z)
    (sums,) = call(earlier_products, [(8, span_z)], 4 << 20, basis)
    own = (tiles, 8, span_z)
    scratch = [pltpu.VMEM((D_BASE, ROWS, span_z), jnp.float32)] * 2
    several = [
        (count, ROWS, span_z)
        for count in (SPECIES * span_x, HALVES, SPECIES * WIDE + 1, SPECIES * WIDE + 1, SIDES, CONDUCTS, 4 * HALVES)
    ]
    v1, v2, wide, wide_side, low, high, side, conducts, side_conducts = call(
        first_steps,
        [own, own] + several,
        1 << 20,
        *kept,
        *x_halos,
        edge,
        *z_own,
        *z_more,
        scratch_shapes=scratch,
    )
    halos = exchange("gx", low, high)
    (sums,) = call(middle_products, [(8, span_z)], 4 << 20, basis, v1, v2, sums)
    v3, v4, rows = call(
        last_steps,
        [own, own, (devices, span_z)],
        1 << 20,
        reaction,
        *x_halos,
        edge,
        side,
        conducts,
        side_conducts,
        wide,
        wide_side,
        *halos,
        basis,
        v1,
        v2,
        sums,
        scratch_shapes=scratch,
    )
    rows = lax.all_to_all(rows.reshape(devices, 1, span_z), AXES, 0, 0)
    new, coeff, triangle = call(
        functools.partial(finish_kernel, entries),
        [(STEPS, tiles, 8, span_z), (STEPS, EARLIER), (STEPS, STEPS)],
        1 << 20,
        rows.reshape(devices // 8, 8, span_z),
        basis,
        v1,
        v2,
        v3,
        v4,
    )
    return new.reshape((STEPS, SPECIES, span_x, span_y, span_z)), coeff.T, triangle


def solution(mesh):
    in_specs = (
        P(None, None, "gx", "gy", "gz"),
        P(None, "gx", "gy", "gz"),
        P(None, None, "gx", "gy", "gz"),
    )
    out_specs = (P(None, None, "gx", "gy", "gz"), P(), P())
    return jax.shard_map(
        on_device, mesh=mesh, in_specs=in_specs, out_specs=out_specs, check_vma=False
    )
```

```python
import functools

import jax
import jax.numpy as jnp
from jax import lax
from jax.experimental import pallas as pl
from jax.experimental.pallas import tpu as pltpu
from jax.sharding import PartitionSpec as P

SPECIES = 4
STEPS = 4
EARLIER = 8
SHIFTS = (6.0, 9.0, 14.0, 17.0)
DAMPING = 0.2
AXES = ("gx", "gy", "gz")

VECTORS = EARLIER + STEPS
SLOT = {}
for _b in range(VECTORS):
    for _a in range(_b + 1):
        SLOT[(_a, _b)] = len(SLOT)

WIDE = 2
DEEP = 4
ROWS = 24
V_PLANES = tuple(range(-WIDE, 4 + WIDE))
R_PLANES = tuple(range(-1, 5))
V_BASE = 0
D_BASE = SPECIES * len(V_PLANES)
R_BASE = 2 * D_BASE
PLANES = R_BASE + SPECIES * SPECIES * len(R_PLANES)
HALVES = SPECIES // 2
SIDES = 2 * HALVES + HALVES * SPECIES
BLOCKS = SIDES // 2


def v_at(s, x):
    return V_BASE + s * len(V_PLANES) + x + WIDE


def d_at(s, x):
    return D_BASE + s * len(V_PLANES) + x + WIDE


def r_at(s, t, x):
    return R_BASE + (s * SPECIES + t) * len(R_PLANES) + x + 1


def iota(shape, dim):
    return lax.broadcasted_iota(jnp.int32, shape, dim)


def roll(value, shift, axis):
    shift %= value.shape[axis]
    return pltpu.roll(value, shift, axis) if shift else value


def x_faces(q_ref, d_ref, r_ref, low_ref, high_ref, v_out, d_out, sems):
    copies = []
    for face, planes, plane in ((low_ref, pl.ds(0, WIDE), 0), (high_ref, pl.ds(4 - WIDE, WIDE), 3)):
        for n, source in enumerate((q_ref.at[EARLIER - 1, :, planes], d_ref.at[:, planes])):
            target = face.at[pl.ds(n * SPECIES * WIDE, SPECIES * WIDE)]
            copies.append((source, target.reshape((SPECIES, WIDE) + face.shape[1:])))
        target = face.at[pl.ds(2 * SPECIES * WIDE, SPECIES * SPECIES)]
        copies.append((r_ref.at[:, :, plane], target.reshape((SPECIES, SPECIES) + face.shape[1:])))
    copies += [(q_ref.at[EARLIER - 1], v_out), (d_ref, d_out)]
    started = [pltpu.make_async_copy(a, b, sems.at[n]) for n, (a, b) in enumerate(copies)]
    for copy in started:
        copy.start()
    for copy in started:
        copy.wait()


def own_planes(v_ref, d_ref, r_ref, before_ref, after_ref):
    def pick(own, slot, width, x):
        if x < 0:
            return lambda rows: before_ref[slot + x + width, rows]
        if x > 3:
            return lambda rows: after_ref[slot + x - 4, rows]
        return lambda rows: own(x, rows)

    planes = []
    for s in range(SPECIES):
        for x in V_PLANES:
            planes.append(pick(lambda x, rows, s=s: v_ref[s, x, rows], s * WIDE, WIDE, x))
    for s in range(SPECIES):
        for x in V_PLANES:
            planes.append(pick(lambda x, rows, s=s: d_ref[s, x, rows], (SPECIES + s) * WIDE, WIDE, x))
    for s in range(SPECIES):
        for t in range(SPECIES):
            slot = 2 * SPECIES * WIDE + s * SPECIES + t
            for x in R_PLANES:
                planes.append(pick(lambda x, rows, s=s, t=t: r_ref[s, t, x, rows], slot, 1, x))
    return planes


def y_places():
    places, used = {}, [0, 0]

    def put(message, planes, rows):
        per = 8 // rows
        for n, plane in enumerate(planes):
            places[plane] = (message, used[message] + n // per, n % per, rows)
        used[message] += len(planes) // per

    near, far, own = [], [], []
    for base in (v_at, d_at):
        for s in range(SPECIES):
            for x in V_PLANES:
                (own if 0 <= x < 4 else near if -1 <= x < 5 else far).append(base(s, x))
    for s in range(SPECIES):
        for t in range(SPECIES):
            for x in R_PLANES:
                (own if 0 <= x < 4 else far).append(r_at(s, t, x))
    put(0, own, DEEP)
    put(1, near, DEEP)
    put(1, far, 2)
    return places, used


Y_PLACES, Y_TILES = y_places()


def y_faces(message, planes, low_ref, high_ref):
    row = iota((8, 128), 0)
    low, high = [None] * Y_TILES[message], [None] * Y_TILES[message]
    for plane, (number, tile, place, rows) in Y_PLACES.items():
        if number != message:
            continue
        first = roll(planes[plane](pl.ds(0, 8)), rows * place, 0)
        final = roll(planes[plane](pl.ds(8, 8)), rows * place + rows, 0)
        here = row // rows == place
        low[tile] = first if low[tile] is None else jnp.where(here, first, low[tile])
        high[tile] = final if high[tile] is None else jnp.where(here, final, high[tile])
    for tile in range(Y_TILES[message]):
        low_ref[tile] = low[tile]
        high_ref[tile] = high[tile]


def own_faces(v_ref, d_ref, r_ref, y_low, y_high, z_low, z_high):
    planes = own_planes(v_ref, d_ref, r_ref, None, None)
    y_faces(0, planes, y_low, y_high)
    for block, found in enumerate(z_groups(True)):
        z_low[block], z_high[block] = pack_z(found, lambda plane: planes[plane](pl.ds(0, 16)), 16)


def more_y_faces(before_ref, after_ref, low_ref, high_ref):
    y_faces(1, own_planes(None, None, None, before_ref, after_ref), low_ref, high_ref)


def side_planes(side):
    found = []
    for half in range(2):
        for x in V_PLANES:
            if side < 2 * HALVES:
                s = side % HALVES * 2 + half
                found.append(v_at(s, x) if side < HALVES else d_at(s, x))
            else:
                pair, t = divmod(side - 2 * HALVES, SPECIES)
                found.append(r_at(2 * pair + half, t, x) if x in R_PLANES else None)
    return found


def z_groups(own):
    blocks = [[] for _ in range(SIDES // 4)]
    for side in range(SIDES):
        for slot, plane in enumerate(side_planes(side)):
            if plane is not None and own == (WIDE <= slot % 8 < WIDE + 4):
                group = (2 * slot + 8 * (side % 4 // 2) + side % 2) % 32
                blocks[side // 4].append((plane, group))
    return blocks


def z_edge_groups():
    blocks = [[] for _ in range(BLOCKS)]
    for side in range(SIDES):
        for slot, plane in enumerate(side_planes(side)):
            if plane is not None:
                blocks[side // 2].append((plane, 2 * slot + side % 2))
    return blocks


def pack_z(planes, value_of, rows):
    group = iota((rows, 128), 1) // DEEP
    low = high = jnp.zeros((rows, 128), jnp.float32)
    for plane, k in planes:
        value = value_of(plane)
        low = jnp.where(group == k, roll(value, DEEP * k, 1), low)
        high = jnp.where(group == k, roll(value, DEEP * k + DEEP, 1), high)
    return low, high


def more_z_faces(x_before, x_after, own_before, own_after, more_before, more_after, edge_ref, low_ref, high_ref):
    planes = own_planes(None, None, None, x_before, x_after)
    top = iota((8, 128), 0) < DEEP
    befores, afters = (own_before, more_before), (own_after, more_after)
    for block, found in enumerate(z_groups(False)):
        low, high = pack_z(found, lambda plane: planes[plane](pl.ds(0, 16)), 16)
        for half in range(2):
            low_ref[2 * block + half] = low[8 * half : 8 * half + 8]
            high_ref[2 * block + half] = high[8 * half : 8 * half + 8]

    def value_of(plane):
        message, tile, place, rows = Y_PLACES[plane]
        after = roll(afters[message][tile], -rows * place, 0)
        before = roll(befores[message][tile], 8 - rows - rows * place, 0)
        edge_ref[plane] = jnp.where(top, after, before)
        return edge_ref[plane]

    for block, found in enumerate(z_edge_groups()):
        low_ref[BLOCKS + block], high_ref[BLOCKS + block] = pack_z(found, value_of, 8)


def unpack_z(side, own_before, own_after, more_before, more_after):
    lane = iota((16, 128), 1)
    block, turned, part = side // 4, side % 4 // 2, side % 2
    own = (lane // 8 % 8 >= WIDE) & (lane // 8 % 8 < WIDE + 4)
    if turned:
        own = ~own

    def rows(own_ref, more_ref):
        more = jnp.concatenate([more_ref[2 * block], more_ref[2 * block + 1]], 0)
        return jnp.where(own, own_ref[block], more)

    def join(before, after, shift):
        early = iota(before.shape, 1) % 8 < DEEP
        return jnp.where(early, roll(before, -shift - DEEP * part, 1), roll(after, DEEP - shift - DEEP * part, 1))

    main = join(rows(own_before, more_before), rows(own_after, more_after), 32 * turned)
    edge = join(more_before[BLOCKS + side // 2], more_after[BLOCKS + side // 2], 0)
    return jnp.concatenate([main, edge], 0)


class Planes:
    def __init__(self, planes, edge_ref):
        self.planes, self.edge_ref = planes, edge_ref

    def __getitem__(self, plane):
        return jnp.concatenate([self.planes[plane](pl.ds(0, 16)), self.edge_ref[plane]], 0)


def masks():
    first = {axis: lax.axis_index(axis) == 0 for axis in AXES}
    final = {axis: lax.axis_index(axis) == lax.axis_size(axis) - 1 for axis in AXES}

    def keep(flag):
        return jnp.where(flag, 0.0, 1.0).astype(jnp.float32)

    row, lane = iota((ROWS, 128), 0), iota((ROWS, 128), 1)
    main = jnp.where(row < 16, 1.0, jnp.where(row < 16 + DEEP, keep(final["gy"]), keep(first["gy"])))
    slot = lane // 8 % 8
    side = main * jnp.where(lane % 8 < DEEP, keep(first["gz"]), keep(final["gz"]))
    before, after = keep(first["gx"]), keep(final["gx"])
    side = side * jnp.where(slot < WIDE, before, jnp.where(slot < WIDE + 4, 1.0, after))
    return main, side, before, after


def mask_of(x, main, before, after):
    if 0 <= x < 4:
        return main
    return main * (before if x < 0 else after)


def next_y(value):
    return roll(value, -1, 0)


def slot_of(s, x):
    return 64 * (s % 2) + 8 * (x + WIDE)


def columns(planes, value_of):
    group = iota((ROWS, 128), 1) // 8
    found = []
    for half in range(HALVES):
        value = jnp.zeros((ROWS, 128), jnp.float32)
        for s in (2 * half, 2 * half + 1):
            for x in planes:
                place = slot_of(s, x)
                value = jnp.where(group == place // 8, roll(value_of(s, x), place + DEEP, 1), value)
        found.append(value)
    return found


def next_z(value, side, place):
    lane = iota((ROWS, 128), 1)
    return jnp.where(lane == 127, roll(side, 127 - place - DEEP, 1), roll(value, -1, 1))


def previous_z(value, side, place):
    lane = iota((ROWS, 128), 1)
    return jnp.where(lane == 0, roll(side, -(place + DEEP - 1), 1), roll(value, 1, 1))


def side_next_z(side, edge):
    return roll(jnp.where(iota((ROWS, 128), 1) % 8 == DEEP, edge, side), -1, 1)


def side_previous_z(side, edge):
    return roll(jnp.where(iota((ROWS, 128), 1) % 8 == DEEP - 1, edge, side), 1, 1)


def cx_at(s, x):
    return s * 7 + x + 2


def cy_at(s, x):
    return SPECIES * 7 + s * 6 + x + 1


def cz_at(s, x):
    return SPECIES * 13 + s * 6 + x + 1


def back_at(s, x):
    return SPECIES * 19 + s * 6 + x + 1


CONDUCTS = SPECIES * 25


def conduct(d_of, d_side, c_ref, c_side):
    for s in range(SPECIES):
        for x in V_PLANES:
            d = d_of(s, x)
            if x < V_PLANES[-1]:
                c_ref[cx_at(s, x)] = 0.5 * (d + d_of(s, x + 1))
            if x in R_PLANES:
                c_ref[cy_at(s, x)] = 0.5 * (d + next_y(d))
                c_ref[cz_at(s, x)] = 0.5 * (d + next_z(d, d_side[s // 2], slot_of(s, x)))
                c_ref[back_at(s, x)] = 0.5 * (d + previous_z(d, d_side[s // 2], slot_of(s, x)))
    edges = columns(R_PLANES, d_of)
    for half in range(HALVES):
        d = d_side[half]
        c_side[4 * half] = 0.5 * (d + roll(d, -8, 1))
        c_side[4 * half + 1] = 0.5 * (d + next_y(d))
        c_side[4 * half + 2] = 0.5 * (d + side_next_z(d, edges[half]))
        c_side[4 * half + 3] = 0.5 * (d + side_previous_z(d, edges[half]))


def step(degree, planes, v_of, v_side, main_ref, side_ref, c_ref, c_side, mask, store, sides=True):
    lane = iota((ROWS, 128), 1)
    for x in planes:
        factor = DAMPING * mask_of(x, mask[0], *mask[2:])
        here = [v_of(t, x) for t in range(SPECIES)]
        for s in range(SPECIES):
            half, place, v = s // 2, slot_of(s, x), here[s]
            value = v * (1.0 - SHIFTS[degree])
            value = value + c_ref[cz_at(s, x)] * (v - next_z(v, v_side[half], place))
            value = value + c_ref[back_at(s, x)] * (v - previous_z(v, v_side[half], place))
            for t in range(SPECIES):
                value = value + main_ref[r_at(s, t, x)] * here[t]
            value = value + c_ref[cx_at(s, x)] * (v - v_of(s, x + 1))
            value = value + c_ref[cx_at(s, x - 1)] * (v - v_of(s, x - 1))
            along = c_ref[cy_at(s, x)] * (v - next_y(v))
            value = value + (along - roll(along, 1, 0))
            store(s, x, value * factor)
    if not sides:
        return None
    edges = columns(planes, v_of)
    both = []
    for half in range(HALVES):
        other = roll(v_side[half], 64, 1)
        both.append(jnp.where(lane < 64, v_side[half], other))
        both.append(jnp.where(lane < 64, other, v_side[half]))
    result = []
    for half in range(HALVES):
        v = v_side[half]
        value = v * (1.0 - SHIFTS[degree])
        value = value + c_side[4 * half + 2] * (v - side_next_z(v, edges[half]))
        value = value + c_side[4 * half + 3] * (v - side_previous_z(v, edges[half]))
        for t in range(SPECIES):
            value = value + side_ref[2 * HALVES + SPECIES * half + t] * both[t]
        across = c_side[4 * half] * (v - roll(v, -8, 1))
        value = value + (across - roll(across, 8, 1))
        along = c_side[4 * half + 1] * (v - next_y(v))
        value = value + (along - roll(along, 1, 0))
        result.append(value * (DAMPING * mask[1]))
    return result


def put_own(out_ref, s, x, value):
    out_ref[8 * s + 2 * x] = value[:8]
    out_ref[8 * s + 2 * x + 1] = value[8:16]


def first_steps(v_ref, d_ref, r_ref, x_before, x_after, edge_ref, own_before, own_after, more_before, more_after, v1_ref, v2_ref, wide_ref, wide_side, low_ref, high_ref, side_ref, c_ref, c_side, v_in, v_mid):
    main_ref = Planes(own_planes(v_ref, d_ref, r_ref, x_before, x_after), edge_ref)
    lane = iota((ROWS, 128), 1)
    for side in range(SIDES):
        side_ref[side] = unpack_z(side, own_before, own_after, more_before, more_after)
    mask = masks()

    def inside(plane, x):
        return main_ref[plane] * mask_of(x, mask[0], *mask[2:])

    v_side = [side_ref[half] * mask[1] for half in range(HALVES)]
    d_side = [side_ref[HALVES + half] * mask[1] for half in range(HALVES)]
    for s in range(SPECIES):
        for x in V_PLANES:
            v_mid[v_at(s, x)] = inside(d_at(s, x), x)
            v_in[v_at(s, x)] = inside(v_at(s, x), x)
    conduct(lambda s, x: v_mid[v_at(s, x)], d_side, c_ref, c_side)

    def store_mid(s, x, value):
        v_mid[v_at(s, x)] = value
        if 0 <= x < 4:
            put_own(v1_ref, s, x, value)

    def store_wide(s, x, value):
        wide_ref[4 * s + x] = value
        put_own(v2_ref, s, x, value)

    more = (main_ref, side_ref, c_ref, c_side, mask)
    v_side = step(0, R_PLANES, lambda s, x: v_in[v_at(s, x)], v_side, *more, store_mid)
    v_side = step(1, range(4), lambda s, x: v_mid[v_at(s, x)], v_side, *more, store_wide)
    for half in range(HALVES):
        wide_side[half] = v_side[half]
    slot = lane // 8 % 8
    for face, start, shift in ((low_ref, 0, -16), (high_ref, 4 - WIDE, 16)):
        for s in range(SPECIES):
            for n in range(WIDE):
                face[s * WIDE + n] = wide_ref[4 * s + start + n]
        kept = (slot >= start + WIDE) & (slot < start + 2 * WIDE)
        face[SPECIES * WIDE] = jnp.where(kept, v_side[0], roll(v_side[1], shift, 1))


def last_steps(r_ref, x_before, x_after, edge_ref, side_ref, c_ref, c_side, wide_ref, wide_side, before_ref, after_ref, q_ref, v1_ref, v2_ref, sums_in, v3_ref, v4_ref, sums_ref, v_in, v_mid):
    main_ref = Planes(own_planes(None, None, r_ref, x_before, x_after), edge_ref)
    mask = masks()
    for s in range(SPECIES):
        for face, start, factor in ((before_ref, -WIDE, mask[2]), (after_ref, 4, mask[3])):
            for n in range(WIDE):
                v_in[v_at(s, start + n)] = face[s * WIDE + n] * factor
    slot = iota((ROWS, 128), 1) // 8 % 8
    before, after = before_ref[SPECIES * WIDE] * mask[2], after_ref[SPECIES * WIDE] * mask[3]
    v_side = []
    for half in range(HALVES):
        value = jnp.where(slot < WIDE, roll(before, -32 - 16 * half, 1), wide_side[half])
        v_side.append(jnp.where(slot >= WIDE + 4, roll(after, 32 + 16 * half, 1), value))

    def first(s, x):
        return wide_ref[4 * s + x] if 0 <= x < 4 else v_in[v_at(s, x)]

    def store_mid(s, x, value):
        v_mid[v_at(s, x)] = value
        if 0 <= x < 4:
            put_own(v3_ref, s, x, value)

    def store_last(s, x, value):
        put_own(v4_ref, s, x, value)

    more = (main_ref, side_ref, c_ref, c_side, mask)
    v_side = step(2, R_PLANES, first, v_side, *more, store_mid)
    step(3, range(4), lambda s, x: v_mid[v_at(s, x)], v_side, *more, store_last, sides=False)

    def load(i):
        return [q_ref[a, i] for a in range(EARLIER)] + [v1_ref[i], v2_ref[i], v3_ref[i], v4_ref[i]]

    row = sums_in[...] + products(new_pairs(2) + new_pairs(3), load, q_ref.shape[1])
    sums_ref[...] = jnp.broadcast_to(jnp.sum(row, 0, keepdims=True), sums_ref.shape)


def middle_products(q_ref, v1_ref, v2_ref, before_ref, out_ref):
    def load(i):
        return [q_ref[a, i] for a in range(EARLIER)] + [v1_ref[i], v2_ref[i]]

    out_ref[...] = before_ref[...] + products(new_pairs(0) + new_pairs(1), load, q_ref.shape[1])


def products(pairs, load, count):
    def body(i, sums):
        values = load(i)
        return tuple(total + values[a] * values[b] for total, (a, b) in zip(sums, pairs))

    zero = jnp.zeros((8, 128), jnp.float32)
    sums = lax.fori_loop(0, count, body, (zero,) * len(pairs))
    lane = lax.broadcasted_iota(jnp.int32, (8, 128), 1)
    row = zero
    for total, pair in zip(sums, pairs):
        row = jnp.where(lane == SLOT[pair], jnp.sum(total, 1, keepdims=True), row)
    return row


def earlier_products(q_ref, out_ref):
    pairs = [(a, b) for b in range(EARLIER) for a in range(b + 1)]
    out_ref[...] = products(pairs, lambda i: [q_ref[a, i] for a in range(EARLIER)], q_ref.shape[1])


def new_pairs(number):
    return [(a, EARLIER + number) for a in range(EARLIER + number + 1)]


def finish_kernel(entries, sums_ref, q_ref, *refs):
    v_refs, (new_ref, coeff_ref, triangle_ref) = refs[:STEPS], refs[STEPS:]
    total = sums_ref[0]
    for i in range(1, sums_ref.shape[0]):
        total = total + sums_ref[i]
    total = jnp.broadcast_to(jnp.sum(total, 0, keepdims=True), total.shape) * (1.0 / entries)

    def entry(a, b):
        k = SLOT[(min(a, b), max(a, b))]
        return jnp.broadcast_to(total[:, k : k + 1], total.shape)

    coeff = [[entry(i, EARLIER + j) for j in range(STEPS)] for i in range(EARLIER)]
    overlap = {(a, b): entry(a, b) for b in range(EARLIER) for a in range(b + 1)}
    gram = {}
    for k in range(STEPS):
        mixed = []
        for i in range(EARLIER):
            term = -2.0 * coeff[i][k]
            for m in range(EARLIER):
                term = term + overlap[(min(i, m), max(i, m))] * coeff[m][k]
            mixed.append(term)
        for j in range(k, STEPS):
            value = entry(EARLIER + k, EARLIER + j)
            for i in range(EARLIER):
                value = value + coeff[i][j] * mixed[i]
            gram[(j, k)] = value
    factor, inverse = {}, []
    for k in range(STEPS):
        pivot = gram[(k, k)]
        for m in range(k):
            pivot = pivot - factor[(k, m)] * factor[(k, m)]
        factor[(k, k)] = jnp.sqrt(pivot)
        inverse.append(1.0 / factor[(k, k)])
        for j in range(k + 1, STEPS):
            value = gram[(j, k)]
            for m in range(k):
                value = value - factor[(j, m)] * factor[(k, m)]
            factor[(j, k)] = value * inverse[k]
    row = lax.broadcasted_iota(jnp.int32, total.shape, 0)
    lane = lax.broadcasted_iota(jnp.int32, total.shape, 1)
    table = jnp.zeros_like(total)
    for i in range(EARLIER):
        for j in range(STEPS):
            table = jnp.where((row == j) & (lane == i), coeff[i][j], table)
    coeff_ref[...] = table[:STEPS, :EARLIER]
    table = jnp.zeros_like(total)
    for (j, k), value in factor.items():
        table = jnp.where((row == k) & (lane == j), value, table)
    triangle_ref[...] = table[:STEPS, :STEPS]

    def body(n, carry):
        earlier = [q_ref[i, n] for i in range(EARLIER)]
        done = []
        for j in range(STEPS):
            value = v_refs[j][n]
            for i in range(EARLIER):
                value = value - coeff[i][j] * earlier[i]
            for k in range(j):
                value = value - factor[(j, k)] * done[k]
            done.append(value * inverse[j])
            new_ref[j, n] = done[j]
        return carry

    lax.fori_loop(0, q_ref.shape[1], body, 0)


def call(body, outs, cost, *args, **more):
    return pl.pallas_call(
        body,
        out_shape=[jax.ShapeDtypeStruct(shape, jnp.float32) for shape in outs],
        cost_estimate=pl.CostEstimate(flops=cost, bytes_accessed=cost, transcendentals=0),
        compiler_params=pltpu.CompilerParams(vmem_limit_bytes=24 << 20),
        **more,
    )(*args)


def shifts(axis):
    count = lax.axis_size(axis)
    up = [(i, (i + 1) % count) for i in range(count)]
    return up, [(target, source) for source, target in up]


def exchange(axis, low, high):
    up, down = shifts(axis)
    return lax.ppermute(high, axis, up), lax.ppermute(low, axis, down)


def on_device(earlier_basis, diffusivity, reaction):
    span_x, span_y, span_z = diffusivity.shape[1:]
    tiles = SPECIES * span_x * span_y // 8
    devices = 1
    for axis in AXES:
        devices *= lax.axis_size(axis)
    entries = tiles * 8 * span_z * devices
    in_hbm = pl.BlockSpec(memory_space=pltpu.HBM)
    given = (earlier_basis, diffusivity, reaction)
    face = (2 * SPECIES * WIDE + SPECIES * SPECIES, span_y, span_z)
    field = diffusivity.shape
    low, high, *kept = call(
        x_faces,
        [face, face, field, field],
        1 << 20,
        *[pltpu.with_memory_space_constraint(a, pltpu.HBM) for a in given],
        in_specs=[in_hbm] * 3,
        scratch_shapes=[pltpu.SemaphoreType.DMA((8,))],
    )
    x_halos = exchange("gx", low, high)
    kept.append(reaction)
    face = (Y_TILES[0], 8, span_z)
    z_face = (SIDES // 4, 16, span_z)
    own = call(own_faces, [face, face, z_face, z_face], 1 << 20, *kept)
    y_own = exchange("gy", *own[:2])
    up, down = shifts("gz")
    z_before = lax.ppermute(own[3], "gz", up)
    z_after = lax.ppermute(own[2], "gz", down)
    z_own = (z_before, z_after)
    face = (Y_TILES[1], 8, span_z)
    faces = call(more_y_faces, [face, face], 1 << 20, *x_halos)
    y_more = exchange("gy", *faces)
    face = (2 * BLOCKS, 8, span_z)
    edge, low, high = call(more_z_faces, [(PLANES, 8, span_z), face, face], 1 << 20, *x_halos, *y_own, *y_more)
    z_more = exchange("gz", low, high)
    basis = earlier_basis.reshape(EARLIER, tiles, 8, span_z)
    (sums,) = call(earlier_products, [(8, span_z)], 4 << 20, basis)
    own = (tiles, 8, span_z)
    scratch = [pltpu.VMEM((D_BASE, ROWS, span_z), jnp.float32)] * 2
    several = [
        (count, ROWS, span_z)
        for count in (SPECIES * span_x, HALVES, SPECIES * WIDE + 1, SPECIES * WIDE + 1, SIDES, CONDUCTS, 4 * HALVES)
    ]
    v1, v2, wide, wide_side, low, high, side, conducts, side_conducts = call(
        first_steps,
        [own, own] + several,
        1 << 20,
        *kept,
        *x_halos,
        edge,
        *z_own,
        *z_more,
        scratch_shapes=scratch,
    )
    halos = exchange("gx", low, high)
    (sums,) = call(middle_products, [(8, span_z)], 4 << 20, basis, v1, v2, sums)
    v3, v4, rows = call(
        last_steps,
        [own, own, (devices, span_z)],
        1 << 20,
        reaction,
        *x_halos,
        edge,
        side,
        conducts,
        side_conducts,
        wide,
        wide_side,
        *halos,
        basis,
        v1,
        v2,
        sums,
        scratch_shapes=scratch,
    )
    rows = lax.all_to_all(rows.reshape(devices, 1, span_z), AXES, 0, 0)
    new, coeff, triangle = call(
        functools.partial(finish_kernel, entries),
        [(STEPS, tiles, 8, span_z), (STEPS, EARLIER), (STEPS, STEPS)],
        1 << 20,
        rows.reshape(devices // 8, 8, span_z),
        basis,
        v1,
        v2,
        v3,
        v4,
    )
    return new.reshape((STEPS, SPECIES, span_x, span_y, span_z)), coeff.T, triangle


def solution(mesh):
    in_specs = (
        P(None, None, "gx", "gy", "gz"),
        P(None, "gx", "gy", "gz"),
        P(None, None, "gx", "gy", "gz"),
    )
    out_specs = (P(None, None, "gx", "gy", "gz"), P(), P())
    return jax.shard_map(
        on_device, mesh=mesh, in_specs=in_specs, out_specs=out_specs, check_vma=False
    )
```

```python
import functools

import jax
import jax.numpy as jnp
from jax import lax
from jax.experimental import pallas as pl
from jax.experimental.pallas import tpu as pltpu
from jax.sharding import PartitionSpec as P

SPECIES = 4
STEPS = 4
EARLIER = 8
SHIFTS = (6.0, 9.0, 14.0, 17.0)
DAMPING = 0.2
AXES = ("gx", "gy", "gz")

VECTORS = EARLIER + STEPS
SLOT = {}
for _b in range(VECTORS):
    for _a in range(_b + 1):
        SLOT[(_a, _b)] = len(SLOT)

WIDE = 2
DEEP = 4
ROWS = 24
V_PLANES = tuple(range(-WIDE, 4 + WIDE))
R_PLANES = tuple(range(-1, 5))
V_BASE = 0
D_BASE = SPECIES * len(V_PLANES)
R_BASE = 2 * D_BASE
PLANES = R_BASE + SPECIES * SPECIES * len(R_PLANES)
HALVES = SPECIES // 2
SIDES = 2 * HALVES + HALVES * SPECIES
BLOCKS = SIDES // 2


def v_at(s, x):
    return V_BASE + s * len(V_PLANES) + x + WIDE


def d_at(s, x):
    return D_BASE + s * len(V_PLANES) + x + WIDE


def r_at(s, t, x):
    return R_BASE + (s * SPECIES + t) * len(R_PLANES) + x + 1


def iota(shape, dim):
    return lax.broadcasted_iota(jnp.int32, shape, dim)


def roll(value, shift, axis):
    shift %= value.shape[axis]
    return pltpu.roll(value, shift, axis) if shift else value


def x_faces(q_ref, d_ref, r_ref, low_ref, high_ref, v_out, d_out, sems):
    copies = []
    for face, planes, plane in ((low_ref, pl.ds(0, WIDE), 0), (high_ref, pl.ds(4 - WIDE, WIDE), 3)):
        for n, source in enumerate((q_ref.at[EARLIER - 1, :, planes], d_ref.at[:, planes])):
            target = face.at[pl.ds(n * SPECIES * WIDE, SPECIES * WIDE)]
            copies.append((source, target.reshape((SPECIES, WIDE) + face.shape[1:])))
        target = face.at[pl.ds(2 * SPECIES * WIDE, SPECIES * SPECIES)]
        copies.append((r_ref.at[:, :, plane], target.reshape((SPECIES, SPECIES) + face.shape[1:])))
    copies += [(q_ref.at[EARLIER - 1], v_out), (d_ref, d_out)]
    started = [pltpu.make_async_copy(a, b, sems.at[n]) for n, (a, b) in enumerate(copies)]
    for copy in started:
        copy.start()
    for copy in started:
        copy.wait()


def own_planes(v_ref, d_ref, r_ref, before_ref, after_ref):
    def pick(own, slot, width, x):
        if x < 0:
            return lambda rows: before_ref[slot + x + width, rows]
        if x > 3:
            return lambda rows: after_ref[slot + x - 4, rows]
        return lambda rows: own(x, rows)

    planes = []
    for s in range(SPECIES):
        for x in V_PLANES:
            planes.append(pick(lambda x, rows, s=s: v_ref[s, x, rows], s * WIDE, WIDE, x))
    for s in range(SPECIES):
        for x in V_PLANES:
            planes.append(pick(lambda x, rows, s=s: d_ref[s, x, rows], (SPECIES + s) * WIDE, WIDE, x))
    for s in range(SPECIES):
        for t in range(SPECIES):
            slot = 2 * SPECIES * WIDE + s * SPECIES + t
            for x in R_PLANES:
                planes.append(pick(lambda x, rows, s=s, t=t: r_ref[s, t, x, rows], slot, 1, x))
    return planes


def y_places():
    places, used = {}, [0, 0]

    def put(message, planes, rows):
        per = 8 // rows
        for n, plane in enumerate(planes):
            places[plane] = (message, used[message] + n // per, n % per, rows)
        used[message] += len(planes) // per

    near, far, own = [], [], []
    for base in (v_at, d_at):
        for s in range(SPECIES):
            for x in V_PLANES:
                (own if 0 <= x < 4 else near if -1 <= x < 5 else far).append(base(s, x))
    for s in range(SPECIES):
        for t in range(SPECIES):
            for x in R_PLANES:
                (own if 0 <= x < 4 else far).append(r_at(s, t, x))
    put(0, own, DEEP)
    put(1, near, DEEP)
    put(1, far, 2)
    return places, used


Y_PLACES, Y_TILES = y_places()


def y_faces(message, planes, low_ref, high_ref):
    row = iota((8, 128), 0)
    low, high = [None] * Y_TILES[message], [None] * Y_TILES[message]
    for plane, (number, tile, place, rows) in Y_PLACES.items():
        if number != message:
            continue
        first = roll(planes[plane](pl.ds(0, 8)), rows * place, 0)
        final = roll(planes[plane](pl.ds(8, 8)), rows * place + rows, 0)
        here = row // rows == place
        low[tile] = first if low[tile] is None else jnp.where(here, first, low[tile])
        high[tile] = final if high[tile] is None else jnp.where(here, final, high[tile])
    for tile in range(Y_TILES[message]):
        low_ref[tile] = low[tile]
        high_ref[tile] = high[tile]


def own_faces(v_ref, d_ref, r_ref, y_low, y_high, z_low, z_high):
    planes = own_planes(v_ref, d_ref, r_ref, None, None)
    y_faces(0, planes, y_low, y_high)
    for block, found in enumerate(z_groups(True)):
        z_low[block], z_high[block] = pack_z(found, lambda plane: planes[plane](pl.ds(0, 16)), 16)


def more_y_faces(before_ref, after_ref, low_ref, high_ref):
    y_faces(1, own_planes(None, None, None, before_ref, after_ref), low_ref, high_ref)


def side_planes(side):
    found = []
    for half in range(2):
        for x in V_PLANES:
            if side < 2 * HALVES:
                s = side % HALVES * 2 + half
                found.append(v_at(s, x) if side < HALVES else d_at(s, x))
            else:
                pair, t = divmod(side - 2 * HALVES, SPECIES)
                found.append(r_at(2 * pair + half, t, x) if x in R_PLANES else None)
    return found


def z_groups(own):
    blocks = [[] for _ in range(SIDES // 4)]
    for side in range(SIDES):
        for slot, plane in enumerate(side_planes(side)):
            if plane is not None and own == (WIDE <= slot % 8 < WIDE + 4):
                group = (2 * slot + 8 * (side % 4 // 2) + side % 2) % 32
                blocks[side // 4].append((plane, group))
    return blocks


def z_edge_groups():
    blocks = [[] for _ in range(BLOCKS)]
    for side in range(SIDES):
        for slot, plane in enumerate(side_planes(side)):
            if plane is not None:
                blocks[side // 2].append((plane, 2 * slot + side % 2))
    return blocks


def pack_z(planes, value_of, rows):
    group = iota((rows, 128), 1) // DEEP
    low = high = jnp.zeros((rows, 128), jnp.float32)
    for plane, k in planes:
        value = value_of(plane)
        low = jnp.where(group == k, roll(value, DEEP * k, 1), low)
        high = jnp.where(group == k, roll(value, DEEP * k + DEEP, 1), high)
    return low, high


def more_z_faces(x_before, x_after, own_before, own_after, more_before, more_after, edge_ref, low_ref, high_ref):
    planes = own_planes(None, None, None, x_before, x_after)
    top = iota((8, 128), 0) < DEEP
    befores, afters = (own_before, more_before), (own_after, more_after)
    for block, found in enumerate(z_groups(False)):
        low, high = pack_z(found, lambda plane: planes[plane](pl.ds(0, 16)), 16)
        for half in range(2):
            low_ref[2 * block + half] = low[8 * half : 8 * half + 8]
            high_ref[2 * block + half] = high[8 * half : 8 * half + 8]

    def value_of(plane):
        message, tile, place, rows = Y_PLACES[plane]
        after = roll(afters[message][tile], -rows * place, 0)
        before = roll(befores[message][tile], 8 - rows - rows * place, 0)
        edge_ref[plane] = jnp.where(top, after, before)
        return edge_ref[plane]

    for block, found in enumerate(z_edge_groups()):
        low_ref[BLOCKS + block], high_ref[BLOCKS + block] = pack_z(found, value_of, 8)


def unpack_z(side, own_before, own_after, more_before, more_after):
    lane = iota((16, 128), 1)
    block, turned, part = side // 4, side % 4 // 2, side % 2
    own = (lane // 8 % 8 >= WIDE) & (lane // 8 % 8 < WIDE + 4)
    if turned:
        own = ~own

    def rows(own_ref, more_ref):
        more = jnp.concatenate([more_ref[2 * block], more_ref[2 * block + 1]], 0)
        return jnp.where(own, own_ref[block], more)

    def join(before, after, shift):
        early = iota(before.shape, 1) % 8 < DEEP
        return jnp.where(early, roll(before, -shift - DEEP * part, 1), roll(after, DEEP - shift - DEEP * part, 1))

    main = join(rows(own_before, more_before), rows(own_after, more_after), 32 * turned)
    edge = join(more_before[BLOCKS + side // 2], more_after[BLOCKS + side // 2], 0)
    return jnp.concatenate([main, edge], 0)


class Planes:
    def __init__(self, planes, edge_ref):
        self.planes, self.edge_ref = planes, edge_ref

    def __getitem__(self, plane):
        return jnp.concatenate([self.planes[plane](pl.ds(0, 16)), self.edge_ref[plane]], 0)


def masks():
    first = {axis: lax.axis_index(axis) == 0 for axis in AXES}
    final = {axis: lax.axis_index(axis) == lax.axis_size(axis) - 1 for axis in AXES}

    def keep(flag):
        return jnp.where(flag, 0.0, 1.0).astype(jnp.float32)

    row, lane = iota((ROWS, 128), 0), iota((ROWS, 128), 1)
    main = jnp.where(row < 16, 1.0, jnp.where(row < 16 + DEEP, keep(final["gy"]), keep(first["gy"])))
    slot = lane // 8 % 8
    side = main * jnp.where(lane % 8 < DEEP, keep(first["gz"]), keep(final["gz"]))
    before, after = keep(first["gx"]), keep(final["gx"])
    side = side * jnp.where(slot < WIDE, before, jnp.where(slot < WIDE + 4, 1.0, after))
    return main, side, before, after


def mask_of(x, main, before, after):
    if 0 <= x < 4:
        return main
    return main * (before if x < 0 else after)


def next_y(value):
    return roll(value, -1, 0)


def slot_of(s, x):
    return 64 * (s % 2) + 8 * (x + WIDE)


def columns(planes, value_of):
    group = iota((ROWS, 128), 1) // 8
    found = []
    for half in range(HALVES):
        value = jnp.zeros((ROWS, 128), jnp.float32)
        for s in (2 * half, 2 * half + 1):
            for x in planes:
                place = slot_of(s, x)
                value = jnp.where(group == place // 8, roll(value_of(s, x), place + DEEP, 1), value)
        found.append(value)
    return found


def next_z(value, side, place):
    lane = iota((ROWS, 128), 1)
    return jnp.where(lane == 127, roll(side, 127 - place - DEEP, 1), roll(value, -1, 1))


def previous_z(value, side, place):
    lane = iota((ROWS, 128), 1)
    return jnp.where(lane == 0, roll(side, -(place + DEEP - 1), 1), roll(value, 1, 1))


def side_next_z(side, edge):
    return roll(jnp.where(iota((ROWS, 128), 1) % 8 == DEEP, edge, side), -1, 1)


def side_previous_z(side, edge):
    return roll(jnp.where(iota((ROWS, 128), 1) % 8 == DEEP - 1, edge, side), 1, 1)


def cx_at(s, x):
    return s * 7 + x + 2


def cy_at(s, x):
    return SPECIES * 7 + s * 6 + x + 1


def cz_at(s, x):
    return SPECIES * 13 + s * 6 + x + 1


def back_at(s, x):
    return SPECIES * 19 + s * 6 + x + 1


CONDUCTS = SPECIES * 25


WITHOUT_Z = SPECIES * 13


class Conducts:
    def __init__(self, plain_ref, z_ref):
        self.plain_ref, self.z_ref = plain_ref, z_ref

    def __getitem__(self, k):
        return self.plain_ref[k] if k < WITHOUT_Z else self.z_ref[k - WITHOUT_Z]


def early_steps(v_ref, d_ref, r_ref, x_before, x_after, edge_ref, v_in, d_in, c_ref, sum_ref, d_edge, v_edge):
    main_ref = Planes(own_planes(v_ref, d_ref, r_ref, x_before, x_after), edge_ref)
    mask = masks()
    for s in range(SPECIES):
        for x in V_PLANES:
            factor = mask_of(x, mask[0], *mask[2:])
            v_in[v_at(s, x)] = main_ref[v_at(s, x)] * factor
            d_in[v_at(s, x)] = main_ref[d_at(s, x)] * factor
    lane = iota((ROWS, 128), 1)
    first, final = lane == 0, lane == 127
    for s in range(SPECIES):
        for x in V_PLANES:
            d = d_in[v_at(s, x)]
            if x < V_PLANES[-1]:
                c_ref[cx_at(s, x)] = 0.5 * (d + d_in[v_at(s, x + 1)])
            if x in R_PLANES:
                c_ref[cy_at(s, x)] = 0.5 * (d + next_y(d))
                c_ref[cz_at(s, x)] = jnp.where(final, 0.0, 0.5 * (d + roll(d, -1, 1)))
                c_ref[back_at(s, x)] = jnp.where(first, 0.0, 0.5 * (d + roll(d, 1, 1)))
    for x in R_PLANES:
        here = [v_in[v_at(t, x)] for t in range(SPECIES)]
        for s in range(SPECIES):
            v = here[s]
            value = v * (1.0 - SHIFTS[0])
            value = value + c_ref[cz_at(s, x)] * (v - roll(v, -1, 1))
            value = value + c_ref[back_at(s, x)] * (v - roll(v, 1, 1))
            for t in range(SPECIES):
                value = value + main_ref[r_at(s, t, x)] * here[t]
            value = value + c_ref[cx_at(s, x)] * (v - v_in[v_at(s, x + 1)])
            value = value + c_ref[cx_at(s, x - 1)] * (v - v_in[v_at(s, x - 1)])
            along = c_ref[cy_at(s, x)] * (v - next_y(v))
            sum_ref[6 * s + x + 1] = value + (along - roll(along, 1, 0))
    for half, (d, v) in enumerate(
        zip(columns(R_PLANES, lambda s, x: d_in[v_at(s, x)]), columns(R_PLANES, lambda s, x: v_in[v_at(s, x)]))
    ):
        d_edge[half] = d
        v_edge[half] = v


def end_first_step(v_in, d_in, c_ref, sum_ref, d_side, v_side, z_ref, mask, store):
    lane = iota((ROWS, 128), 1)
    first, final = lane == 0, lane == 127
    for s in range(SPECIES):
        for x in R_PLANES:
            place, half, n = slot_of(s, x), s // 2, 6 * s + x + 1

            def beyond(side, place=place, half=half):
                return jnp.where(final, roll(side[half], 127 - place - DEEP, 1), roll(side[half], 1 - DEEP - place, 1))

            more = jnp.where(first | final, 0.5 * (d_in[v_at(s, x)] + beyond(d_side)), 0.0)
            z_ref[cz_at(s, x) - WITHOUT_Z] = jnp.where(final, more, c_ref[cz_at(s, x)])
            z_ref[back_at(s, x) - WITHOUT_Z] = jnp.where(first, more, c_ref[back_at(s, x)])
            value = sum_ref[n] + more * (v_in[v_at(s, x)] - beyond(v_side))
            store(s, x, value * (DAMPING * mask_of(x, mask[0], *mask[2:])))


def side_conduct(d_side, edges, c_side):
    for half in range(HALVES):
        d = d_side[half]
        c_side[4 * half] = 0.5 * (d + roll(d, -8, 1))
        c_side[4 * half + 1] = 0.5 * (d + next_y(d))
        c_side[4 * half + 2] = 0.5 * (d + side_next_z(d, edges[half]))
        c_side[4 * half + 3] = 0.5 * (d + side_previous_z(d, edges[half]))


def step(degree, planes, v_of, v_side, main_ref, side_ref, c_ref, c_side, mask, store, sides=True):
    lane = iota((ROWS, 128), 1)
    for x in planes:
        factor = DAMPING * mask_of(x, mask[0], *mask[2:])
        here = [v_of(t, x) for t in range(SPECIES)]
        for s in range(SPECIES):
            half, place, v = s // 2, slot_of(s, x), here[s]
            value = v * (1.0 - SHIFTS[degree])
            value = value + c_ref[cz_at(s, x)] * (v - next_z(v, v_side[half], place))
            value = value + c_ref[back_at(s, x)] * (v - previous_z(v, v_side[half], place))
            for t in range(SPECIES):
                value = value + main_ref[r_at(s, t, x)] * here[t]
            value = value + c_ref[cx_at(s, x)] * (v - v_of(s, x + 1))
            value = value + c_ref[cx_at(s, x - 1)] * (v - v_of(s, x - 1))
            along = c_ref[cy_at(s, x)] * (v - next_y(v))
            value = value + (along - roll(along, 1, 0))
            store(s, x, value * factor)
    if not sides:
        return None
    return side_step(degree, columns(planes, v_of), v_side, side_ref, c_side, mask)


def side_step(degree, edges, v_side, side_ref, c_side, mask):
    lane = iota((ROWS, 128), 1)
    both = []
    for half in range(HALVES):
        other = roll(v_side[half], 64, 1)
        both.append(jnp.where(lane < 64, v_side[half], other))
        both.append(jnp.where(lane < 64, other, v_side[half]))
    result = []
    for half in range(HALVES):
        v = v_side[half]
        value = v * (1.0 - SHIFTS[degree])
        value = value + c_side[4 * half + 2] * (v - side_next_z(v, edges[half]))
        value = value + c_side[4 * half + 3] * (v - side_previous_z(v, edges[half]))
        for t in range(SPECIES):
            value = value + side_ref[2 * HALVES + SPECIES * half + t] * both[t]
        across = c_side[4 * half] * (v - roll(v, -8, 1))
        value = value + (across - roll(across, 8, 1))
        along = c_side[4 * half + 1] * (v - next_y(v))
        value = value + (along - roll(along, 1, 0))
        result.append(value * (DAMPING * mask[1]))
    return result


FACE_EDGES = SPECIES * WIDE * 2
FACE_SIDE = FACE_EDGES + SPECIES
FACE_TILES = FACE_SIDE + 3


def put_own(out_ref, s, x, value):
    out_ref[8 * s + 2 * x] = value[:8]
    out_ref[8 * s + 2 * x + 1] = value[8:16]


def first_steps(r_ref, x_before, x_after, edge_ref, v_in, d_in, c_early, sum_ref, d_edge, v_edge, own_before, own_after, more_before, more_after, v1_ref, v2_ref, wide_ref, wide_side, low_ref, high_ref, side_ref, z_ref, c_side, v_mid):
    main_ref = Planes(own_planes(None, None, r_ref, x_before, x_after), edge_ref)
    lane = iota((ROWS, 128), 1)
    for side in range(SIDES):
        side_ref[side] = unpack_z(side, own_before, own_after, more_before, more_after)
    mask = masks()
    v_side = [side_ref[half] * mask[1] for half in range(HALVES)]
    d_side = [side_ref[HALVES + half] * mask[1] for half in range(HALVES)]
    side_conduct(d_side, d_edge, c_side)
    c_ref = Conducts(c_early, z_ref)

    def store_mid(s, x, value):
        v_mid[v_at(s, x)] = value
        if 0 <= x < 4:
            put_own(v1_ref, s, x, value)

    def store_wide(s, x, value):
        wide_ref[4 * s + x] = value
        put_own(v2_ref, s, x, value)

    more = (main_ref, side_ref, c_ref, c_side, mask)
    end_first_step(v_in, d_in, c_early, sum_ref, d_side, v_side, z_ref, mask, store_mid)
    v_side = side_step(0, v_edge, v_side, side_ref, c_side, mask)
    v_side = step(1, range(4), lambda s, x: v_mid[v_at(s, x)], v_side, *more, store_wide)
    for half in range(HALVES):
        wide_side[half] = v_side[half]
    slot = lane // 8 % 8
    row = iota((8, 128), 0)
    near = (row < 2) | (row >= 6)
    for face, start, shift in ((low_ref, 0, -16), (high_ref, 4 - WIDE, 16)):
        for s in range(SPECIES):
            values = [wide_ref[4 * s + start + n] for n in range(WIDE)]
            for n in range(WIDE):
                face[(s * WIDE + n) * 2] = values[n][:8]
                face[(s * WIDE + n) * 2 + 1] = values[n][8:16]
            face[FACE_EDGES + s] = jnp.where(near, values[0][16:], roll(values[1][16:], DEEP, 0))
        kept = (slot >= start + WIDE) & (slot < start + 2 * WIDE)
        packed = jnp.where(kept, v_side[0], roll(v_side[1], shift, 1))
        for n in range(3):
            face[FACE_SIDE + n] = packed[8 * n : 8 * n + 8]


def last_steps(r_ref, x_before, x_after, edge_ref, side_ref, c_early, z_ref, c_side, wide_ref, wide_side, before_ref, after_ref, q_ref, v1_ref, v2_ref, sums_in, v3_ref, v4_ref, sums_ref, v_in, v_mid):
    main_ref = Planes(own_planes(None, None, r_ref, x_before, x_after), edge_ref)
    c_ref = Conducts(c_early, z_ref)
    mask = masks()
    for s in range(SPECIES):
        for face, start, factor in ((before_ref, -WIDE, mask[2]), (after_ref, 4, mask[3])):
            for n in range(WIDE):
                k = (s * WIDE + n) * 2
                value = jnp.concatenate([face[k], face[k + 1], roll(face[FACE_EDGES + s], DEEP * n, 0)], 0)
                v_in[v_at(s, start + n)] = value * factor
    slot = iota((ROWS, 128), 1) // 8 % 8
    before, after = (
        jnp.concatenate([face[FACE_SIDE + n] for n in range(3)], 0) * factor
        for face, factor in ((before_ref, mask[2]), (after_ref, mask[3]))
    )
    v_side = []
    for half in range(HALVES):
        value = jnp.where(slot < WIDE, roll(before, -32 - 16 * half, 1), wide_side[half])
        v_side.append(jnp.where(slot >= WIDE + 4, roll(after, 32 + 16 * half, 1), value))

    def first(s, x):
        return wide_ref[4 * s + x] if 0 <= x < 4 else v_in[v_at(s, x)]

    def store_mid(s, x, value):
        v_mid[v_at(s, x)] = value
        if 0 <= x < 4:
            put_own(v3_ref, s, x, value)

    def store_last(s, x, value):
        put_own(v4_ref, s, x, value)

    more = (main_ref, side_ref, c_ref, c_side, mask)
    v_side = step(2, R_PLANES, first, v_side, *more, store_mid)
    step(3, range(4), lambda s, x: v_mid[v_at(s, x)], v_side, *more, store_last, sides=False)

    def load(i):
        return [q_ref[a, i] for a in range(EARLIER)] + [v1_ref[i], v2_ref[i], v3_ref[i], v4_ref[i]]

    row = sums_in[...] + products(new_pairs(2) + new_pairs(3), load, q_ref.shape[1])
    sums_ref[...] = jnp.broadcast_to(jnp.sum(row, 0, keepdims=True), sums_ref.shape)


def middle_products(q_ref, v1_ref, v2_ref, before_ref, out_ref):
    def load(i):
        return [q_ref[a, i] for a in range(EARLIER)] + [v1_ref[i], v2_ref[i]]

    out_ref[...] = before_ref[...] + products(new_pairs(0) + new_pairs(1), load, q_ref.shape[1])


def products(pairs, load, count):
    def body(i, sums):
        values = load(i)
        return tuple(total + values[a] * values[b] for total, (a, b) in zip(sums, pairs))

    zero = jnp.zeros((8, 128), jnp.float32)
    sums = lax.fori_loop(0, count, body, (zero,) * len(pairs))
    lane = lax.broadcasted_iota(jnp.int32, (8, 128), 1)
    row = zero
    for total, pair in zip(sums, pairs):
        row = jnp.where(lane == SLOT[pair], jnp.sum(total, 1, keepdims=True), row)
    return row


def earlier_products(q_ref, out_ref):
    pairs = [(a, b) for b in range(EARLIER) for a in range(b + 1)]
    out_ref[...] = products(pairs, lambda i: [q_ref[a, i] for a in range(EARLIER)], q_ref.shape[1])


def new_pairs(number):
    return [(a, EARLIER + number) for a in range(EARLIER + number + 1)]


def finish_kernel(entries, sums_ref, q_ref, *refs):
    v_refs, (new_ref, coeff_ref, triangle_ref) = refs[:STEPS], refs[STEPS:]
    total = sums_ref[0]
    for i in range(1, sums_ref.shape[0]):
        total = total + sums_ref[i]
    total = jnp.broadcast_to(jnp.sum(total, 0, keepdims=True), total.shape) * (1.0 / entries)

    def entry(a, b):
        k = SLOT[(min(a, b), max(a, b))]
        return jnp.broadcast_to(total[:, k : k + 1], total.shape)

    coeff = [[entry(i, EARLIER + j) for j in range(STEPS)] for i in range(EARLIER)]
    overlap = {(a, b): entry(a, b) for b in range(EARLIER) for a in range(b + 1)}
    gram = {}
    for k in range(STEPS):
        mixed = []
        for i in range(EARLIER):
            term = -2.0 * coeff[i][k]
            for m in range(EARLIER):
                term = term + overlap[(min(i, m), max(i, m))] * coeff[m][k]
            mixed.append(term)
        for j in range(k, STEPS):
            value = entry(EARLIER + k, EARLIER + j)
            for i in range(EARLIER):
                value = value + coeff[i][j] * mixed[i]
            gram[(j, k)] = value
    factor, inverse = {}, []
    for k in range(STEPS):
        pivot = gram[(k, k)]
        for m in range(k):
            pivot = pivot - factor[(k, m)] * factor[(k, m)]
        factor[(k, k)] = jnp.sqrt(pivot)
        inverse.append(1.0 / factor[(k, k)])
        for j in range(k + 1, STEPS):
            value = gram[(j, k)]
            for m in range(k):
                value = value - factor[(j, m)] * factor[(k, m)]
            factor[(j, k)] = value * inverse[k]
    row = lax.broadcasted_iota(jnp.int32, total.shape, 0)
    lane = lax.broadcasted_iota(jnp.int32, total.shape, 1)
    table = jnp.zeros_like(total)
    for i in range(EARLIER):
        for j in range(STEPS):
            table = jnp.where((row == j) & (lane == i), coeff[i][j], table)
    coeff_ref[...] = table[:STEPS, :EARLIER]
    table = jnp.zeros_like(total)
    for (j, k), value in factor.items():
        table = jnp.where((row == k) & (lane == j), value, table)
    triangle_ref[...] = table[:STEPS, :STEPS]

    def body(n, carry):
        earlier = [q_ref[i, n] for i in range(EARLIER)]
        done = []
        for j in range(STEPS):
            value = v_refs[j][n]
            for i in range(EARLIER):
                value = value - coeff[i][j] * earlier[i]
            for k in range(j):
                value = value - factor[(j, k)] * done[k]
            done.append(value * inverse[j])
            new_ref[j, n] = done[j]
        return carry

    lax.fori_loop(0, q_ref.shape[1], body, 0)


def call(body, outs, cost, *args, **more):
    return pl.pallas_call(
        body,
        out_shape=[jax.ShapeDtypeStruct(shape, jnp.float32) for shape in outs],
        cost_estimate=pl.CostEstimate(flops=cost, bytes_accessed=cost, transcendentals=0),
        compiler_params=pltpu.CompilerParams(vmem_limit_bytes=24 << 20),
        **more,
    )(*args)


def shifts(axis):
    count = lax.axis_size(axis)
    up = [(i, (i + 1) % count) for i in range(count)]
    return up, [(target, source) for source, target in up]


def exchange(axis, low, high):
    up, down = shifts(axis)
    return lax.ppermute(high, axis, up), lax.ppermute(low, axis, down)


def on_device(earlier_basis, diffusivity, reaction):
    span_x, span_y, span_z = diffusivity.shape[1:]
    tiles = SPECIES * span_x * span_y // 8
    devices = 1
    for axis in AXES:
        devices *= lax.axis_size(axis)
    entries = tiles * 8 * span_z * devices
    in_hbm = pl.BlockSpec(memory_space=pltpu.HBM)
    given = (earlier_basis, diffusivity, reaction)
    face = (2 * SPECIES * WIDE + SPECIES * SPECIES, span_y, span_z)
    field = diffusivity.shape
    low, high, *kept = call(
        x_faces,
        [face, face, field, field],
        1 << 20,
        *[pltpu.with_memory_space_constraint(a, pltpu.HBM) for a in given],
        in_specs=[in_hbm] * 3,
        scratch_shapes=[pltpu.SemaphoreType.DMA((8,))],
    )
    x_halos = exchange("gx", low, high)
    kept.append(reaction)
    face = (Y_TILES[0], 8, span_z)
    z_face = (SIDES // 4, 16, span_z)
    own = call(own_faces, [face, face, z_face, z_face], 1 << 20, *kept)
    y_own = exchange("gy", *own[:2])
    up, down = shifts("gz")
    z_before = lax.ppermute(own[3], "gz", up)
    z_after = lax.ppermute(own[2], "gz", down)
    z_own = (z_before, z_after)
    face = (Y_TILES[1], 8, span_z)
    faces = call(more_y_faces, [face, face], 1 << 20, *x_halos)
    y_more = exchange("gy", *faces)
    face = (2 * BLOCKS, 8, span_z)
    edge, low, high = call(more_z_faces, [(PLANES, 8, span_z), face, face], 1 << 20, *x_halos, *y_own, *y_more)
    z_more = exchange("gz", low, high)
    basis = earlier_basis.reshape(EARLIER, tiles, 8, span_z)
    (sums,) = call(earlier_products, [(8, span_z)], 4 << 20, basis)
    own = (tiles, 8, span_z)
    plane = (ROWS, span_z)
    early = call(
        early_steps,
        [(count,) + plane for count in (D_BASE, D_BASE, CONDUCTS, SPECIES * len(R_PLANES), HALVES, HALVES)],
        1 << 20,
        *kept,
        *x_halos,
        edge,
    )
    scratch = [pltpu.VMEM((D_BASE,) + plane, jnp.float32)]
    face = (FACE_TILES, 8, span_z)
    several = [(count,) + plane for count in (SPECIES * span_x, HALVES)] + [face, face]
    several += [(count,) + plane for count in (SIDES, CONDUCTS - WITHOUT_Z, 4 * HALVES)]
    v1, v2, wide, wide_side, low, high, side, z_conducts, side_conducts = call(
        first_steps,
        [own, own] + several,
        1 << 20,
        reaction,
        *x_halos,
        edge,
        *early,
        *z_own,
        *z_more,
        scratch_shapes=scratch,
    )
    halos = exchange("gx", low, high)
    (sums,) = call(middle_products, [(8, span_z)], 4 << 20, basis, v1, v2, sums)
    v3, v4, rows = call(
        last_steps,
        [own, own, (devices, span_z)],
        1 << 20,
        reaction,
        *x_halos,
        edge,
        side,
        early[2],
        z_conducts,
        side_conducts,
        wide,
        wide_side,
        *halos,
        basis,
        v1,
        v2,
        sums,
        scratch_shapes=scratch * 2,
    )
    rows = lax.all_to_all(rows.reshape(devices, 1, span_z), AXES, 0, 0)
    new, coeff, triangle = call(
        functools.partial(finish_kernel, entries),
        [(STEPS, tiles, 8, span_z), (STEPS, EARLIER), (STEPS, STEPS)],
        1 << 20,
        rows.reshape(devices // 8, 8, span_z),
        basis,
        v1,
        v2,
        v3,
        v4,
    )
    return new.reshape((STEPS, SPECIES, span_x, span_y, span_z)), coeff.T, triangle


def solution(mesh):
    in_specs = (
        P(None, None, "gx", "gy", "gz"),
        P(None, "gx", "gy", "gz"),
        P(None, None, "gx", "gy", "gz"),
    )
    out_specs = (P(None, None, "gx", "gy", "gz"), P(), P())
    return jax.shard_map(
        on_device, mesh=mesh, in_specs=in_specs, out_specs=out_specs, check_vma=False
    )
```

```python
import functools

import jax
import jax.numpy as jnp
from jax import lax
from jax.experimental import pallas as pl
from jax.experimental.pallas import tpu as pltpu
from jax.sharding import PartitionSpec as P

SPECIES = 4
STEPS = 4
EARLIER = 8
SHIFTS = (6.0, 9.0, 14.0, 17.0)
DAMPING = 0.2
AXES = ("gx", "gy", "gz")

VECTORS = EARLIER + STEPS
SLOT = {}
for _b in range(VECTORS):
    for _a in range(_b + 1):
        SLOT[(_a, _b)] = len(SLOT)

WIDE = 2
DEEP = 4
ROWS = 24
V_PLANES = tuple(range(-WIDE, 4 + WIDE))
R_PLANES = tuple(range(-1, 5))
V_BASE = 0
D_BASE = SPECIES * len(V_PLANES)
R_BASE = 2 * D_BASE
PLANES = R_BASE + SPECIES * SPECIES * len(R_PLANES)
HALVES = SPECIES // 2
SIDES = 2 * HALVES + HALVES * SPECIES
BLOCKS = SIDES // 2


def v_at(s, x):
    return V_BASE + s * len(V_PLANES) + x + WIDE


def d_at(s, x):
    return D_BASE + s * len(V_PLANES) + x + WIDE


def r_at(s, t, x):
    return R_BASE + (s * SPECIES + t) * len(R_PLANES) + x + 1


def iota(shape, dim):
    return lax.broadcasted_iota(jnp.int32, shape, dim)


def roll(value, shift, axis):
    shift %= value.shape[axis]
    return pltpu.roll(value, shift, axis) if shift else value


def x_faces(q_ref, d_ref, r_ref, low_ref, high_ref, v_out, d_out, sems):
    copies = []
    for face, planes, plane in ((low_ref, pl.ds(0, WIDE), 0), (high_ref, pl.ds(4 - WIDE, WIDE), 3)):
        for n, source in enumerate((q_ref.at[EARLIER - 1, :, planes], d_ref.at[:, planes])):
            target = face.at[pl.ds(n * SPECIES * WIDE, SPECIES * WIDE)]
            copies.append((source, target.reshape((SPECIES, WIDE) + face.shape[1:])))
        target = face.at[pl.ds(2 * SPECIES * WIDE, SPECIES * SPECIES)]
        copies.append((r_ref.at[:, :, plane], target.reshape((SPECIES, SPECIES) + face.shape[1:])))
    copies += [(q_ref.at[EARLIER - 1], v_out), (d_ref, d_out)]
    started = [pltpu.make_async_copy(a, b, sems.at[n]) for n, (a, b) in enumerate(copies)]
    for copy in started:
        copy.start()
    for copy in started:
        copy.wait()


def own_planes(v_ref, d_ref, r_ref, before_ref, after_ref):
    def pick(own, slot, width, x):
        if x < 0:
            return lambda rows: before_ref[slot + x + width, rows]
        if x > 3:
            return lambda rows: after_ref[slot + x - 4, rows]
        return lambda rows: own(x, rows)

    planes = []
    for s in range(SPECIES):
        for x in V_PLANES:
            planes.append(pick(lambda x, rows, s=s: v_ref[s, x, rows], s * WIDE, WIDE, x))
    for s in range(SPECIES):
        for x in V_PLANES:
            planes.append(pick(lambda x, rows, s=s: d_ref[s, x, rows], (SPECIES + s) * WIDE, WIDE, x))
    for s in range(SPECIES):
        for t in range(SPECIES):
            slot = 2 * SPECIES * WIDE + s * SPECIES + t
            for x in R_PLANES:
                planes.append(pick(lambda x, rows, s=s, t=t: r_ref[s, t, x, rows], slot, 1, x))
    return planes


def y_places():
    places, used = {}, [0, 0]

    def put(message, planes, rows):
        per = 8 // rows
        for n, plane in enumerate(planes):
            places[plane] = (message, used[message] + n // per, n % per, rows)
        used[message] += len(planes) // per

    near, far, own = [], [], []
    for base in (v_at, d_at):
        for s in range(SPECIES):
            for x in V_PLANES:
                (own if 0 <= x < 4 else near if -1 <= x < 5 else far).append(base(s, x))
    for s in range(SPECIES):
        for t in range(SPECIES):
            for x in R_PLANES:
                (own if 0 <= x < 4 else far).append(r_at(s, t, x))
    put(0, own, DEEP)
    put(1, near, DEEP)
    put(1, far, 2)
    return places, used


Y_PLACES, Y_TILES = y_places()


def y_faces(message, planes, low_ref, high_ref):
    row = iota((8, 128), 0)
    low, high = [None] * Y_TILES[message], [None] * Y_TILES[message]
    for plane, (number, tile, place, rows) in Y_PLACES.items():
        if number != message:
            continue
        first = roll(planes[plane](pl.ds(0, 8)), rows * place, 0)
        final = roll(planes[plane](pl.ds(8, 8)), rows * place + rows, 0)
        here = row // rows == place
        low[tile] = first if low[tile] is None else jnp.where(here, first, low[tile])
        high[tile] = final if high[tile] is None else jnp.where(here, final, high[tile])
    for tile in range(Y_TILES[message]):
        low_ref[tile] = low[tile]
        high_ref[tile] = high[tile]


def own_faces(v_ref, d_ref, r_ref, y_low, y_high, z_low, z_high):
    planes = own_planes(v_ref, d_ref, r_ref, None, None)
    y_faces(0, planes, y_low, y_high)
    for block, found in enumerate(z_groups(True)):
        z_low[block], z_high[block] = pack_z(found, lambda plane: planes[plane](pl.ds(0, 16)), 16)


def more_y_faces(before_ref, after_ref, low_ref, high_ref):
    y_faces(1, own_planes(None, None, None, before_ref, after_ref), low_ref, high_ref)


def side_planes(side):
    found = []
    for half in range(2):
        for x in V_PLANES:
            if side < 2 * HALVES:
                s = side % HALVES * 2 + half
                found.append(v_at(s, x) if side < HALVES else d_at(s, x))
            else:
                pair, t = divmod(side - 2 * HALVES, SPECIES)
                found.append(r_at(2 * pair + half, t, x) if x in R_PLANES else None)
    return found


def z_groups(own):
    blocks = [[] for _ in range(SIDES // 4)]
    for side in range(SIDES):
        for slot, plane in enumerate(side_planes(side)):
            if plane is not None and own == (WIDE <= slot % 8 < WIDE + 4):
                group = (2 * slot + 8 * (side % 4 // 2) + side % 2) % 32
                blocks[side // 4].append((plane, group))
    return blocks


def z_edge_groups():
    blocks = [[] for _ in range(BLOCKS)]
    for side in range(SIDES):
        for slot, plane in enumerate(side_planes(side)):
            if plane is not None:
                blocks[side // 2].append((plane, 2 * slot + side % 2))
    return blocks


def pack_z(planes, value_of, rows):
    group = iota((rows, 128), 1) // DEEP
    low = high = jnp.zeros((rows, 128), jnp.float32)
    for plane, k in planes:
        value = value_of(plane)
        low = jnp.where(group == k, roll(value, DEEP * k, 1), low)
        high = jnp.where(group == k, roll(value, DEEP * k + DEEP, 1), high)
    return low, high


def is_own(plane):
    return Y_PLACES[plane][0] == 0


def y_edge(plane, before_ref, after_ref):
    _, tile, place, rows = Y_PLACES[plane]
    after = roll(after_ref[tile], -rows * place, 0)
    return jnp.where(iota((8, 128), 0) < DEEP, after, roll(before_ref[tile], 8 - rows - rows * place, 0))


def some_z_faces(x_before, x_after, y_before, y_after, edge_ref, low_ref, high_ref):
    planes = own_planes(None, None, None, x_before, x_after)
    for block, found in enumerate(z_groups(False)):
        low, high = pack_z(found, lambda plane: planes[plane](pl.ds(0, 16)), 16)
        for half in range(2):
            low_ref[2 * block + half] = low[8 * half : 8 * half + 8]
            high_ref[2 * block + half] = high[8 * half : 8 * half + 8]

    def value_of(plane):
        edge_ref[plane] = y_edge(plane, y_before, y_after)
        return edge_ref[plane]

    for block, found in enumerate(z_edge_groups()):
        found = [(plane, k) for plane, k in found if is_own(plane)]
        low_ref[BLOCKS + block], high_ref[BLOCKS + block] = pack_z(found, value_of, 8)


def more_z_faces(y_before, y_after, some_low, some_high, edge_ref, low_ref, high_ref):
    def value_of(plane):
        edge_ref[plane] = y_edge(plane, y_before, y_after)
        return edge_ref[plane]

    for block, found in enumerate(z_edge_groups()):
        low_ref[block], high_ref[block] = some_low[block], some_high[block]
        found = [(plane, k) for plane, k in found if not is_own(plane)]
        low, high = pack_z(found, value_of, 8)
        low_ref[BLOCKS + block] = some_low[BLOCKS + block] + low
        high_ref[BLOCKS + block] = some_high[BLOCKS + block] + high


def unpack_z(side, own_before, own_after, more_before, more_after):
    lane = iota((16, 128), 1)
    block, turned, part = side // 4, side % 4 // 2, side % 2
    own = (lane // 8 % 8 >= WIDE) & (lane // 8 % 8 < WIDE + 4)
    if turned:
        own = ~own

    def rows(own_ref, more_ref):
        more = jnp.concatenate([more_ref[2 * block], more_ref[2 * block + 1]], 0)
        return jnp.where(own, own_ref[block], more)

    def join(before, after, shift):
        early = iota(before.shape, 1) % 8 < DEEP
        return jnp.where(early, roll(before, -shift - DEEP * part, 1), roll(after, DEEP - shift - DEEP * part, 1))

    main = join(rows(own_before, more_before), rows(own_after, more_after), 32 * turned)
    edge = join(more_before[BLOCKS + side // 2], more_after[BLOCKS + side // 2], 0)
    return jnp.concatenate([main, edge], 0)


class Planes:
    def __init__(self, planes, edge_own, edge_more):
        self.planes, self.edge_own, self.edge_more = planes, edge_own, edge_more

    def __getitem__(self, plane):
        edge_ref = self.edge_own if is_own(plane) else self.edge_more
        return jnp.concatenate([self.planes[plane](pl.ds(0, 16)), edge_ref[plane]], 0)


def masks():
    first = {axis: lax.axis_index(axis) == 0 for axis in AXES}
    final = {axis: lax.axis_index(axis) == lax.axis_size(axis) - 1 for axis in AXES}

    def keep(flag):
        return jnp.where(flag, 0.0, 1.0).astype(jnp.float32)

    row, lane = iota((ROWS, 128), 0), iota((ROWS, 128), 1)
    main = jnp.where(row < 16, 1.0, jnp.where(row < 16 + DEEP, keep(final["gy"]), keep(first["gy"])))
    slot = lane // 8 % 8
    side = main * jnp.where(lane % 8 < DEEP, keep(first["gz"]), keep(final["gz"]))
    before, after = keep(first["gx"]), keep(final["gx"])
    side = side * jnp.where(slot < WIDE, before, jnp.where(slot < WIDE + 4, 1.0, after))
    return main, side, before, after


def mask_of(x, main, before, after):
    if 0 <= x < 4:
        return main
    return main * (before if x < 0 else after)


def next_y(value):
    return roll(value, -1, 0)


def slot_of(s, x):
    return 64 * (s % 2) + 8 * (x + WIDE)


def columns(planes, value_of):
    group = iota((ROWS, 128), 1) // 8
    found = []
    for half in range(HALVES):
        value = jnp.zeros((ROWS, 128), jnp.float32)
        for s in (2 * half, 2 * half + 1):
            for x in planes:
                place = slot_of(s, x)
                value = jnp.where(group == place // 8, roll(value_of(s, x), place + DEEP, 1), value)
        found.append(value)
    return found


def next_z(value, side, place):
    lane = iota((ROWS, 128), 1)
    return jnp.where(lane == 127, roll(side, 127 - place - DEEP, 1), roll(value, -1, 1))


def previous_z(value, side, place):
    lane = iota((ROWS, 128), 1)
    return jnp.where(lane == 0, roll(side, -(place + DEEP - 1), 1), roll(value, 1, 1))


def side_next_z(side, edge):
    return roll(jnp.where(iota((ROWS, 128), 1) % 8 == DEEP, edge, side), -1, 1)


def side_previous_z(side, edge):
    return roll(jnp.where(iota((ROWS, 128), 1) % 8 == DEEP - 1, edge, side), 1, 1)


def cx_at(s, x):
    return s * 7 + x + 2


def cy_at(s, x):
    return SPECIES * 7 + s * 6 + x + 1


def cz_at(s, x):
    return SPECIES * 13 + s * 6 + x + 1


def back_at(s, x):
    return SPECIES * 19 + s * 6 + x + 1


CONDUCTS = SPECIES * 25


WITHOUT_Z = SPECIES * 13


class Conducts:
    def __init__(self, plain_ref, z_ref):
        self.plain_ref, self.z_ref = plain_ref, z_ref

    def __getitem__(self, k):
        return self.plain_ref[k] if k < WITHOUT_Z else self.z_ref[k - WITHOUT_Z]


def early_steps(v_ref, d_ref, r_ref, x_before, x_after, edge_own, edge_more, v_in, d_in, c_ref, sum_ref, d_edge, v_edge):
    main_ref = Planes(own_planes(v_ref, d_ref, r_ref, x_before, x_after), edge_own, edge_more)
    mask = masks()
    for s in range(SPECIES):
        for x in V_PLANES:
            factor = mask_of(x, mask[0], *mask[2:])
            v_in[v_at(s, x)] = main_ref[v_at(s, x)] * factor
            d_in[v_at(s, x)] = main_ref[d_at(s, x)] * factor
    lane = iota((ROWS, 128), 1)
    first, final = lane == 0, lane == 127
    for s in range(SPECIES):
        for x in V_PLANES:
            d = d_in[v_at(s, x)]
            if x < V_PLANES[-1]:
                c_ref[cx_at(s, x)] = 0.5 * (d + d_in[v_at(s, x + 1)])
            if x in R_PLANES:
                c_ref[cy_at(s, x)] = 0.5 * (d + next_y(d))
                c_ref[cz_at(s, x)] = jnp.where(final, 0.0, 0.5 * (d + roll(d, -1, 1)))
                c_ref[back_at(s, x)] = jnp.where(first, 0.0, 0.5 * (d + roll(d, 1, 1)))
    for x in R_PLANES:
        here = [v_in[v_at(t, x)] for t in range(SPECIES)]
        for s in range(SPECIES):
            v = here[s]
            value = v * (1.0 - SHIFTS[0])
            value = value + c_ref[cz_at(s, x)] * (v - roll(v, -1, 1))
            value = value + c_ref[back_at(s, x)] * (v - roll(v, 1, 1))
            for t in range(SPECIES):
                value = value + main_ref[r_at(s, t, x)] * here[t]
            value = value + c_ref[cx_at(s, x)] * (v - v_in[v_at(s, x + 1)])
            value = value + c_ref[cx_at(s, x - 1)] * (v - v_in[v_at(s, x - 1)])
            along = c_ref[cy_at(s, x)] * (v - next_y(v))
            sum_ref[6 * s + x + 1] = value + (along - roll(along, 1, 0))
    for half, (d, v) in enumerate(
        zip(columns(R_PLANES, lambda s, x: d_in[v_at(s, x)]), columns(R_PLANES, lambda s, x: v_in[v_at(s, x)]))
    ):
        d_edge[half] = d
        v_edge[half] = v


def end_first_step(v_in, d_in, c_ref, sum_ref, d_side, v_side, z_ref, mask, store):
    lane = iota((ROWS, 128), 1)
    first, final = lane == 0, lane == 127
    for s in range(SPECIES):
        for x in R_PLANES:
            place, half, n = slot_of(s, x), s // 2, 6 * s + x + 1

            def beyond(side, place=place, half=half):
                return jnp.where(final, roll(side[half], 127 - place - DEEP, 1), roll(side[half], 1 - DEEP - place, 1))

            more = jnp.where(first | final, 0.5 * (d_in[v_at(s, x)] + beyond(d_side)), 0.0)
            z_ref[cz_at(s, x) - WITHOUT_Z] = jnp.where(final, more, c_ref[cz_at(s, x)])
            z_ref[back_at(s, x) - WITHOUT_Z] = jnp.where(first, more, c_ref[back_at(s, x)])
            value = sum_ref[n] + more * (v_in[v_at(s, x)] - beyond(v_side))
            store(s, x, value * (DAMPING * mask_of(x, mask[0], *mask[2:])))


def side_conduct(d_side, edges, c_side):
    for half in range(HALVES):
        d = d_side[half]
        c_side[4 * half] = 0.5 * (d + roll(d, -8, 1))
        c_side[4 * half + 1] = 0.5 * (d + next_y(d))
        c_side[4 * half + 2] = 0.5 * (d + side_next_z(d, edges[half]))
        c_side[4 * half + 3] = 0.5 * (d + side_previous_z(d, edges[half]))


def plane_sum(degree, s, x, v_of, v_side, main_ref, c_ref, before=True, after=True):
    half, place, v = s // 2, slot_of(s, x), v_of(s, x)
    value = v * (1.0 - SHIFTS[degree])
    value = value + c_ref[cz_at(s, x)] * (v - next_z(v, v_side[half], place))
    value = value + c_ref[back_at(s, x)] * (v - previous_z(v, v_side[half], place))
    for t in range(SPECIES):
        value = value + main_ref[r_at(s, t, x)] * v_of(t, x)
    if after:
        value = value + c_ref[cx_at(s, x)] * (v - v_of(s, x + 1))
    if before:
        value = value + c_ref[cx_at(s, x - 1)] * (v - v_of(s, x - 1))
    along = c_ref[cy_at(s, x)] * (v - next_y(v))
    return value + (along - roll(along, 1, 0))


def step(degree, planes, v_of, v_side, main_ref, side_ref, c_ref, c_side, mask, store, sides=True):
    for x in planes:
        factor = DAMPING * mask_of(x, mask[0], *mask[2:])
        for s in range(SPECIES):
            store(s, x, plane_sum(degree, s, x, v_of, v_side, main_ref, c_ref) * factor)
    if not sides:
        return None
    return side_step(degree, columns(planes, v_of), v_side, side_ref, c_side, mask)


def side_step(degree, edges, v_side, side_ref, c_side, mask):
    lane = iota((ROWS, 128), 1)
    both = []
    for half in range(HALVES):
        other = roll(v_side[half], 64, 1)
        both.append(jnp.where(lane < 64, v_side[half], other))
        both.append(jnp.where(lane < 64, other, v_side[half]))
    result = []
    for half in range(HALVES):
        v = v_side[half]
        value = v * (1.0 - SHIFTS[degree])
        value = value + c_side[4 * half + 2] * (v - side_next_z(v, edges[half]))
        value = value + c_side[4 * half + 3] * (v - side_previous_z(v, edges[half]))
        for t in range(SPECIES):
            value = value + side_ref[2 * HALVES + SPECIES * half + t] * both[t]
        across = c_side[4 * half] * (v - roll(v, -8, 1))
        value = value + (across - roll(across, 8, 1))
        along = c_side[4 * half + 1] * (v - next_y(v))
        value = value + (along - roll(along, 1, 0))
        result.append(value * (DAMPING * mask[1]))
    return result


FACE_EDGES = SPECIES * WIDE * 2
FACE_SIDE = FACE_EDGES + SPECIES
FACE_TILES = FACE_SIDE + 3


def put_own(out_ref, s, x, value):
    out_ref[8 * s + 2 * x] = value[:8]
    out_ref[8 * s + 2 * x + 1] = value[8:16]


def first_steps(r_ref, x_before, x_after, edge_own, edge_more, v_in, d_in, c_early, sum_ref, d_edge, v_edge, own_before, own_after, more_before, more_after, v1_ref, v2_ref, wide_ref, wide_side, low_ref, high_ref, side_ref, z_ref, c_side, v_mid):
    main_ref = Planes(own_planes(None, None, r_ref, x_before, x_after), edge_own, edge_more)
    lane = iota((ROWS, 128), 1)
    for side in range(SIDES):
        side_ref[side] = unpack_z(side, own_before, own_after, more_before, more_after)
    mask = masks()
    v_side = [side_ref[half] * mask[1] for half in range(HALVES)]
    d_side = [side_ref[HALVES + half] * mask[1] for half in range(HALVES)]
    side_conduct(d_side, d_edge, c_side)
    c_ref = Conducts(c_early, z_ref)

    def store_mid(s, x, value):
        v_mid[v_at(s, x)] = value
        if 0 <= x < 4:
            put_own(v1_ref, s, x, value)

    def store_wide(s, x, value):
        wide_ref[4 * s + x] = value
        put_own(v2_ref, s, x, value)

    more = (main_ref, side_ref, c_ref, c_side, mask)
    end_first_step(v_in, d_in, c_early, sum_ref, d_side, v_side, z_ref, mask, store_mid)
    v_side = side_step(0, v_edge, v_side, side_ref, c_side, mask)
    v_side = step(1, range(4), lambda s, x: v_mid[v_at(s, x)], v_side, *more, store_wide)
    for half in range(HALVES):
        wide_side[half] = v_side[half]
    slot = lane // 8 % 8
    row = iota((8, 128), 0)
    near = (row < 2) | (row >= 6)
    for face, start, shift in ((low_ref, 0, -16), (high_ref, 4 - WIDE, 16)):
        for s in range(SPECIES):
            values = [wide_ref[4 * s + start + n] for n in range(WIDE)]
            for n in range(WIDE):
                face[(s * WIDE + n) * 2] = values[n][:8]
                face[(s * WIDE + n) * 2 + 1] = values[n][8:16]
            face[FACE_EDGES + s] = jnp.where(near, values[0][16:], roll(values[1][16:], DEEP, 0))
        kept = (slot >= start + WIDE) & (slot < start + 2 * WIDE)
        packed = jnp.where(kept, v_side[0], roll(v_side[1], shift, 1))
        for n in range(3):
            face[FACE_SIDE + n] = packed[8 * n : 8 * n + 8]


def middle_step(r_ref, x_before, x_after, edge_own, edge_more, c_early, z_ref, wide_ref, wide_side, sum_ref, v_edge):
    main_ref = Planes(own_planes(None, None, r_ref, x_before, x_after), edge_own, edge_more)
    c_ref = Conducts(c_early, z_ref)

    def v_of(s, x):
        return wide_ref[4 * s + x]

    for x in range(4):
        for s in range(SPECIES):
            sum_ref[4 * s + x] = plane_sum(2, s, x, v_of, wide_side, main_ref, c_ref, x > 0, x < 3)
    for half, value in enumerate(columns(range(4), v_of)):
        v_edge[half] = value


def last_steps(r_ref, x_before, x_after, edge_own, edge_more, side_ref, c_early, z_ref, c_side, wide_ref, wide_side, sum_ref, v_edge, before_ref, after_ref, q_ref, v1_ref, v2_ref, sums_in, v3_ref, v4_ref, sums_ref, v_in, v_mid):
    main_ref = Planes(own_planes(None, None, r_ref, x_before, x_after), edge_own, edge_more)
    c_ref = Conducts(c_early, z_ref)
    mask = masks()
    for s in range(SPECIES):
        for face, start, factor in ((before_ref, -WIDE, mask[2]), (after_ref, 4, mask[3])):
            for n in range(WIDE):
                k = (s * WIDE + n) * 2
                value = jnp.concatenate([face[k], face[k + 1], roll(face[FACE_EDGES + s], DEEP * n, 0)], 0)
                v_in[v_at(s, start + n)] = value * factor
    slot = iota((ROWS, 128), 1) // 8 % 8
    before, after = (
        jnp.concatenate([face[FACE_SIDE + n] for n in range(3)], 0) * factor
        for face, factor in ((before_ref, mask[2]), (after_ref, mask[3]))
    )
    v_side = []
    for half in range(HALVES):
        value = jnp.where(slot < WIDE, roll(before, -32 - 16 * half, 1), wide_side[half])
        v_side.append(jnp.where(slot >= WIDE + 4, roll(after, 32 + 16 * half, 1), value))

    def first(s, x):
        return wide_ref[4 * s + x] if 0 <= x < 4 else v_in[v_at(s, x)]

    def store_mid(s, x, value):
        v_mid[v_at(s, x)] = value
        if 0 <= x < 4:
            put_own(v3_ref, s, x, value)

    def store_last(s, x, value):
        put_own(v4_ref, s, x, value)

    more = (main_ref, side_ref, c_ref, c_side, mask)
    for x in R_PLANES:
        factor = DAMPING * mask_of(x, mask[0], *mask[2:])
        for s in range(SPECIES):
            if 0 <= x < 4:
                value = sum_ref[4 * s + x]
                if x == 0:
                    value = value + c_ref[cx_at(s, -1)] * (first(s, 0) - first(s, -1))
                if x == 3:
                    value = value + c_ref[cx_at(s, 3)] * (first(s, 3) - first(s, 4))
            else:
                value = plane_sum(2, s, x, first, v_side, main_ref, c_ref)
            store_mid(s, x, value * factor)
    edges = [v_edge[half] + more for half, more in enumerate(columns((-1, 4), first))]
    v_side = side_step(2, edges, v_side, side_ref, c_side, mask)
    step(3, range(4), lambda s, x: v_mid[v_at(s, x)], v_side, *more, store_last, sides=False)

    def load(i):
        return [q_ref[a, i] for a in range(EARLIER)] + [v1_ref[i], v2_ref[i], v3_ref[i], v4_ref[i]]

    row = sums_in[...] + products(new_pairs(2) + new_pairs(3), load, q_ref.shape[1])
    sums_ref[...] = jnp.broadcast_to(jnp.sum(row, 0, keepdims=True), sums_ref.shape)


def middle_products(q_ref, v1_ref, v2_ref, before_ref, out_ref):
    def load(i):
        return [q_ref[a, i] for a in range(EARLIER)] + [v1_ref[i], v2_ref[i]]

    out_ref[...] = before_ref[...] + products(new_pairs(0) + new_pairs(1), load, q_ref.shape[1])


def products(pairs, load, count):
    def body(i, sums):
        values = load(i)
        return tuple(total + values[a] * values[b] for total, (a, b) in zip(sums, pairs))

    zero = jnp.zeros((8, 128), jnp.float32)
    sums = lax.fori_loop(0, count, body, (zero,) * len(pairs))
    lane = lax.broadcasted_iota(jnp.int32, (8, 128), 1)
    row = zero
    for total, pair in zip(sums, pairs):
        row = jnp.where(lane == SLOT[pair], jnp.sum(total, 1, keepdims=True), row)
    return row


def earlier_products(q_ref, out_ref):
    pairs = [(a, b) for b in range(EARLIER) for a in range(b + 1)]
    out_ref[...] = products(pairs, lambda i: [q_ref[a, i] for a in range(EARLIER)], q_ref.shape[1])


def new_pairs(number):
    return [(a, EARLIER + number) for a in range(EARLIER + number + 1)]


def finish_kernel(entries, sums_ref, q_ref, *refs):
    v_refs, (new_ref, coeff_ref, triangle_ref) = refs[:STEPS], refs[STEPS:]
    total = sums_ref[0]
    for i in range(1, sums_ref.shape[0]):
        total = total + sums_ref[i]
    total = jnp.broadcast_to(jnp.sum(total, 0, keepdims=True), total.shape) * (1.0 / entries)

    def entry(a, b):
        k = SLOT[(min(a, b), max(a, b))]
        return jnp.broadcast_to(total[:, k : k + 1], total.shape)

    coeff = [[entry(i, EARLIER + j) for j in range(STEPS)] for i in range(EARLIER)]
    overlap = {(a, b): entry(a, b) for b in range(EARLIER) for a in range(b + 1)}
    gram = {}
    for k in range(STEPS):
        mixed = []
        for i in range(EARLIER):
            term = -2.0 * coeff[i][k]
            for m in range(EARLIER):
                term = term + overlap[(min(i, m), max(i, m))] * coeff[m][k]
            mixed.append(term)
        for j in range(k, STEPS):
            value = entry(EARLIER + k, EARLIER + j)
            for i in range(EARLIER):
                value = value + coeff[i][j] * mixed[i]
            gram[(j, k)] = value
    factor, inverse = {}, []
    for k in range(STEPS):
        pivot = gram[(k, k)]
        for m in range(k):
            pivot = pivot - factor[(k, m)] * factor[(k, m)]
        factor[(k, k)] = jnp.sqrt(pivot)
        inverse.append(1.0 / factor[(k, k)])
        for j in range(k + 1, STEPS):
            value = gram[(j, k)]
            for m in range(k):
                value = value - factor[(j, m)] * factor[(k, m)]
            factor[(j, k)] = value * inverse[k]
    row = lax.broadcasted_iota(jnp.int32, total.shape, 0)
    lane = lax.broadcasted_iota(jnp.int32, total.shape, 1)
    table = jnp.zeros_like(total)
    for i in range(EARLIER):
        for j in range(STEPS):
            table = jnp.where((row == j) & (lane == i), coeff[i][j], table)
    coeff_ref[...] = table[:STEPS, :EARLIER]
    table = jnp.zeros_like(total)
    for (j, k), value in factor.items():
        table = jnp.where((row == k) & (lane == j), value, table)
    triangle_ref[...] = table[:STEPS, :STEPS]

    def body(n, carry):
        earlier = [q_ref[i, n] for i in range(EARLIER)]
        done = []
        for j in range(STEPS):
            value = v_refs[j][n]
            for i in range(EARLIER):
                value = value - coeff[i][j] * earlier[i]
            for k in range(j):
                value = value - factor[(j, k)] * done[k]
            done.append(value * inverse[j])
            new_ref[j, n] = done[j]
        return carry

    lax.fori_loop(0, q_ref.shape[1], body, 0)


def call(body, outs, cost, *args, **more):
    return pl.pallas_call(
        body,
        out_shape=[jax.ShapeDtypeStruct(shape, jnp.float32) for shape in outs],
        cost_estimate=pl.CostEstimate(flops=cost, bytes_accessed=cost, transcendentals=0),
        compiler_params=pltpu.CompilerParams(vmem_limit_bytes=24 << 20),
        **more,
    )(*args)


def shifts(axis):
    count = lax.axis_size(axis)
    up = [(i, (i + 1) % count) for i in range(count)]
    return up, [(target, source) for source, target in up]


def exchange(axis, low, high):
    up, down = shifts(axis)
    return lax.ppermute(high, axis, up), lax.ppermute(low, axis, down)


def on_device(earlier_basis, diffusivity, reaction):
    span_x, span_y, span_z = diffusivity.shape[1:]
    tiles = SPECIES * span_x * span_y // 8
    devices = 1
    for axis in AXES:
        devices *= lax.axis_size(axis)
    entries = tiles * 8 * span_z * devices
    in_hbm = pl.BlockSpec(memory_space=pltpu.HBM)
    given = (earlier_basis, diffusivity, reaction)
    face = (2 * SPECIES * WIDE + SPECIES * SPECIES, span_y, span_z)
    field = diffusivity.shape
    low, high, *kept = call(
        x_faces,
        [face, face, field, field],
        1 << 20,
        *[pltpu.with_memory_space_constraint(a, pltpu.HBM) for a in given],
        in_specs=[in_hbm] * 3,
        scratch_shapes=[pltpu.SemaphoreType.DMA((8,))],
    )
    x_halos = exchange("gx", low, high)
    kept.append(reaction)
    face = (Y_TILES[0], 8, span_z)
    z_face = (SIDES // 4, 16, span_z)
    own = call(own_faces, [face, face, z_face, z_face], 1 << 20, *kept)
    y_own = exchange("gy", *own[:2])
    up, down = shifts("gz")
    z_before = lax.ppermute(own[3], "gz", up)
    z_after = lax.ppermute(own[2], "gz", down)
    z_own = (z_before, z_after)
    face = (Y_TILES[1], 8, span_z)
    faces = call(more_y_faces, [face, face], 1 << 20, *x_halos)
    y_more = exchange("gy", *faces)
    face = (2 * BLOCKS, 8, span_z)
    edges = (PLANES, 8, span_z)
    edge_own, low, high = call(some_z_faces, [edges, face, face], 1 << 20, *x_halos, *y_own)
    edge_more, low, high = call(more_z_faces, [edges, face, face], 1 << 20, *y_more, low, high)
    edge = (edge_own, edge_more)
    z_more = exchange("gz", low, high)
    basis = earlier_basis.reshape(EARLIER, tiles, 8, span_z)
    (sums,) = call(earlier_products, [(8, span_z)], 4 << 20, basis)
    own = (tiles, 8, span_z)
    plane = (ROWS, span_z)
    early = call(
        early_steps,
        [(count,) + plane for count in (D_BASE, D_BASE, CONDUCTS, SPECIES * len(R_PLANES), HALVES, HALVES)],
        1 << 20,
        *kept,
        *x_halos,
        *edge,
    )
    scratch = [pltpu.VMEM((D_BASE,) + plane, jnp.float32)]
    face = (FACE_TILES, 8, span_z)
    several = [(count,) + plane for count in (SPECIES * span_x, HALVES)] + [face, face]
    several += [(count,) + plane for count in (SIDES, CONDUCTS - WITHOUT_Z, 4 * HALVES)]
    v1, v2, wide, wide_side, low, high, side, z_conducts, side_conducts = call(
        first_steps,
        [own, own] + several,
        1 << 20,
        reaction,
        *x_halos,
        *edge,
        *early,
        *z_own,
        *z_more,
        scratch_shapes=scratch,
    )
    halos = exchange("gx", low, high)
    (sums,) = call(middle_products, [(8, span_z)], 4 << 20, basis, v1, v2, sums)
    plane_sums = call(
        middle_step,
        [(SPECIES * span_x,) + plane, (HALVES,) + plane],
        1 << 20,
        reaction,
        *x_halos,
        *edge,
        early[2],
        z_conducts,
        wide,
        wide_side,
    )
    v3, v4, rows = call(
        last_steps,
        [own, own, (devices, span_z)],
        1 << 20,
        reaction,
        *x_halos,
        *edge,
        side,
        early[2],
        z_conducts,
        side_conducts,
        wide,
        wide_side,
        *plane_sums,
        *halos,
        basis,
        v1,
        v2,
        sums,
        scratch_shapes=scratch * 2,
    )
    rows = lax.all_to_all(rows.reshape(devices, 1, span_z), AXES, 0, 0)
    new, coeff, triangle = call(
        functools.partial(finish_kernel, entries),
        [(STEPS, tiles, 8, span_z), (STEPS, EARLIER), (STEPS, STEPS)],
        1 << 20,
        rows.reshape(devices // 8, 8, span_z),
        basis,
        v1,
        v2,
        v3,
        v4,
    )
    return new.reshape((STEPS, SPECIES, span_x, span_y, span_z)), coeff.T, triangle


def solution(mesh):
    in_specs = (
        P(None, None, "gx", "gy", "gz"),
        P(None, "gx", "gy", "gz"),
        P(None, None, "gx", "gy", "gz"),
    )
    out_specs = (P(None, None, "gx", "gy", "gz"), P(), P())
    return jax.shard_map(
        on_device, mesh=mesh, in_specs=in_specs, out_specs=out_specs, check_vma=False
    )
```

```python
import functools

import jax
import jax.numpy as jnp
from jax import lax
from jax.experimental import pallas as pl
from jax.experimental.pallas import tpu as pltpu
from jax.sharding import PartitionSpec as P

SPECIES = 4
STEPS = 4
EARLIER = 8
SHIFTS = (6.0, 9.0, 14.0, 17.0)
DAMPING = 0.2
AXES = ("gx", "gy", "gz")

VECTORS = EARLIER + STEPS
SLOT = {}
for _b in range(VECTORS):
    for _a in range(_b + 1):
        SLOT[(_a, _b)] = len(SLOT)

WIDE = 2
DEEP = 4
ROWS = 24
V_PLANES = tuple(range(-WIDE, 4 + WIDE))
R_PLANES = tuple(range(-1, 5))
V_BASE = 0
D_BASE = SPECIES * len(V_PLANES)
R_BASE = 2 * D_BASE
PLANES = R_BASE + SPECIES * SPECIES * len(R_PLANES)
HALVES = SPECIES // 2
SIDES = 2 * HALVES + HALVES * SPECIES
BLOCKS = SIDES // 2


def v_at(s, x):
    return V_BASE + s * len(V_PLANES) + x + WIDE


def d_at(s, x):
    return D_BASE + s * len(V_PLANES) + x + WIDE


def r_at(s, t, x):
    return R_BASE + (s * SPECIES + t) * len(R_PLANES) + x + 1


def iota(shape, dim):
    return lax.broadcasted_iota(jnp.int32, shape, dim)


def roll(value, shift, axis):
    shift %= value.shape[axis]
    return pltpu.roll(value, shift, axis) if shift else value


def x_faces(q_ref, d_ref, r_ref, low_ref, high_ref, v_out, d_out, sems):
    copies = []
    for face, planes, plane in ((low_ref, pl.ds(0, WIDE), 0), (high_ref, pl.ds(4 - WIDE, WIDE), 3)):
        for n, source in enumerate((q_ref.at[EARLIER - 1, :, planes], d_ref.at[:, planes])):
            target = face.at[pl.ds(n * SPECIES * WIDE, SPECIES * WIDE)]
            copies.append((source, target.reshape((SPECIES, WIDE) + face.shape[1:])))
        target = face.at[pl.ds(2 * SPECIES * WIDE, SPECIES * SPECIES)]
        copies.append((r_ref.at[:, :, plane], target.reshape((SPECIES, SPECIES) + face.shape[1:])))
    copies += [(q_ref.at[EARLIER - 1], v_out), (d_ref, d_out)]
    started = [pltpu.make_async_copy(a, b, sems.at[n]) for n, (a, b) in enumerate(copies)]
    for copy in started:
        copy.start()
    for copy in started:
        copy.wait()


def own_planes(v_ref, d_ref, r_ref, before_ref, after_ref):
    def pick(own, slot, width, x):
        if x < 0:
            return lambda rows: before_ref[slot + x + width, rows]
        if x > 3:
            return lambda rows: after_ref[slot + x - 4, rows]
        return lambda rows: own(x, rows)

    planes = []
    for s in range(SPECIES):
        for x in V_PLANES:
            planes.append(pick(lambda x, rows, s=s: v_ref[s, x, rows], s * WIDE, WIDE, x))
    for s in range(SPECIES):
        for x in V_PLANES:
            planes.append(pick(lambda x, rows, s=s: d_ref[s, x, rows], (SPECIES + s) * WIDE, WIDE, x))
    for s in range(SPECIES):
        for t in range(SPECIES):
            slot = 2 * SPECIES * WIDE + s * SPECIES + t
            for x in R_PLANES:
                planes.append(pick(lambda x, rows, s=s, t=t: r_ref[s, t, x, rows], slot, 1, x))
    return planes


def y_places():
    places, used = {}, [0, 0]

    def put(message, planes, rows):
        per = 8 // rows
        for n, plane in enumerate(planes):
            places[plane] = (message, used[message] + n // per, n % per, rows)
        used[message] += len(planes) // per

    near, far, own = [], [], []
    for base in (v_at, d_at):
        for s in range(SPECIES):
            for x in V_PLANES:
                (own if 0 <= x < 4 else near if -1 <= x < 5 else far).append(base(s, x))
    for s in range(SPECIES):
        for t in range(SPECIES):
            for x in R_PLANES:
                (own if 0 <= x < 4 else far).append(r_at(s, t, x))
    put(0, own, DEEP)
    put(1, near, DEEP)
    put(1, far, 2)
    return places, used


Y_PLACES, Y_TILES = y_places()


def y_faces(message, planes, low_ref, high_ref):
    row = iota((8, 128), 0)
    low, high = [None] * Y_TILES[message], [None] * Y_TILES[message]
    for plane, (number, tile, place, rows) in Y_PLACES.items():
        if number != message:
            continue
        first = roll(planes[plane](pl.ds(0, 8)), rows * place, 0)
        final = roll(planes[plane](pl.ds(8, 8)), rows * place + rows, 0)
        here = row // rows == place
        low[tile] = first if low[tile] is None else jnp.where(here, first, low[tile])
        high[tile] = final if high[tile] is None else jnp.where(here, final, high[tile])
    for tile in range(Y_TILES[message]):
        low_ref[tile] = low[tile]
        high_ref[tile] = high[tile]


def own_faces(v_ref, d_ref, r_ref, y_low, y_high, z_low, z_high):
    planes = own_planes(v_ref, d_ref, r_ref, None, None)
    y_faces(0, planes, y_low, y_high)
    for block, found in enumerate(z_groups(True)):
        z_low[block], z_high[block] = pack_z(found, lambda plane: planes[plane](pl.ds(0, 16)), 16)


def more_y_faces(before_ref, after_ref, low_ref, high_ref):
    y_faces(1, own_planes(None, None, None, before_ref, after_ref), low_ref, high_ref)


def side_planes(side):
    found = []
    for half in range(2):
        for x in V_PLANES:
            if side < 2 * HALVES:
                s = side % HALVES * 2 + half
                found.append(v_at(s, x) if side < HALVES else d_at(s, x))
            else:
                pair, t = divmod(side - 2 * HALVES, SPECIES)
                found.append(r_at(2 * pair + half, t, x) if x in R_PLANES else None)
    return found


def z_groups(own):
    blocks = [[] for _ in range(SIDES // 4)]
    for side in range(SIDES):
        for slot, plane in enumerate(side_planes(side)):
            if plane is not None and own == (WIDE <= slot % 8 < WIDE + 4):
                group = (2 * slot + 8 * (side % 4 // 2) + side % 2) % 32
                blocks[side // 4].append((plane, group))
    return blocks


def z_edge_groups():
    blocks = [[] for _ in range(BLOCKS)]
    for side in range(SIDES):
        for slot, plane in enumerate(side_planes(side)):
            if plane is not None:
                blocks[side // 2].append((plane, 2 * slot + side % 2))
    return blocks


def pack_z(planes, value_of, rows):
    group = iota((rows, 128), 1) // DEEP
    low = high = jnp.zeros((rows, 128), jnp.float32)
    for plane, k in planes:
        value = value_of(plane)
        low = jnp.where(group == k, roll(value, DEEP * k, 1), low)
        high = jnp.where(group == k, roll(value, DEEP * k + DEEP, 1), high)
    return low, high


def is_own(plane):
    return Y_PLACES[plane][0] == 0


def y_edge(plane, before_ref, after_ref):
    _, tile, place, rows = Y_PLACES[plane]
    after = roll(after_ref[tile], -rows * place, 0)
    return jnp.where(iota((8, 128), 0) < DEEP, after, roll(before_ref[tile], 8 - rows - rows * place, 0))


def some_z_faces(x_before, x_after, y_before, y_after, edge_ref, low_ref, high_ref):
    planes = own_planes(None, None, None, x_before, x_after)
    for block, found in enumerate(z_groups(False)):
        low, high = pack_z(found, lambda plane: planes[plane](pl.ds(0, 16)), 16)
        for half in range(2):
            low_ref[2 * block + half] = low[8 * half : 8 * half + 8]
            high_ref[2 * block + half] = high[8 * half : 8 * half + 8]

    def value_of(plane):
        edge_ref[plane] = y_edge(plane, y_before, y_after)
        return edge_ref[plane]

    for block, found in enumerate(z_edge_groups()):
        found = [(plane, k) for plane, k in found if is_own(plane)]
        low_ref[BLOCKS + block], high_ref[BLOCKS + block] = pack_z(found, value_of, 8)


def more_z_faces(y_before, y_after, some_low, some_high, edge_ref, low_ref, high_ref):
    def value_of(plane):
        edge_ref[plane] = y_edge(plane, y_before, y_after)
        return edge_ref[plane]

    for block, found in enumerate(z_edge_groups()):
        low_ref[block], high_ref[block] = some_low[block], some_high[block]
        found = [(plane, k) for plane, k in found if not is_own(plane)]
        low, high = pack_z(found, value_of, 8)
        low_ref[BLOCKS + block] = some_low[BLOCKS + block] + low
        high_ref[BLOCKS + block] = some_high[BLOCKS + block] + high


def unpack_z(side, own_before, own_after, more_before, more_after):
    lane = iota((16, 128), 1)
    block, turned, part = side // 4, side % 4 // 2, side % 2
    own = (lane // 8 % 8 >= WIDE) & (lane // 8 % 8 < WIDE + 4)
    if turned:
        own = ~own

    def rows(own_ref, more_ref):
        more = jnp.concatenate([more_ref[2 * block], more_ref[2 * block + 1]], 0)
        return jnp.where(own, own_ref[block], more)

    def join(before, after, shift):
        early = iota(before.shape, 1) % 8 < DEEP
        return jnp.where(early, roll(before, -shift - DEEP * part, 1), roll(after, DEEP - shift - DEEP * part, 1))

    main = join(rows(own_before, more_before), rows(own_after, more_after), 32 * turned)
    edge = join(more_before[BLOCKS + side // 2], more_after[BLOCKS + side // 2], 0)
    return jnp.concatenate([main, edge], 0)


class Planes:
    def __init__(self, planes, edge_own, edge_more):
        self.planes, self.edge_own, self.edge_more = planes, edge_own, edge_more

    def __getitem__(self, plane):
        edge_ref = self.edge_own if is_own(plane) else self.edge_more
        return jnp.concatenate([self.planes[plane](pl.ds(0, 16)), edge_ref[plane]], 0)


def masks():
    first = {axis: lax.axis_index(axis) == 0 for axis in AXES}
    final = {axis: lax.axis_index(axis) == lax.axis_size(axis) - 1 for axis in AXES}

    def keep(flag):
        return jnp.where(flag, 0.0, 1.0).astype(jnp.float32)

    row, lane = iota((ROWS, 128), 0), iota((ROWS, 128), 1)
    main = jnp.where(row < 16, 1.0, jnp.where(row < 16 + DEEP, keep(final["gy"]), keep(first["gy"])))
    slot = lane // 8 % 8
    side = main * jnp.where(lane % 8 < DEEP, keep(first["gz"]), keep(final["gz"]))
    before, after = keep(first["gx"]), keep(final["gx"])
    side = side * jnp.where(slot < WIDE, before, jnp.where(slot < WIDE + 4, 1.0, after))
    return main, side, before, after


def mask_of(x, main, before, after):
    if 0 <= x < 4:
        return main
    return main * (before if x < 0 else after)


def next_y(value):
    return roll(value, -1, 0)


def slot_of(s, x):
    return 64 * (s % 2) + 8 * (x + WIDE)


def columns(planes, value_of):
    group = iota((ROWS, 128), 1) // 8
    found = []
    for half in range(HALVES):
        value = jnp.zeros((ROWS, 128), jnp.float32)
        for s in (2 * half, 2 * half + 1):
            for x in planes:
                place = slot_of(s, x)
                value = jnp.where(group == place // 8, roll(value_of(s, x), place + DEEP, 1), value)
        found.append(value)
    return found


def next_z(value, side, place):
    lane = iota((ROWS, 128), 1)
    return jnp.where(lane == 127, roll(side, 127 - place - DEEP, 1), roll(value, -1, 1))


def previous_z(value, side, place):
    lane = iota((ROWS, 128), 1)
    return jnp.where(lane == 0, roll(side, -(place + DEEP - 1), 1), roll(value, 1, 1))


def side_next_z(side, edge):
    return roll(jnp.where(iota((ROWS, 128), 1) % 8 == DEEP, edge, side), -1, 1)


def side_previous_z(side, edge):
    return roll(jnp.where(iota((ROWS, 128), 1) % 8 == DEEP - 1, edge, side), 1, 1)


def cx_at(s, x):
    return s * 7 + x + 2


def cy_at(s, x):
    return SPECIES * 7 + s * 6 + x + 1


def cz_at(s, x):
    return SPECIES * 13 + s * 6 + x + 1


def back_at(s, x):
    return SPECIES * 19 + s * 6 + x + 1


CONDUCTS = SPECIES * 25


WITHOUT_Z = SPECIES * 13


class Conducts:
    def __init__(self, plain_ref, z_ref):
        self.plain_ref, self.z_ref = plain_ref, z_ref

    def __getitem__(self, k):
        return self.plain_ref[k] if k < WITHOUT_Z else self.z_ref[k - WITHOUT_Z]


def early_steps(v_ref, d_ref, r_ref, x_before, x_after, edge_own, edge_more, v_in, d_in, c_ref, sum_ref, d_edge, v_edge):
    main_ref = Planes(own_planes(v_ref, d_ref, r_ref, x_before, x_after), edge_own, edge_more)
    mask = masks()
    for s in range(SPECIES):
        for x in V_PLANES:
            factor = mask_of(x, mask[0], *mask[2:])
            v_in[v_at(s, x)] = main_ref[v_at(s, x)] * factor
            d_in[v_at(s, x)] = main_ref[d_at(s, x)] * factor
    lane = iota((ROWS, 128), 1)
    first, final = lane == 0, lane == 127
    for s in range(SPECIES):
        for x in V_PLANES:
            d = d_in[v_at(s, x)]
            if x < V_PLANES[-1]:
                c_ref[cx_at(s, x)] = 0.5 * (d + d_in[v_at(s, x + 1)])
            if x in R_PLANES:
                c_ref[cy_at(s, x)] = 0.5 * (d + next_y(d))
                c_ref[cz_at(s, x)] = jnp.where(final, 0.0, 0.5 * (d + roll(d, -1, 1)))
                c_ref[back_at(s, x)] = jnp.where(first, 0.0, 0.5 * (d + roll(d, 1, 1)))
    for x in R_PLANES:
        here = [v_in[v_at(t, x)] for t in range(SPECIES)]
        for s in range(SPECIES):
            v = here[s]
            value = v * (1.0 - SHIFTS[0])
            value = value + c_ref[cz_at(s, x)] * (v - roll(v, -1, 1))
            value = value + c_ref[back_at(s, x)] * (v - roll(v, 1, 1))
            for t in range(SPECIES):
                value = value + main_ref[r_at(s, t, x)] * here[t]
            value = value + c_ref[cx_at(s, x)] * (v - v_in[v_at(s, x + 1)])
            value = value + c_ref[cx_at(s, x - 1)] * (v - v_in[v_at(s, x - 1)])
            along = c_ref[cy_at(s, x)] * (v - next_y(v))
            sum_ref[6 * s + x + 1] = value + (along - roll(along, 1, 0))
    for half, (d, v) in enumerate(
        zip(columns(R_PLANES, lambda s, x: d_in[v_at(s, x)]), columns(R_PLANES, lambda s, x: v_in[v_at(s, x)]))
    ):
        d_edge[half] = d
        v_edge[half] = v


def end_first_step(v_in, d_in, c_ref, sum_ref, d_side, v_side, z_ref, mask, store):
    lane = iota((ROWS, 128), 1)
    first, final = lane == 0, lane == 127
    for s in range(SPECIES):
        for x in R_PLANES:
            place, half, n = slot_of(s, x), s // 2, 6 * s + x + 1

            def beyond(side, place=place, half=half):
                return jnp.where(final, roll(side[half], 127 - place - DEEP, 1), roll(side[half], 1 - DEEP - place, 1))

            more = jnp.where(first | final, 0.5 * (d_in[v_at(s, x)] + beyond(d_side)), 0.0)
            z_ref[cz_at(s, x) - WITHOUT_Z] = jnp.where(final, more, c_ref[cz_at(s, x)])
            z_ref[back_at(s, x) - WITHOUT_Z] = jnp.where(first, more, c_ref[back_at(s, x)])
            value = sum_ref[n] + more * (v_in[v_at(s, x)] - beyond(v_side))
            store(s, x, value * (DAMPING * mask_of(x, mask[0], *mask[2:])))


def side_conduct(d_side, edges, c_side):
    for half in range(HALVES):
        d = d_side[half]
        c_side[4 * half] = 0.5 * (d + roll(d, -8, 1))
        c_side[4 * half + 1] = 0.5 * (d + next_y(d))
        c_side[4 * half + 2] = 0.5 * (d + side_next_z(d, edges[half]))
        c_side[4 * half + 3] = 0.5 * (d + side_previous_z(d, edges[half]))


def plane_sum(degree, s, x, v_of, v_side, main_ref, c_ref, before=True, after=True):
    half, place, v = s // 2, slot_of(s, x), v_of(s, x)
    value = v * (1.0 - SHIFTS[degree])
    value = value + c_ref[cz_at(s, x)] * (v - next_z(v, v_side[half], place))
    value = value + c_ref[back_at(s, x)] * (v - previous_z(v, v_side[half], place))
    for t in range(SPECIES):
        value = value + main_ref[r_at(s, t, x)] * v_of(t, x)
    if after:
        value = value + c_ref[cx_at(s, x)] * (v - v_of(s, x + 1))
    if before:
        value = value + c_ref[cx_at(s, x - 1)] * (v - v_of(s, x - 1))
    along = c_ref[cy_at(s, x)] * (v - next_y(v))
    return value + (along - roll(along, 1, 0))


def step(degree, planes, v_of, v_side, main_ref, side_ref, c_ref, c_side, mask, store, sides=True):
    for x in planes:
        factor = DAMPING * mask_of(x, mask[0], *mask[2:])
        for s in range(SPECIES):
            store(s, x, plane_sum(degree, s, x, v_of, v_side, main_ref, c_ref) * factor)
    if not sides:
        return None
    return side_step(degree, columns(planes, v_of), v_side, side_ref, c_side, mask)


def side_step(degree, edges, v_side, side_ref, c_side, mask):
    lane = iota((ROWS, 128), 1)
    both = []
    for half in range(HALVES):
        other = roll(v_side[half], 64, 1)
        both.append(jnp.where(lane < 64, v_side[half], other))
        both.append(jnp.where(lane < 64, other, v_side[half]))
    result = []
    for half in range(HALVES):
        v = v_side[half]
        value = v * (1.0 - SHIFTS[degree])
        value = value + c_side[4 * half + 2] * (v - side_next_z(v, edges[half]))
        value = value + c_side[4 * half + 3] * (v - side_previous_z(v, edges[half]))
        for t in range(SPECIES):
            value = value + side_ref[2 * HALVES + SPECIES * half + t] * both[t]
        across = c_side[4 * half] * (v - roll(v, -8, 1))
        value = value + (across - roll(across, 8, 1))
        along = c_side[4 * half + 1] * (v - next_y(v))
        value = value + (along - roll(along, 1, 0))
        result.append(value * (DAMPING * mask[1]))
    return result


FACE_EDGES = SPECIES * WIDE * 2
FACE_SIDE = FACE_EDGES + SPECIES
FACE_TILES = FACE_SIDE + 3


def put_own(out_ref, s, x, value):
    out_ref[8 * s + 2 * x] = value[:8]
    out_ref[8 * s + 2 * x + 1] = value[8:16]


def first_steps(r_ref, x_before, x_after, edge_own, edge_more, v_in, d_in, c_early, sum_ref, d_edge, v_edge, own_before, own_after, more_before, more_after, v1_ref, v2_ref, wide_ref, wide_side, low_ref, high_ref, side_ref, z_ref, c_side, v_mid):
    main_ref = Planes(own_planes(None, None, r_ref, x_before, x_after), edge_own, edge_more)
    lane = iota((ROWS, 128), 1)
    for side in range(SIDES):
        side_ref[side] = unpack_z(side, own_before, own_after, more_before, more_after)
    mask = masks()
    v_side = [side_ref[half] * mask[1] for half in range(HALVES)]
    d_side = [side_ref[HALVES + half] * mask[1] for half in range(HALVES)]
    side_conduct(d_side, d_edge, c_side)
    c_ref = Conducts(c_early, z_ref)

    def store_mid(s, x, value):
        v_mid[v_at(s, x)] = value
        if 0 <= x < 4:
            put_own(v1_ref, s, x, value)

    def store_wide(s, x, value):
        wide_ref[4 * s + x] = value
        put_own(v2_ref, s, x, value)

    more = (main_ref, side_ref, c_ref, c_side, mask)
    end_first_step(v_in, d_in, c_early, sum_ref, d_side, v_side, z_ref, mask, store_mid)
    v_side = side_step(0, v_edge, v_side, side_ref, c_side, mask)
    v_side = step(1, range(4), lambda s, x: v_mid[v_at(s, x)], v_side, *more, store_wide)
    for half in range(HALVES):
        wide_side[half] = v_side[half]
    slot = lane // 8 % 8
    row = iota((8, 128), 0)
    near = (row < 2) | (row >= 6)
    for face, start, shift in ((low_ref, 0, -16), (high_ref, 4 - WIDE, 16)):
        for s in range(SPECIES):
            values = [wide_ref[4 * s + start + n] for n in range(WIDE)]
            for n in range(WIDE):
                face[(s * WIDE + n) * 2] = values[n][:8]
                face[(s * WIDE + n) * 2 + 1] = values[n][8:16]
            face[FACE_EDGES + s] = jnp.where(near, values[0][16:], roll(values[1][16:], DEEP, 0))
        kept = (slot >= start + WIDE) & (slot < start + 2 * WIDE)
        packed = jnp.where(kept, v_side[0], roll(v_side[1], shift, 1))
        for n in range(3):
            face[FACE_SIDE + n] = packed[8 * n : 8 * n + 8]


def middle_step(r_ref, x_before, x_after, edge_own, edge_more, c_early, z_ref, wide_ref, wide_side, sum_ref, v_edge):
    main_ref = Planes(own_planes(None, None, r_ref, x_before, x_after), edge_own, edge_more)
    c_ref = Conducts(c_early, z_ref)

    def v_of(s, x):
        return wide_ref[4 * s + x]

    for x in range(4):
        for s in range(SPECIES):
            sum_ref[4 * s + x] = plane_sum(2, s, x, v_of, wide_side, main_ref, c_ref, x > 0, x < 3)
    for half, value in enumerate(columns(range(4), v_of)):
        v_edge[half] = value


def last_steps(r_ref, x_before, x_after, edge_own, edge_more, side_ref, c_early, z_ref, c_side, wide_ref, wide_side, sum_ref, v_edge, before_ref, after_ref, q_ref, v1_ref, v2_ref, sums_in, v3_ref, v4_ref, sums_ref, v_in, v_mid):
    main_ref = Planes(own_planes(None, None, r_ref, x_before, x_after), edge_own, edge_more)
    c_ref = Conducts(c_early, z_ref)
    mask = masks()
    for s in range(SPECIES):
        for face, start, factor in ((before_ref, -WIDE, mask[2]), (after_ref, 4, mask[3])):
            for n in range(WIDE):
                k = (s * WIDE + n) * 2
                value = jnp.concatenate([face[k], face[k + 1], roll(face[FACE_EDGES + s], DEEP * n, 0)], 0)
                v_in[v_at(s, start + n)] = value * factor
    slot = iota((ROWS, 128), 1) // 8 % 8
    before, after = (
        jnp.concatenate([face[FACE_SIDE + n] for n in range(3)], 0) * factor
        for face, factor in ((before_ref, mask[2]), (after_ref, mask[3]))
    )
    v_side = []
    for half in range(HALVES):
        value = jnp.where(slot < WIDE, roll(before, -32 - 16 * half, 1), wide_side[half])
        v_side.append(jnp.where(slot >= WIDE + 4, roll(after, 32 + 16 * half, 1), value))

    def first(s, x):
        return wide_ref[4 * s + x] if 0 <= x < 4 else v_in[v_at(s, x)]

    def store_mid(s, x, value):
        v_mid[v_at(s, x)] = value
        if 0 <= x < 4:
            put_own(v3_ref, s, x, value)

    def store_last(s, x, value):
        put_own(v4_ref, s, x, value)

    more = (main_ref, side_ref, c_ref, c_side, mask)
    for x in R_PLANES:
        factor = DAMPING * mask_of(x, mask[0], *mask[2:])
        for s in range(SPECIES):
            if 0 <= x < 4:
                value = sum_ref[4 * s + x]
                if x == 0:
                    value = value + c_ref[cx_at(s, -1)] * (first(s, 0) - first(s, -1))
                if x == 3:
                    value = value + c_ref[cx_at(s, 3)] * (first(s, 3) - first(s, 4))
            else:
                value = plane_sum(2, s, x, first, v_side, main_ref, c_ref)
            store_mid(s, x, value * factor)
    edges = [v_edge[half] + more for half, more in enumerate(columns((-1, 4), first))]
    v_side = side_step(2, edges, v_side, side_ref, c_side, mask)
    step(3, range(4), lambda s, x: v_mid[v_at(s, x)], v_side, *more, store_last, sides=False)

    def load(i):
        return [q_ref[a, i] for a in range(EARLIER)] + [v1_ref[i], v2_ref[i], v3_ref[i], v4_ref[i]]

    row = sums_in[...] + products(new_pairs(2) + new_pairs(3), load, q_ref.shape[1])
    sums_ref[...] = jnp.broadcast_to(jnp.sum(row, 0, keepdims=True), sums_ref.shape)


def middle_products(q_ref, v1_ref, v2_ref, before_ref, out_ref):
    def load(i):
        return [q_ref[a, i] for a in range(EARLIER)] + [v1_ref[i], v2_ref[i]]

    out_ref[...] = before_ref[...] + products(new_pairs(0) + new_pairs(1), load, q_ref.shape[1])


def products(pairs, load, count):
    def body(i, sums):
        values = load(i)
        return tuple(total + values[a] * values[b] for total, (a, b) in zip(sums, pairs))

    zero = jnp.zeros((8, 128), jnp.float32)
    sums = lax.fori_loop(0, count, body, (zero,) * len(pairs), unroll=4)
    lane = lax.broadcasted_iota(jnp.int32, (8, 128), 1)
    row = zero
    for total, pair in zip(sums, pairs):
        row = jnp.where(lane == SLOT[pair], jnp.sum(total, 1, keepdims=True), row)
    return row


def earlier_products(q_ref, out_ref):
    pairs = [(a, b) for b in range(EARLIER) for a in range(b + 1)]
    out_ref[...] = products(pairs, lambda i: [q_ref[a, i] for a in range(EARLIER)], q_ref.shape[1])


def new_pairs(number):
    return [(a, EARLIER + number) for a in range(EARLIER + number + 1)]


def finish_kernel(entries, sums_ref, q_ref, *refs):
    v_refs, (new_ref, coeff_ref, triangle_ref) = refs[:STEPS], refs[STEPS:]
    parts = [sums_ref[i] for i in range(sums_ref.shape[0])]
    while len(parts) > 1:
        parts = [parts[i] + parts[i + 1] for i in range(0, len(parts), 2)]
    total = parts[0]
    total = jnp.broadcast_to(jnp.sum(total, 0, keepdims=True), total.shape) * (1.0 / entries)

    def entry(a, b):
        k = SLOT[(min(a, b), max(a, b))]
        return jnp.broadcast_to(total[:, k : k + 1], total.shape)

    coeff = [[entry(i, EARLIER + j) for j in range(STEPS)] for i in range(EARLIER)]
    overlap = {(a, b): entry(a, b) for b in range(EARLIER) for a in range(b + 1)}
    gram = {}
    for k in range(STEPS):
        mixed = []
        for i in range(EARLIER):
            term = -2.0 * coeff[i][k]
            for m in range(EARLIER):
                term = term + overlap[(min(i, m), max(i, m))] * coeff[m][k]
            mixed.append(term)
        for j in range(k, STEPS):
            value = entry(EARLIER + k, EARLIER + j)
            for i in range(EARLIER):
                value = value + coeff[i][j] * mixed[i]
            gram[(j, k)] = value
    factor, inverse = {}, []
    for k in range(STEPS):
        pivot = gram[(k, k)]
        for m in range(k):
            pivot = pivot - factor[(k, m)] * factor[(k, m)]
        inverse.append(lax.rsqrt(pivot))
        factor[(k, k)] = pivot * inverse[k]
        for j in range(k + 1, STEPS):
            value = gram[(j, k)]
            for m in range(k):
                value = value - factor[(j, m)] * factor[(k, m)]
            factor[(j, k)] = value * inverse[k]
    row = lax.broadcasted_iota(jnp.int32, total.shape, 0)
    lane = lax.broadcasted_iota(jnp.int32, total.shape, 1)
    table = jnp.zeros_like(total)
    for i in range(EARLIER):
        for j in range(STEPS):
            table = jnp.where((row == j) & (lane == i), coeff[i][j], table)
    coeff_ref[...] = table[:STEPS, :EARLIER]
    table = jnp.zeros_like(total)
    for (j, k), value in factor.items():
        table = jnp.where((row == k) & (lane == j), value, table)
    triangle_ref[...] = table[:STEPS, :STEPS]

    def body(n, carry):
        earlier = [q_ref[i, n] for i in range(EARLIER)]
        done = []
        for j in range(STEPS):
            value = v_refs[j][n]
            for i in range(EARLIER):
                value = value - coeff[i][j] * earlier[i]
            for k in range(j):
                value = value - factor[(j, k)] * done[k]
            done.append(value * inverse[j])
            new_ref[j, n] = done[j]
        return carry

    lax.fori_loop(0, q_ref.shape[1], body, 0, unroll=8)


def call(body, outs, cost, *args, **more):
    return pl.pallas_call(
        body,
        out_shape=[jax.ShapeDtypeStruct(shape, jnp.float32) for shape in outs],
        cost_estimate=pl.CostEstimate(flops=cost, bytes_accessed=cost, transcendentals=0),
        compiler_params=pltpu.CompilerParams(vmem_limit_bytes=24 << 20),
        **more,
    )(*args)


def shifts(axis):
    count = lax.axis_size(axis)
    up = [(i, (i + 1) % count) for i in range(count)]
    return up, [(target, source) for source, target in up]


def exchange(axis, low, high):
    up, down = shifts(axis)
    return lax.ppermute(high, axis, up), lax.ppermute(low, axis, down)


def on_device(earlier_basis, diffusivity, reaction):
    span_x, span_y, span_z = diffusivity.shape[1:]
    tiles = SPECIES * span_x * span_y // 8
    devices = 1
    for axis in AXES:
        devices *= lax.axis_size(axis)
    entries = tiles * 8 * span_z * devices
    in_hbm = pl.BlockSpec(memory_space=pltpu.HBM)
    given = (earlier_basis, diffusivity, reaction)
    face = (2 * SPECIES * WIDE + SPECIES * SPECIES, span_y, span_z)
    field = diffusivity.shape
    low, high, *kept = call(
        x_faces,
        [face, face, field, field],
        1 << 20,
        *[pltpu.with_memory_space_constraint(a, pltpu.HBM) for a in given],
        in_specs=[in_hbm] * 3,
        scratch_shapes=[pltpu.SemaphoreType.DMA((8,))],
    )
    x_halos = exchange("gx", low, high)
    kept.append(reaction)
    face = (Y_TILES[0], 8, span_z)
    z_face = (SIDES // 4, 16, span_z)
    own = call(own_faces, [face, face, z_face, z_face], 1 << 20, *kept)
    y_own = exchange("gy", *own[:2])
    up, down = shifts("gz")
    z_before = lax.ppermute(own[3], "gz", up)
    z_after = lax.ppermute(own[2], "gz", down)
    z_own = (z_before, z_after)
    face = (Y_TILES[1], 8, span_z)
    faces = call(more_y_faces, [face, face], 1 << 20, *x_halos)
    y_more = exchange("gy", *faces)
    face = (2 * BLOCKS, 8, span_z)
    edges = (PLANES, 8, span_z)
    edge_own, low, high = call(some_z_faces, [edges, face, face], 1 << 20, *x_halos, *y_own)
    edge_more, low, high = call(more_z_faces, [edges, face, face], 1 << 20, *y_more, low, high)
    edge = (edge_own, edge_more)
    z_more = exchange("gz", low, high)
    basis = earlier_basis.reshape(EARLIER, tiles, 8, span_z)
    (sums,) = call(earlier_products, [(8, span_z)], 4 << 20, basis)
    own = (tiles, 8, span_z)
    plane = (ROWS, span_z)
    early = call(
        early_steps,
        [(count,) + plane for count in (D_BASE, D_BASE, CONDUCTS, SPECIES * len(R_PLANES), HALVES, HALVES)],
        1 << 20,
        *kept,
        *x_halos,
        *edge,
    )
    scratch = [pltpu.VMEM((D_BASE,) + plane, jnp.float32)]
    face = (FACE_TILES, 8, span_z)
    several = [(count,) + plane for count in (SPECIES * span_x, HALVES)] + [face, face]
    several += [(count,) + plane for count in (SIDES, CONDUCTS - WITHOUT_Z, 4 * HALVES)]
    v1, v2, wide, wide_side, low, high, side, z_conducts, side_conducts = call(
        first_steps,
        [own, own] + several,
        1 << 20,
        reaction,
        *x_halos,
        *edge,
        *early,
        *z_own,
        *z_more,
        scratch_shapes=scratch,
    )
    halos = exchange("gx", low, high)
    (sums,) = call(middle_products, [(8, span_z)], 4 << 20, basis, v1, v2, sums)
    plane_sums = call(
        middle_step,
        [(SPECIES * span_x,) + plane, (HALVES,) + plane],
        1 << 20,
        reaction,
        *x_halos,
        *edge,
        early[2],
        z_conducts,
        wide,
        wide_side,
    )
    v3, v4, rows = call(
        last_steps,
        [own, own, (devices, span_z)],
        1 << 20,
        reaction,
        *x_halos,
        *edge,
        side,
        early[2],
        z_conducts,
        side_conducts,
        wide,
        wide_side,
        *plane_sums,
        *halos,
        basis,
        v1,
        v2,
        sums,
        scratch_shapes=scratch * 2,
    )
    rows = lax.all_to_all(rows.reshape(devices, 1, span_z), AXES, 0, 0)
    new, coeff, triangle = call(
        functools.partial(finish_kernel, entries),
        [(STEPS, tiles, 8, span_z), (STEPS, EARLIER), (STEPS, STEPS)],
        1 << 20,
        rows.reshape(devices // 8, 8, span_z),
        basis,
        v1,
        v2,
        v3,
        v4,
    )
    return new.reshape((STEPS, SPECIES, span_x, span_y, span_z)), coeff.T, triangle


def solution(mesh):
    in_specs = (
        P(None, None, "gx", "gy", "gz"),
        P(None, "gx", "gy", "gz"),
        P(None, None, "gx", "gy", "gz"),
    )
    out_specs = (P(None, None, "gx", "gy", "gz"), P(), P())
    return jax.shard_map(
        on_device, mesh=mesh, in_specs=in_specs, out_specs=out_specs, check_vma=False
    )
```

```python
import functools

import jax
import jax.numpy as jnp
from jax import lax
from jax.experimental import pallas as pl
from jax.experimental.pallas import tpu as pltpu
from jax.sharding import PartitionSpec as P

SPECIES = 4
STEPS = 4
EARLIER = 8
SHIFTS = (6.0, 9.0, 14.0, 17.0)
DAMPING = 0.2
AXES = ("gx", "gy", "gz")

VECTORS = EARLIER + STEPS
SLOT = {}
for _b in range(VECTORS):
    for _a in range(_b + 1):
        SLOT[(_a, _b)] = len(SLOT)

WIDE = 2
DEEP = 4
ROWS = 24
V_PLANES = tuple(range(-WIDE, 4 + WIDE))
R_PLANES = tuple(range(-1, 5))
V_BASE = 0
D_BASE = SPECIES * len(V_PLANES)
R_BASE = 2 * D_BASE
PLANES = R_BASE + SPECIES * SPECIES * len(R_PLANES)
HALVES = SPECIES // 2
SIDES = 2 * HALVES + HALVES * SPECIES
BLOCKS = SIDES // 2


def v_at(s, x):
    return V_BASE + s * len(V_PLANES) + x + WIDE


def d_at(s, x):
    return D_BASE + s * len(V_PLANES) + x + WIDE


def r_at(s, t, x):
    return R_BASE + (s * SPECIES + t) * len(R_PLANES) + x + 1


def iota(shape, dim):
    return lax.broadcasted_iota(jnp.int32, shape, dim)


def roll(value, shift, axis):
    shift %= value.shape[axis]
    return pltpu.roll(value, shift, axis) if shift else value


def x_faces(q_ref, d_ref, r_ref, low_ref, high_ref, v_out, d_out, sems):
    copies = []
    for face, planes, plane in ((low_ref, pl.ds(0, WIDE), 0), (high_ref, pl.ds(4 - WIDE, WIDE), 3)):
        for n, source in enumerate((q_ref.at[EARLIER - 1, :, planes], d_ref.at[:, planes])):
            target = face.at[pl.ds(n * SPECIES * WIDE, SPECIES * WIDE)]
            copies.append((source, target.reshape((SPECIES, WIDE) + face.shape[1:])))
        target = face.at[pl.ds(2 * SPECIES * WIDE, SPECIES * SPECIES)]
        copies.append((r_ref.at[:, :, plane], target.reshape((SPECIES, SPECIES) + face.shape[1:])))
    copies += [(q_ref.at[EARLIER - 1], v_out), (d_ref, d_out)]
    started = [pltpu.make_async_copy(a, b, sems.at[n]) for n, (a, b) in enumerate(copies)]
    for copy in started:
        copy.start()
    for copy in started:
        copy.wait()


def own_planes(v_ref, d_ref, r_ref, before_ref, after_ref):
    def pick(own, slot, width, x):
        if x < 0:
            return lambda rows: before_ref[slot + x + width, rows]
        if x > 3:
            return lambda rows: after_ref[slot + x - 4, rows]
        return lambda rows: own(x, rows)

    planes = []
    for s in range(SPECIES):
        for x in V_PLANES:
            planes.append(pick(lambda x, rows, s=s: v_ref[s, x, rows], s * WIDE, WIDE, x))
    for s in range(SPECIES):
        for x in V_PLANES:
            planes.append(pick(lambda x, rows, s=s: d_ref[s, x, rows], (SPECIES + s) * WIDE, WIDE, x))
    for s in range(SPECIES):
        for t in range(SPECIES):
            slot = 2 * SPECIES * WIDE + s * SPECIES + t
            for x in R_PLANES:
                planes.append(pick(lambda x, rows, s=s, t=t: r_ref[s, t, x, rows], slot, 1, x))
    return planes


def y_places():
    places, used = {}, [0, 0]

    def put(message, planes, rows):
        per = 8 // rows
        for n, plane in enumerate(planes):
            places[plane] = (message, used[message] + n // per, n % per, rows)
        used[message] += len(planes) // per

    near, far, own = [], [], []
    for base in (v_at, d_at):
        for s in range(SPECIES):
            for x in V_PLANES:
                (own if 0 <= x < 4 else near if -1 <= x < 5 else far).append(base(s, x))
    for s in range(SPECIES):
        for t in range(SPECIES):
            for x in R_PLANES:
                (own if 0 <= x < 4 else far).append(r_at(s, t, x))
    put(0, own, DEEP)
    put(1, near, DEEP)
    put(1, far, 2)
    return places, used


Y_PLACES, Y_TILES = y_places()


def y_faces(message, planes, near_ref, far_ref):
    even = lax.rem(lax.axis_index("gy"), 2) == 0
    row = iota((8, 128), 0)
    low, high = [None] * Y_TILES[message], [None] * Y_TILES[message]
    for plane, (number, tile, place, rows) in Y_PLACES.items():
        if number != message:
            continue
        first = roll(planes[plane](pl.ds(0, 8)), rows * place, 0)
        final = roll(planes[plane](pl.ds(8, 8)), rows * place + rows, 0)
        here = row // rows == place
        low[tile] = first if low[tile] is None else jnp.where(here, first, low[tile])
        high[tile] = final if high[tile] is None else jnp.where(here, final, high[tile])
    for tile in range(Y_TILES[message]):
        near_ref[tile] = jnp.where(even, high[tile], low[tile])
        far_ref[tile] = jnp.where(even, low[tile], high[tile])


def own_faces(v_ref, d_ref, r_ref, y_low, y_high, z_low, z_high):
    planes = own_planes(v_ref, d_ref, r_ref, None, None)
    y_faces(0, planes, y_low, y_high)
    for block, found in enumerate(z_groups(True)):
        z_low[block], z_high[block] = pack_z(found, lambda plane: planes[plane](pl.ds(0, 16)), 16)


def more_y_faces(before_ref, after_ref, low_ref, high_ref):
    y_faces(1, own_planes(None, None, None, before_ref, after_ref), low_ref, high_ref)


def side_planes(side):
    found = []
    for half in range(2):
        for x in V_PLANES:
            if side < 2 * HALVES:
                s = side % HALVES * 2 + half
                found.append(v_at(s, x) if side < HALVES else d_at(s, x))
            else:
                pair, t = divmod(side - 2 * HALVES, SPECIES)
                found.append(r_at(2 * pair + half, t, x) if x in R_PLANES else None)
    return found


def z_groups(own):
    blocks = [[] for _ in range(SIDES // 4)]
    for side in range(SIDES):
        for slot, plane in enumerate(side_planes(side)):
            if plane is not None and own == (WIDE <= slot % 8 < WIDE + 4):
                group = (2 * slot + 8 * (side % 4 // 2) + side % 2) % 32
                blocks[side // 4].append((plane, group))
    return blocks


def z_edge_groups():
    blocks = [[] for _ in range(BLOCKS)]
    for side in range(SIDES):
        for slot, plane in enumerate(side_planes(side)):
            if plane is not None:
                blocks[side // 2].append((plane, 2 * slot + side % 2))
    return blocks


def pack_z(planes, value_of, rows):
    group = iota((rows, 128), 1) // DEEP
    low = high = jnp.zeros((rows, 128), jnp.float32)
    for plane, k in planes:
        value = value_of(plane)
        low = jnp.where(group == k, roll(value, DEEP * k, 1), low)
        high = jnp.where(group == k, roll(value, DEEP * k + DEEP, 1), high)
    return low, high


def is_own(plane):
    return Y_PLACES[plane][0] == 0


def y_edge(plane, near_ref, far_ref):
    _, tile, place, rows = Y_PLACES[plane]
    even = lax.rem(lax.axis_index("gy"), 2) == 0
    near, far = near_ref[tile], far_ref[tile]
    after = roll(jnp.where(even, near, far), -rows * place, 0)
    before = roll(jnp.where(even, far, near), 8 - rows - rows * place, 0)
    return jnp.where(iota((8, 128), 0) < DEEP, after, before)


def some_z_faces(x_before, x_after, y_before, y_after, edge_ref, low_ref, high_ref):
    planes = own_planes(None, None, None, x_before, x_after)
    for block, found in enumerate(z_groups(False)):
        low, high = pack_z(found, lambda plane: planes[plane](pl.ds(0, 16)), 16)
        for half in range(2):
            low_ref[2 * block + half] = low[8 * half : 8 * half + 8]
            high_ref[2 * block + half] = high[8 * half : 8 * half + 8]

    def value_of(plane):
        edge_ref[plane] = y_edge(plane, y_before, y_after)
        return edge_ref[plane]

    for block, found in enumerate(z_edge_groups()):
        found = [(plane, k) for plane, k in found if is_own(plane)]
        low_ref[BLOCKS + block], high_ref[BLOCKS + block] = pack_z(found, value_of, 8)


def more_z_faces(y_before, y_after, some_low, some_high, edge_ref, low_ref, high_ref):
    def value_of(plane):
        edge_ref[plane] = y_edge(plane, y_before, y_after)
        return edge_ref[plane]

    for block, found in enumerate(z_edge_groups()):
        low_ref[block], high_ref[block] = some_low[block], some_high[block]
        found = [(plane, k) for plane, k in found if not is_own(plane)]
        low, high = pack_z(found, value_of, 8)
        low_ref[BLOCKS + block] = some_low[BLOCKS + block] + low
        high_ref[BLOCKS + block] = some_high[BLOCKS + block] + high


def unpack_z(side, own_before, own_after, more_before, more_after):
    lane = iota((16, 128), 1)
    block, turned, part = side // 4, side % 4 // 2, side % 2
    own = (lane // 8 % 8 >= WIDE) & (lane // 8 % 8 < WIDE + 4)
    if turned:
        own = ~own

    def rows(own_ref, more_ref):
        more = jnp.concatenate([more_ref[2 * block], more_ref[2 * block + 1]], 0)
        return jnp.where(own, own_ref[block], more)

    def join(before, after, shift):
        early = iota(before.shape, 1) % 8 < DEEP
        return jnp.where(early, roll(before, -shift - DEEP * part, 1), roll(after, DEEP - shift - DEEP * part, 1))

    main = join(rows(own_before, more_before), rows(own_after, more_after), 32 * turned)
    edge = join(more_before[BLOCKS + side // 2], more_after[BLOCKS + side // 2], 0)
    return jnp.concatenate([main, edge], 0)


class Planes:
    def __init__(self, planes, edge_own, edge_more):
        self.planes, self.edge_own, self.edge_more = planes, edge_own, edge_more

    def __getitem__(self, plane):
        edge_ref = self.edge_own if is_own(plane) else self.edge_more
        return jnp.concatenate([self.planes[plane](pl.ds(0, 16)), edge_ref[plane]], 0)


def masks():
    first = {axis: lax.axis_index(axis) == 0 for axis in AXES}
    final = {axis: lax.axis_index(axis) == lax.axis_size(axis) - 1 for axis in AXES}

    def keep(flag):
        return jnp.where(flag, 0.0, 1.0).astype(jnp.float32)

    row, lane = iota((ROWS, 128), 0), iota((ROWS, 128), 1)
    main = jnp.where(row < 16, 1.0, jnp.where(row < 16 + DEEP, keep(final["gy"]), keep(first["gy"])))
    slot = lane // 8 % 8
    side = main * jnp.where(lane % 8 < DEEP, keep(first["gz"]), keep(final["gz"]))
    before, after = keep(first["gx"]), keep(final["gx"])
    side = side * jnp.where(slot < WIDE, before, jnp.where(slot < WIDE + 4, 1.0, after))
    return main, side, before, after


def mask_of(x, main, before, after):
    if 0 <= x < 4:
        return main
    return main * (before if x < 0 else after)


def next_y(value):
    return roll(value, -1, 0)


def slot_of(s, x):
    return 64 * (s % 2) + 8 * (x + WIDE)


def columns(planes, value_of):
    group = iota((ROWS, 128), 1) // 8
    found = []
    for half in range(HALVES):
        value = jnp.zeros((ROWS, 128), jnp.float32)
        for s in (2 * half, 2 * half + 1):
            for x in planes:
                place = slot_of(s, x)
                value = jnp.where(group == place // 8, roll(value_of(s, x), place + DEEP, 1), value)
        found.append(value)
    return found


def next_z(value, side, place):
    lane = iota((ROWS, 128), 1)
    return jnp.where(lane == 127, roll(side, 127 - place - DEEP, 1), roll(value, -1, 1))


def previous_z(value, side, place):
    lane = iota((ROWS, 128), 1)
    return jnp.where(lane == 0, roll(side, -(place + DEEP - 1), 1), roll(value, 1, 1))


def side_next_z(side, edge):
    return roll(jnp.where(iota((ROWS, 128), 1) % 8 == DEEP, edge, side), -1, 1)


def side_previous_z(side, edge):
    return roll(jnp.where(iota((ROWS, 128), 1) % 8 == DEEP - 1, edge, side), 1, 1)


def cx_at(s, x):
    return s * 7 + x + 2


def cy_at(s, x):
    return SPECIES * 7 + s * 6 + x + 1


def cz_at(s, x):
    return SPECIES * 13 + s * 6 + x + 1


def back_at(s, x):
    return SPECIES * 19 + s * 6 + x + 1


CONDUCTS = SPECIES * 25


WITHOUT_Z = SPECIES * 13


class Conducts:
    def __init__(self, plain_ref, z_ref):
        self.plain_ref, self.z_ref = plain_ref, z_ref

    def __getitem__(self, k):
        return self.plain_ref[k] if k < WITHOUT_Z else self.z_ref[k - WITHOUT_Z]


def early_steps(v_ref, d_ref, r_ref, x_before, x_after, edge_own, edge_more, v_in, d_in, c_ref, sum_ref, d_edge, v_edge):
    main_ref = Planes(own_planes(v_ref, d_ref, r_ref, x_before, x_after), edge_own, edge_more)
    mask = masks()
    for s in range(SPECIES):
        for x in V_PLANES:
            factor = mask_of(x, mask[0], *mask[2:])
            v_in[v_at(s, x)] = main_ref[v_at(s, x)] * factor
            d_in[v_at(s, x)] = main_ref[d_at(s, x)] * factor
    lane = iota((ROWS, 128), 1)
    first, final = lane == 0, lane == 127
    for s in range(SPECIES):
        for x in V_PLANES:
            d = d_in[v_at(s, x)]
            if x < V_PLANES[-1]:
                c_ref[cx_at(s, x)] = 0.5 * (d + d_in[v_at(s, x + 1)])
            if x in R_PLANES:
                c_ref[cy_at(s, x)] = 0.5 * (d + next_y(d))
                c_ref[cz_at(s, x)] = jnp.where(final, 0.0, 0.5 * (d + roll(d, -1, 1)))
                c_ref[back_at(s, x)] = jnp.where(first, 0.0, 0.5 * (d + roll(d, 1, 1)))
    for x in R_PLANES:
        here = [v_in[v_at(t, x)] for t in range(SPECIES)]
        for s in range(SPECIES):
            v = here[s]
            value = v * (1.0 - SHIFTS[0])
            value = value + c_ref[cz_at(s, x)] * (v - roll(v, -1, 1))
            value = value + c_ref[back_at(s, x)] * (v - roll(v, 1, 1))
            for t in range(SPECIES):
                value = value + main_ref[r_at(s, t, x)] * here[t]
            value = value + c_ref[cx_at(s, x)] * (v - v_in[v_at(s, x + 1)])
            value = value + c_ref[cx_at(s, x - 1)] * (v - v_in[v_at(s, x - 1)])
            along = c_ref[cy_at(s, x)] * (v - next_y(v))
            sum_ref[6 * s + x + 1] = value + (along - roll(along, 1, 0))
    for half, (d, v) in enumerate(
        zip(columns(R_PLANES, lambda s, x: d_in[v_at(s, x)]), columns(R_PLANES, lambda s, x: v_in[v_at(s, x)]))
    ):
        d_edge[half] = d
        v_edge[half] = v


def end_first_step(v_in, d_in, c_ref, sum_ref, d_side, v_side, z_ref, mask, store):
    lane = iota((ROWS, 128), 1)
    first, final = lane == 0, lane == 127
    for s in range(SPECIES):
        for x in R_PLANES:
            place, half, n = slot_of(s, x), s // 2, 6 * s + x + 1

            def beyond(side, place=place, half=half):
                return jnp.where(final, roll(side[half], 127 - place - DEEP, 1), roll(side[half], 1 - DEEP - place, 1))

            more = jnp.where(first | final, 0.5 * (d_in[v_at(s, x)] + beyond(d_side)), 0.0)
            z_ref[cz_at(s, x) - WITHOUT_Z] = jnp.where(final, more, c_ref[cz_at(s, x)])
            z_ref[back_at(s, x) - WITHOUT_Z] = jnp.where(first, more, c_ref[back_at(s, x)])
            value = sum_ref[n] + more * (v_in[v_at(s, x)] - beyond(v_side))
            store(s, x, value * (DAMPING * mask_of(x, mask[0], *mask[2:])))


def side_conduct(d_side, edges, c_side):
    for half in range(HALVES):
        d = d_side[half]
        c_side[4 * half] = 0.5 * (d + roll(d, -8, 1))
        c_side[4 * half + 1] = 0.5 * (d + next_y(d))
        c_side[4 * half + 2] = 0.5 * (d + side_next_z(d, edges[half]))
        c_side[4 * half + 3] = 0.5 * (d + side_previous_z(d, edges[half]))


def plane_sum(degree, s, x, v_of, v_side, main_ref, c_ref, before=True, after=True):
    half, place, v = s // 2, slot_of(s, x), v_of(s, x)
    value = v * (1.0 - SHIFTS[degree])
    value = value + c_ref[cz_at(s, x)] * (v - next_z(v, v_side[half], place))
    value = value + c_ref[back_at(s, x)] * (v - previous_z(v, v_side[half], place))
    for t in range(SPECIES):
        value = value + main_ref[r_at(s, t, x)] * v_of(t, x)
    if after:
        value = value + c_ref[cx_at(s, x)] * (v - v_of(s, x + 1))
    if before:
        value = value + c_ref[cx_at(s, x - 1)] * (v - v_of(s, x - 1))
    along = c_ref[cy_at(s, x)] * (v - next_y(v))
    return value + (along - roll(along, 1, 0))


def step(degree, planes, v_of, v_side, main_ref, side_ref, c_ref, c_side, mask, store, sides=True):
    for x in planes:
        factor = DAMPING * mask_of(x, mask[0], *mask[2:])
        for s in range(SPECIES):
            store(s, x, plane_sum(degree, s, x, v_of, v_side, main_ref, c_ref) * factor)
    if not sides:
        return None
    return side_step(degree, columns(planes, v_of), v_side, side_ref, c_side, mask)


def side_step(degree, edges, v_side, side_ref, c_side, mask):
    lane = iota((ROWS, 128), 1)
    both = []
    for half in range(HALVES):
        other = roll(v_side[half], 64, 1)
        both.append(jnp.where(lane < 64, v_side[half], other))
        both.append(jnp.where(lane < 64, other, v_side[half]))
    result = []
    for half in range(HALVES):
        v = v_side[half]
        value = v * (1.0 - SHIFTS[degree])
        value = value + c_side[4 * half + 2] * (v - side_next_z(v, edges[half]))
        value = value + c_side[4 * half + 3] * (v - side_previous_z(v, edges[half]))
        for t in range(SPECIES):
            value = value + side_ref[2 * HALVES + SPECIES * half + t] * both[t]
        across = c_side[4 * half] * (v - roll(v, -8, 1))
        value = value + (across - roll(across, 8, 1))
        along = c_side[4 * half + 1] * (v - next_y(v))
        value = value + (along - roll(along, 1, 0))
        result.append(value * (DAMPING * mask[1]))
    return result


FACE_EDGES = SPECIES * WIDE * 2
FACE_SIDE = FACE_EDGES + SPECIES
FACE_TILES = FACE_SIDE + 3


def put_own(out_ref, s, x, value):
    out_ref[8 * s + 2 * x] = value[:8]
    out_ref[8 * s + 2 * x + 1] = value[8:16]


def first_steps(r_ref, x_before, x_after, edge_own, edge_more, v_in, d_in, c_early, sum_ref, d_edge, v_edge, own_before, own_after, more_before, more_after, v1_ref, v2_ref, wide_ref, wide_side, low_ref, high_ref, side_ref, z_ref, c_side, v_mid):
    main_ref = Planes(own_planes(None, None, r_ref, x_before, x_after), edge_own, edge_more)
    lane = iota((ROWS, 128), 1)
    for side in range(SIDES):
        side_ref[side] = unpack_z(side, own_before, own_after, more_before, more_after)
    mask = masks()
    v_side = [side_ref[half] * mask[1] for half in range(HALVES)]
    d_side = [side_ref[HALVES + half] * mask[1] for half in range(HALVES)]
    side_conduct(d_side, d_edge, c_side)
    c_ref = Conducts(c_early, z_ref)

    def store_mid(s, x, value):
        v_mid[v_at(s, x)] = value
        if 0 <= x < 4:
            put_own(v1_ref, s, x, value)

    def store_wide(s, x, value):
        wide_ref[4 * s + x] = value
        put_own(v2_ref, s, x, value)

    more = (main_ref, side_ref, c_ref, c_side, mask)
    end_first_step(v_in, d_in, c_early, sum_ref, d_side, v_side, z_ref, mask, store_mid)
    v_side = side_step(0, v_edge, v_side, side_ref, c_side, mask)
    v_side = step(1, range(4), lambda s, x: v_mid[v_at(s, x)], v_side, *more, store_wide)
    for half in range(HALVES):
        wide_side[half] = v_side[half]
    slot = lane // 8 % 8
    row = iota((8, 128), 0)
    near = (row < 2) | (row >= 6)
    for face, start, shift in ((low_ref, 0, -16), (high_ref, 4 - WIDE, 16)):
        for s in range(SPECIES):
            values = [wide_ref[4 * s + start + n] for n in range(WIDE)]
            for n in range(WIDE):
                face[(s * WIDE + n) * 2] = values[n][:8]
                face[(s * WIDE + n) * 2 + 1] = values[n][8:16]
            face[FACE_EDGES + s] = jnp.where(near, values[0][16:], roll(values[1][16:], DEEP, 0))
        kept = (slot >= start + WIDE) & (slot < start + 2 * WIDE)
        packed = jnp.where(kept, v_side[0], roll(v_side[1], shift, 1))
        for n in range(3):
            face[FACE_SIDE + n] = packed[8 * n : 8 * n + 8]


def middle_step(r_ref, x_before, x_after, edge_own, edge_more, c_early, z_ref, wide_ref, wide_side, sum_ref, v_edge):
    main_ref = Planes(own_planes(None, None, r_ref, x_before, x_after), edge_own, edge_more)
    c_ref = Conducts(c_early, z_ref)

    def v_of(s, x):
        return wide_ref[4 * s + x]

    for x in range(4):
        for s in range(SPECIES):
            sum_ref[4 * s + x] = plane_sum(2, s, x, v_of, wide_side, main_ref, c_ref, x > 0, x < 3)
    for half, value in enumerate(columns(range(4), v_of)):
        v_edge[half] = value


def last_steps(r_ref, x_before, x_after, edge_own, edge_more, side_ref, c_early, z_ref, c_side, wide_ref, wide_side, sum_ref, v_edge, before_ref, after_ref, q_ref, v1_ref, v2_ref, sums_in, v3_ref, v4_ref, sums_ref, v_in, v_mid):
    main_ref = Planes(own_planes(None, None, r_ref, x_before, x_after), edge_own, edge_more)
    c_ref = Conducts(c_early, z_ref)
    mask = masks()
    for s in range(SPECIES):
        for face, start, factor in ((before_ref, -WIDE, mask[2]), (after_ref, 4, mask[3])):
            for n in range(WIDE):
                k = (s * WIDE + n) * 2
                value = jnp.concatenate([face[k], face[k + 1], roll(face[FACE_EDGES + s], DEEP * n, 0)], 0)
                v_in[v_at(s, start + n)] = value * factor
    slot = iota((ROWS, 128), 1) // 8 % 8
    before, after = (
        jnp.concatenate([face[FACE_SIDE + n] for n in range(3)], 0) * factor
        for face, factor in ((before_ref, mask[2]), (after_ref, mask[3]))
    )
    v_side = []
    for half in range(HALVES):
        value = jnp.where(slot < WIDE, roll(before, -32 - 16 * half, 1), wide_side[half])
        v_side.append(jnp.where(slot >= WIDE + 4, roll(after, 32 + 16 * half, 1), value))

    def first(s, x):
        return wide_ref[4 * s + x] if 0 <= x < 4 else v_in[v_at(s, x)]

    def store_mid(s, x, value):
        v_mid[v_at(s, x)] = value
        if 0 <= x < 4:
            put_own(v3_ref, s, x, value)

    def store_last(s, x, value):
        put_own(v4_ref, s, x, value)

    more = (main_ref, side_ref, c_ref, c_side, mask)
    for x in R_PLANES:
        factor = DAMPING * mask_of(x, mask[0], *mask[2:])
        for s in range(SPECIES):
            if 0 <= x < 4:
                value = sum_ref[4 * s + x]
                if x == 0:
                    value = value + c_ref[cx_at(s, -1)] * (first(s, 0) - first(s, -1))
                if x == 3:
                    value = value + c_ref[cx_at(s, 3)] * (first(s, 3) - first(s, 4))
            else:
                value = plane_sum(2, s, x, first, v_side, main_ref, c_ref)
            store_mid(s, x, value * factor)
    edges = [v_edge[half] + more for half, more in enumerate(columns((-1, 4), first))]
    v_side = side_step(2, edges, v_side, side_ref, c_side, mask)
    step(3, range(4), lambda s, x: v_mid[v_at(s, x)], v_side, *more, store_last, sides=False)

    def load(i):
        return [q_ref[a, i] for a in range(EARLIER)] + [v1_ref[i], v2_ref[i], v3_ref[i], v4_ref[i]]

    row = sums_in[...] + products(new_pairs(2) + new_pairs(3), load, q_ref.shape[1])
    sums_ref[...] = jnp.broadcast_to(jnp.sum(row, 0, keepdims=True), sums_ref.shape)


def middle_products(q_ref, v1_ref, v2_ref, before_ref, out_ref):
    def load(i):
        return [q_ref[a, i] for a in range(EARLIER)] + [v1_ref[i], v2_ref[i]]

    out_ref[...] = before_ref[...] + products(new_pairs(0) + new_pairs(1), load, q_ref.shape[1])


def products(pairs, load, count):
    def body(i, sums):
        values = load(i)
        return tuple(total + values[a] * values[b] for total, (a, b) in zip(sums, pairs))

    zero = jnp.zeros((8, 128), jnp.float32)
    sums = lax.fori_loop(0, count, body, (zero,) * len(pairs), unroll=4)
    lane = lax.broadcasted_iota(jnp.int32, (8, 128), 1)
    row = zero
    for total, pair in zip(sums, pairs):
        row = jnp.where(lane == SLOT[pair], jnp.sum(total, 1, keepdims=True), row)
    return row


def earlier_products(q_ref, out_ref):
    pairs = [(a, b) for b in range(EARLIER) for a in range(b + 1)]
    out_ref[...] = products(pairs, lambda i: [q_ref[a, i] for a in range(EARLIER)], q_ref.shape[1])


def new_pairs(number):
    return [(a, EARLIER + number) for a in range(EARLIER + number + 1)]


def finish_kernel(entries, sums_ref, q_ref, *refs):
    v_refs, (new_ref, coeff_ref, triangle_ref) = refs[:STEPS], refs[STEPS:]
    parts = [sums_ref[i] for i in range(sums_ref.shape[0])]
    while len(parts) > 1:
        parts = [parts[i] + parts[i + 1] for i in range(0, len(parts), 2)]
    total = parts[0]
    total = jnp.broadcast_to(jnp.sum(total, 0, keepdims=True), total.shape) * (1.0 / entries)

    def entry(a, b):
        k = SLOT[(min(a, b), max(a, b))]
        return jnp.broadcast_to(total[:, k : k + 1], total.shape)

    coeff = [[entry(i, EARLIER + j) for j in range(STEPS)] for i in range(EARLIER)]
    overlap = {(a, b): entry(a, b) for b in range(EARLIER) for a in range(b + 1)}
    gram = {}
    for k in range(STEPS):
        mixed = []
        for i in range(EARLIER):
            term = -2.0 * coeff[i][k]
            for m in range(EARLIER):
                term = term + overlap[(min(i, m), max(i, m))] * coeff[m][k]
            mixed.append(term)
        for j in range(k, STEPS):
            value = entry(EARLIER + k, EARLIER + j)
            for i in range(EARLIER):
                value = value + coeff[i][j] * mixed[i]
            gram[(j, k)] = value
    factor, inverse = {}, []
    for k in range(STEPS):
        pivot = gram[(k, k)]
        for m in range(k):
            pivot = pivot - factor[(k, m)] * factor[(k, m)]
        inverse.append(lax.rsqrt(pivot))
        factor[(k, k)] = pivot * inverse[k]
        for j in range(k + 1, STEPS):
            value = gram[(j, k)]
            for m in range(k):
                value = value - factor[(j, m)] * factor[(k, m)]
            factor[(j, k)] = value * inverse[k]
    row = lax.broadcasted_iota(jnp.int32, total.shape, 0)
    lane = lax.broadcasted_iota(jnp.int32, total.shape, 1)
    table = jnp.zeros_like(total)
    for i in range(EARLIER):
        for j in range(STEPS):
            table = jnp.where((row == j) & (lane == i), coeff[i][j], table)
    coeff_ref[...] = table[:STEPS, :EARLIER]
    table = jnp.zeros_like(total)
    for (j, k), value in factor.items():
        table = jnp.where((row == k) & (lane == j), value, table)
    triangle_ref[...] = table[:STEPS, :STEPS]

    def body(n, carry):
        earlier = [q_ref[i, n] for i in range(EARLIER)]
        done = []
        for j in range(STEPS):
            value = v_refs[j][n]
            for i in range(EARLIER):
                value = value - coeff[i][j] * earlier[i]
            for k in range(j):
                value = value - factor[(j, k)] * done[k]
            done.append(value * inverse[j])
            new_ref[j, n] = done[j]
        return carry

    lax.fori_loop(0, q_ref.shape[1], body, 0, unroll=8)


def call(body, outs, cost, *args, **more):
    return pl.pallas_call(
        body,
        out_shape=[jax.ShapeDtypeStruct(shape, jnp.float32) for shape in outs],
        cost_estimate=pl.CostEstimate(flops=cost, bytes_accessed=cost, transcendentals=0),
        compiler_params=pltpu.CompilerParams(vmem_limit_bytes=24 << 20),
        **more,
    )(*args)


def shifts(axis):
    count = lax.axis_size(axis)
    up = [(i, (i + 1) % count) for i in range(count)]
    return up, [(target, source) for source, target in up]


def exchange(axis, low, high):
    up, down = shifts(axis)
    return lax.ppermute(high, axis, up), lax.ppermute(low, axis, down)


def exchange_y(near, far):
    count = lax.axis_size("gy")
    inner = [(i, i + 1 - i % 2 * 2) for i in range(count)]
    outer = [(i, (i - 1 + i % 2 * 2) % count) for i in range(count)]
    beyond = lax.ppermute(far, "gy", outer)
    return lax.ppermute(near, "gy", inner), beyond


def on_device(earlier_basis, diffusivity, reaction):
    span_x, span_y, span_z = diffusivity.shape[1:]
    tiles = SPECIES * span_x * span_y // 8
    devices = 1
    for axis in AXES:
        devices *= lax.axis_size(axis)
    entries = tiles * 8 * span_z * devices
    in_hbm = pl.BlockSpec(memory_space=pltpu.HBM)
    given = (earlier_basis, diffusivity, reaction)
    face = (2 * SPECIES * WIDE + SPECIES * SPECIES, span_y, span_z)
    field = diffusivity.shape
    low, high, *kept = call(
        x_faces,
        [face, face, field, field],
        1 << 20,
        *[pltpu.with_memory_space_constraint(a, pltpu.HBM) for a in given],
        in_specs=[in_hbm] * 3,
        scratch_shapes=[pltpu.SemaphoreType.DMA((8,))],
    )
    x_halos = exchange("gx", low, high)
    kept.append(reaction)
    face = (Y_TILES[0], 8, span_z)
    z_face = (SIDES // 4, 16, span_z)
    own = call(own_faces, [face, face, z_face, z_face], 1 << 20, *kept)
    y_own = exchange_y(*own[:2])
    up, down = shifts("gz")
    z_before = lax.ppermute(own[3], "gz", up)
    z_after = lax.ppermute(own[2], "gz", down)
    z_own = (z_before, z_after)
    face = (Y_TILES[1], 8, span_z)
    faces = call(more_y_faces, [face, face], 1 << 20, *x_halos)
    y_more = exchange_y(*faces)
    face = (2 * BLOCKS, 8, span_z)
    edges = (PLANES, 8, span_z)
    edge_own, low, high = call(some_z_faces, [edges, face, face], 1 << 20, *x_halos, *y_own)
    edge_more, low, high = call(more_z_faces, [edges, face, face], 1 << 20, *y_more, low, high)
    edge = (edge_own, edge_more)
    z_more = exchange("gz", low, high)
    basis = earlier_basis.reshape(EARLIER, tiles, 8, span_z)
    (sums,) = call(earlier_products, [(8, span_z)], 4 << 20, basis)
    own = (tiles, 8, span_z)
    plane = (ROWS, span_z)
    early = call(
        early_steps,
        [(count,) + plane for count in (D_BASE, D_BASE, CONDUCTS, SPECIES * len(R_PLANES), HALVES, HALVES)],
        1 << 20,
        *kept,
        *x_halos,
        *edge,
    )
    scratch = [pltpu.VMEM((D_BASE,) + plane, jnp.float32)]
    face = (FACE_TILES, 8, span_z)
    several = [(count,) + plane for count in (SPECIES * span_x, HALVES)] + [face, face]
    several += [(count,) + plane for count in (SIDES, CONDUCTS - WITHOUT_Z, 4 * HALVES)]
    v1, v2, wide, wide_side, low, high, side, z_conducts, side_conducts = call(
        first_steps,
        [own, own] + several,
        1 << 20,
        reaction,
        *x_halos,
        *edge,
        *early,
        *z_own,
        *z_more,
        scratch_shapes=scratch,
    )
    halos = exchange("gx", low, high)
    (sums,) = call(middle_products, [(8, span_z)], 4 << 20, basis, v1, v2, sums)
    plane_sums = call(
        middle_step,
        [(SPECIES * span_x,) + plane, (HALVES,) + plane],
        1 << 20,
        reaction,
        *x_halos,
        *edge,
        early[2],
        z_conducts,
        wide,
        wide_side,
    )
    v3, v4, rows = call(
        last_steps,
        [own, own, (devices, span_z)],
        1 << 20,
        reaction,
        *x_halos,
        *edge,
        side,
        early[2],
        z_conducts,
        side_conducts,
        wide,
        wide_side,
        *plane_sums,
        *halos,
        basis,
        v1,
        v2,
        sums,
        scratch_shapes=scratch * 2,
    )
    rows = lax.all_to_all(rows.reshape(devices, 1, span_z), AXES, 0, 0)
    new, coeff, triangle = call(
        functools.partial(finish_kernel, entries),
        [(STEPS, tiles, 8, span_z), (STEPS, EARLIER), (STEPS, STEPS)],
        1 << 20,
        rows.reshape(devices // 8, 8, span_z),
        basis,
        v1,
        v2,
        v3,
        v4,
    )
    return new.reshape((STEPS, SPECIES, span_x, span_y, span_z)), coeff.T, triangle


def solution(mesh):
    in_specs = (
        P(None, None, "gx", "gy", "gz"),
        P(None, "gx", "gy", "gz"),
        P(None, None, "gx", "gy", "gz"),
    )
    out_specs = (P(None, None, "gx", "gy", "gz"), P(), P())
    return jax.shard_map(
        on_device, mesh=mesh, in_specs=in_specs, out_specs=out_specs, check_vma=False
    )
```
